128 devices in a mesh: det: 4 (over x), tm: 32 (over y, z, core).
Axes of the slice: x: 4, y: 4, z: 4, core: 2. Of those that a mesh axis runs over, the one named last changes fastest.
Arguments:
- samples: float32 [4, 32, 128, 256], P('det', 'tm')
- pointing: int32 [4, 32, 128, 256], P('det', 'tm'), may hold values from 0 to 16383, as said below
- angles: float32 [4, 32, 128, 256], P('det', 'tm'), may hold values from -3.1415927 to 3.1415927
- counts: int32 [4, 32, 128], P('det', 'tm'), may hold values from 1 to 256, as said below
- sky_map: float32 [3, 256, 8192], P(None, ('det', 'tm'))
- prior_precision: float32 [3, 256, 4096], P(None, 'det', 'tm'), may hold values from 0.5 to 5
- omega_noise: float32 [6, 256, 4096], P(None, 'det', 'tm'), may hold values from -6 to 6
- omega_prior: float32 [6, 256, 4096], P(None, 'det', 'tm'), may hold values from -6 to 6
Outputs:
- gains: float32 [4, 32], P('det', 'tm')
- binned: float32 [3, 256, 8192], P(None, ('det', 'tm'))
- solution: float32 [6, 256, 4096], P(None, 'det', 'tm')
The draws below stay inside these ranges and needn't reach their ends.
Inputs may be any that keep to these rules, and one draw needn't show every extreme that they name: The first counts[g, t, k] slots of a row hold samples; some sky tile takes 256 samples from every device, and every device fills at least one tile. `pointing`: pixel within the destination tile, cycle-major with 8192 pixels a cycle.
All inputs are finite; a program needn't handle non-finite values.
Results may differ from the reference program's by a relative error of at most 0.0003.
Values sent between devices are 32-bit elements; how exact they have to be, the bound alone decides.
A program may use at most 128 MiB of HBM per device.

```python
import math
import jax
import jax.numpy as jnp
from jax import lax

NPHI = 8192
M = 4096
RDEV = 2
CAP = 256
ITERS = 3
NDG = 4
NTC = 32
TILES = 128
CYCLES = 256
PIXT = 16384


def shared_draw(key):
    sky = jax.random.normal(jax.random.fold_in(key, 11), (3, CYCLES, NPHI), jnp.float32)
    shape = (NDG, NTC, TILES, CAP)
    pointing = jax.random.randint(jax.random.fold_in(key, 13), shape, 0, PIXT).astype(jnp.int32)
    pointing = pointing.at[0, 0, 0, 0].set(PIXT - 1)
    angles = jax.random.uniform(jax.random.fold_in(key, 14), shape, jnp.float32, -3.1415927, 3.1415927)
    true_gain = jax.random.uniform(jax.random.fold_in(key, 15), (NDG, NTC, 1, 1), jnp.float32, 0.6, 1.4)
    noise = jax.random.normal(jax.random.fold_in(key, 16), shape, jnp.float32)
    sky_flat = sky.reshape(3, TILES, PIXT)
    tile_index = lax.broadcasted_iota(jnp.int32, shape, 2)
    signal = sky_flat[0][tile_index, pointing] + sky_flat[1][tile_index, pointing] * jnp.cos(2.0 * angles) + sky_flat[2][tile_index, pointing] * jnp.sin(2.0 * angles)
    samples = true_gain * signal + noise
    return (sky, pointing, angles, samples)


def draw_sky_map(key, part):
    return shared_draw(key)[0]


def draw_pointing(key, part):
    return shared_draw(key)[1]


def draw_angles(key, part):
    return shared_draw(key)[2]


def draw_samples(key, part):
    return shared_draw(key)[3]


def draw_counts(key, part):
    base = jax.random.randint(jax.random.fold_in(key, 21), (NDG, NTC, TILES), 0, CAP * 3 // 4 + 1)
    factor = jax.random.randint(jax.random.fold_in(key, 22), (1, 1, TILES), 1, 5)
    filled = jnp.maximum(CAP // 4 + base * factor // 4, 1)
    column = lax.broadcasted_iota(jnp.int32, (NDG, NTC, TILES), 2)
    common = jax.random.randint(jax.random.fold_in(key, 23), (), 0, TILES)
    single = jax.random.randint(jax.random.fold_in(key, 24), (NDG, NTC, 1), 0, TILES)
    filled = jnp.where(column == common, CAP, filled)
    filled = jnp.where(column == single, CAP, filled)
    return filled.astype(jnp.int32)


def shard_levels(stream_key, extent, split, least, top_value):
    def one(dim, parts):
        steps = jax.random.uniform(jax.random.fold_in(jax.random.fold_in(stream_key, 6), dim), (parts,), jnp.float32, least / len(split), top_value / len(split))
        return jnp.repeat(jnp.exp(steps), extent[dim] // parts).reshape((-1,) + (1,) * (len(extent) - dim - 1))

    factor_of = one(*split[0])
    for cut in split[1:]:
        factor_of = factor_of * one(*cut)
    return factor_of


def centred(key, dims, width, bound, shards=(), held_as=jnp.bfloat16):
    gain = shard_levels(key, dims, shards, -0.22, 0.18) if shards else 1.0
    result = jax.random.normal(key, dims, jnp.float32) * width * gain
    return jnp.minimum(jnp.maximum(result, -bound), bound).astype(held_as)


def setup_inputs(seed: int = 0) -> dict:
    key_list = jax.random.split(jax.random.key(seed), 9)
    return {
        "samples": draw_samples(jax.random.fold_in(key_list[8], 71), 0),
        "pointing": draw_pointing(jax.random.fold_in(key_list[8], 71), 0),
        "angles": draw_angles(jax.random.fold_in(key_list[8], 71), 0),
        "counts": draw_counts(jax.random.fold_in(key_list[8], 71), 0),
        "sky_map": draw_sky_map(jax.random.fold_in(key_list[8], 71), 0),
        "prior_precision": jnp.clip(jnp.exp(math.log(5.0) - 2.3025851 * jax.random.uniform(key_list[5], (3, CYCLES, M), jnp.float32) ** shard_levels(key_list[5], (3, CYCLES, M), ((1, 4), (2, 32)), -0.2, 0.2)), 0.5, 5.0),
        "omega_noise": centred(key_list[6], (6, CYCLES, M), 1.0, 6.0, ((1, 4), (2, 32)), jnp.float32),
        "omega_prior": centred(key_list[7], (6, CYCLES, M), 1.0, 6.0, ((1, 4), (2, 32)), jnp.float32),
    }


def template(sky_flat, pointing, angles):
    tile_index = lax.broadcasted_iota(jnp.int32, pointing.shape, pointing.ndim - 2)
    cosine = jnp.cos(2.0 * angles)
    sine = jnp.sin(2.0 * angles)
    signal = sky_flat[0][tile_index, pointing] + sky_flat[1][tile_index, pointing] * cosine + sky_flat[2][tile_index, pointing] * sine
    return (signal, cosine, sine)

def validity(samples, counts):
    slots = lax.broadcasted_iota(jnp.int32, samples.shape, samples.ndim - 1)
    return (slots < counts[..., None]).astype(jnp.float32)

def operate(field, root, diagonal):
    scaled = root * field
    padded = jnp.pad(scaled, ((0, 0), (1, 1), (0, 0)))
    beside = padded[:, 2:] + padded[:, :-2]
    return diagonal * field - 0.45 * root * beside

def reference(samples, pointing, angles, counts, sky_map, prior_precision, omega_noise, omega_prior):
    sky_flat = sky_map.reshape(3, TILES, PIXT)

    def group_sums(items):
        samples_g, pointing_g, angles_g, counts_g = items
        signal, cosine, sine = template(sky_flat, pointing_g, angles_g)
        valid = validity(samples_g, counts_g)
        return (lax.optimization_barrier(jnp.sum(valid * signal * samples_g, axis=(1, 2))), lax.optimization_barrier(jnp.sum(valid * signal * signal, axis=(1, 2))))
    sums_a, sums_b = lax.map(group_sums, (samples, pointing, angles, counts))
    gains = sums_a / (sums_b + 1e-06)

    def accumulate(carry, items):
        binned, hits = carry
        samples_g, pointing_g, angles_g, counts_g, gains_g = items
        signal, cosine, sine = template(sky_flat, pointing_g, angles_g)
        valid = validity(samples_g, counts_g)
        residual = valid * (samples_g - gains_g[:, None, None] * signal)
        tile_index = lax.broadcasted_iota(jnp.int32, pointing_g.shape, 1)
        where = (tile_index * PIXT + pointing_g).reshape(-1)
        weights = jnp.stack([residual, residual * cosine, residual * sine]).reshape(3, -1)
        binned = binned.at[:, where].add(weights)
        cycle = (tile_index * RDEV + pointing_g // NPHI).reshape(-1)
        hits = hits.at[cycle].add(valid.reshape(-1))
        return ((binned, hits), None)
    start = (jnp.zeros((3, TILES * PIXT), jnp.float32), jnp.zeros((CYCLES,), jnp.float32))
    (binned, hits), _ = lax.scan(accumulate, start, (samples, pointing, angles, counts, gains))
    binned = binned.reshape(3, CYCLES, NPHI)
    spectrum = jnp.fft.rfft(binned, axis=-1)[..., :M] / math.sqrt(NPHI)
    planes = jnp.stack([jnp.real(spectrum), jnp.imag(spectrum)], axis=1).reshape(6, CYCLES, M).astype(jnp.float32)
    weight = (hits / NPHI)[None, :, None]
    precision = jnp.repeat(prior_precision, 2, axis=0)
    root = jnp.sqrt(precision)
    diagonal = precision + weight
    rhs = planes + jnp.sqrt(weight) * omega_noise + root * omega_prior
    solution = jnp.zeros_like(rhs)
    resid = rhs
    direction = rhs
    norm_now = jnp.sum(resid * resid)
    for iteration in range(ITERS):
        image = operate(direction, root, diagonal)
        alpha = norm_now / jnp.sum(direction * image)
        solution = solution + alpha * direction
        resid = resid - alpha * image
        norm_next = jnp.sum(resid * resid)
        direction = resid + norm_next / norm_now * direction
        norm_now = norm_next
    return (gains, binned, solution)
```

```python
import math

import jax
import jax.numpy as jnp
import numpy as np
from jax import lax
from jax.experimental import pallas as pl
from jax.experimental.pallas import tpu as pltpu
from jax.sharding import PartitionSpec as P

MESH = pl.DeviceIdType.MESH
HIGHEST = lax.Precision.HIGHEST
F32 = jnp.float32
BF16 = jnp.bfloat16
NDET = 4
NTM = 32
NDEV = NDET * NTM
GROUP = 16
NGROUP = NDEV // GROUP
UNROLL_G = 2
UNROLL_S = 2
SHIFT = 4.0
SCALE = 4.0
STEP_MAX = 20.0


def tables():
    h, i = np.divmod(np.arange(128), 64)
    a = 2 * i + h
    k = np.arange(128)
    ang = 2.0 * np.pi * (np.outer(a, k) % 128) / 128
    first = np.concatenate([np.cos(ang), -np.sin(ang)], axis=1)
    b = np.arange(64)
    ang = 2.0 * np.pi * np.outer(b, k) / 8192
    twist = np.stack([np.cos(ang), np.sin(ang)])
    q = np.arange(32)
    ang = 2.0 * np.pi * (np.outer(q, b) % 64) / 64
    c, s = np.cos(ang), np.sin(ang)
    last = np.concatenate([np.concatenate([c, s], axis=1), np.concatenate([-s, c], axis=1)], axis=0)
    last = last / math.sqrt(8192)
    return [np.asarray(x, np.float32) for x in (first, twist, last)]


def one_hot(row, rows):
    value = jnp.broadcast_to(row, (16, 128)).astype(BF16)
    index = lax.broadcasted_iota(jnp.int32, (rows, 128), 0).astype(F32).astype(BF16)
    same = index.reshape(rows // 16, 16, 128) == value[None]
    return jnp.where(same, jnp.ones((), BF16), jnp.zeros((), BF16)).reshape(rows, 128)


def kernel(
    samples, pointing, angles, counts, sky, prec, onoise, oprior, first, twist, last,
    gain_out, map_out, sol_out,
    sbuf, rbuf, table, hi_s, lo_s, cos_s, sin_s, look, wsplit, acc,
    stat_r, spec_s, spec_r, pp, bw, v1_s, v2_s, mom_r,
    send_sem, recv_sem, stat_send, stat_recv, spec_send, spec_recv,
    edge_send, edge_recv, mom_send, mom_recv,
):
    det = lax.axis_index("det")
    tm = lax.axis_index("tm")
    me = det * NTM + tm

    def place(p):
        return (p // NTM, p % NTM)

    barrier = pltpu.get_barrier_semaphore()

    @pl.loop(1, NDEV)
    def _(o):
        pl.semaphore_signal(barrier, inc=1, device_id=place((me + o) % NDEV), device_id_type=MESH)

    row_i = lax.broadcasted_iota(jnp.int32, (128, 128), 0)
    col_i = lax.broadcasted_iota(jnp.int32, (128, 128), 1)
    for half in range(2):
        lanes = slice(half * 128, half * 128 + 128)
        sbuf[pl.ds(half, 128, stride=8), :] = samples[:, lanes]
        sbuf[pl.ds(2 + half, 128, stride=8), :] = angles[:, lanes]
        sbuf[pl.ds(4 + half, 128, stride=8), :] = pointing[:, lanes].astype(F32)
    count_row = jnp.broadcast_to(counts[...].astype(F32), (128, 128))
    count_col = jnp.sum(jnp.where(row_i == col_i, count_row, 0.0), axis=1, keepdims=True)
    count_full = jnp.broadcast_to(count_col, (128, 128))
    sbuf[pl.ds(6, 128, stride=8), :] = count_full
    sbuf[pl.ds(7, 128, stride=8), :] = count_full

    for c in range(3):
        blocks = []
        for cyc in range(2):
            turned = sky[c, pl.ds(cyc, 64, stride=2), :].T
            blocks.append(jnp.concatenate([turned[:64], turned[64:]], axis=1))
        full = jnp.concatenate(blocks, axis=1)
        upper = full.astype(BF16)
        table[pl.ds(c * 64, 64), :] = upper
        table[pl.ds(192 + c * 64, 64), :] = (full - upper.astype(F32)).astype(BF16)

    pp[:, 8:72, :] = prec[...]

    @pl.when(det == 0)
    def _():
        pp[:, 0:8, :] = jnp.zeros((3, 8, 128), F32)
        bw[:, 0:8, :] = jnp.zeros((7, 8, 128), F32)

    @pl.when(det == NDET - 1)
    def _():
        pp[:, 72:80, :] = jnp.zeros((3, 8, 128), F32)
        bw[:, 72:80, :] = jnp.zeros((7, 8, 128), F32)

    acc[...] = jnp.zeros_like(acc)
    pl.semaphore_wait(barrier, NDEV - 1)

    my_group = me // GROUP

    @pl.loop(1, NDEV)
    def _(o):
        to = (me + o) % NDEV
        pltpu.make_async_remote_copy(
            sbuf.at[pl.ds(to * 8, 8)], rbuf.at[pl.ds(me * 8, 8)],
            send_sem, recv_sem.at[my_group], device_id=place(to), device_id_type=MESH,
        ).start()

    def edge_copy(src, dst, index, where):
        return pltpu.make_async_remote_copy(
            src, dst, edge_send.at[index], edge_recv.at[index], device_id=where, device_id_type=MESH
        )

    prec_down = edge_copy(prec.at[:, 56:64, :], pp.at[:, 0:8, :], 0, ((det + 1) % NDET, tm))
    prec_up = edge_copy(prec.at[:, 0:8, :], pp.at[:, 72:80, :], 1, ((det + NDET - 1) % NDET, tm))

    @pl.when(det < NDET - 1)
    def _():
        prec_down.start()

    @pl.when(det > 0)
    def _():
        prec_up.start()

    rbuf[pl.ds(me * 8, 8), :] = sbuf[pl.ds(me * 8, 8), :]

    col_index = lax.broadcasted_iota(jnp.int32, (64, 128), 0).astype(F32)

    def gather_group(group):
        base = group * GROUP
        for half in range(2):
            pixel = rbuf[pl.ds(base * 8 + 4 + half, GROUP, stride=8), :].astype(jnp.int32)
            upper = (pixel >> 13) * 128 + ((pixel >> 6) & 1) * 64 + ((pixel >> 7) & 63)
            hi_s[half, pl.ds(base, GROUP), :] = upper.astype(F32)
            lo_s[half, pl.ds(base, GROUP), :] = (pixel & 63).astype(F32)

        @pl.loop(0, GROUP // UNROLL_G)
        def _(step):
            for u in range(UNROLL_G):
                s = base + step * UNROLL_G + u
                hots = [one_hot(hi_s[half, pl.ds(s, 1), :], 256) for half in range(2)]
                got = jnp.dot(table[...], jnp.concatenate(hots, axis=1), preferred_element_type=F32)
                got = got[:192] + got[192:]
                for half in range(2):
                    low = lo_s[half, pl.ds(s, 1), :]
                    same = col_index == low
                    for c in range(3):
                        part = got[c * 64 : c * 64 + 64, half * 128 : half * 128 + 128]
                        look[c, half, pl.ds(s, 1), :] = jnp.sum(
                            jnp.where(same, part, 0.0), axis=0, keepdims=True
                        )

    @pl.loop(0, NGROUP)
    def _(t):
        group = (my_group + t) % NGROUP

        @pl.when(t == 0)
        def _():
            span = rbuf.at[pl.ds(0, (GROUP - 1) * 8)]
            pltpu.make_async_copy(span, span, recv_sem.at[my_group]).wait()

        @pl.when(t > 0)
        def _():
            span = rbuf.at[pl.ds(0, GROUP * 8)]
            pltpu.make_async_copy(span, span, recv_sem.at[group]).wait()

        gather_group(group)

    count = rbuf[pl.ds(6, 128, stride=8), :]
    slot = col_i.astype(F32)
    cross = jnp.zeros((128, 128), F32)
    square = jnp.zeros((128, 128), F32)
    for half in range(2):
        angle = rbuf[pl.ds(2 + half, 128, stride=8), :]
        cosine = jnp.cos(2.0 * angle)
        sine = jnp.sin(2.0 * angle)
        cos_s[half] = cosine
        sin_s[half] = sine
        signal = look[0, half] + look[1, half] * cosine + look[2, half] * sine
        look[0, half] = signal
        masked = jnp.where(slot + 128.0 * half < count, signal, 0.0)
        cross = cross + masked * rbuf[pl.ds(half, 128, stride=8), :]
        square = square + masked * signal
    cross = jnp.sum(cross.T, axis=0, keepdims=True)
    square = jnp.sum(square.T, axis=0, keepdims=True)
    stat_r[me] = jnp.concatenate([cross, square], axis=0)

    @pl.loop(1, NDEV)
    def _(o):
        pltpu.make_async_remote_copy(
            stat_r.at[me], stat_r.at[me], stat_send, stat_recv,
            device_id=place((me + o) % NDEV), device_id_type=MESH,
        ).start()

    rest = stat_r.at[pl.ds(0, NDEV - 1)]
    pltpu.make_async_copy(rest, rest, stat_recv).wait()
    total = jnp.sum(stat_r[...], axis=0)
    gains = total[0:1] / (total[1:2] + 1e-06)
    lane = lax.broadcasted_iota(jnp.int32, (1, 128), 1)
    gain_out[...] = jnp.sum(jnp.where(lane == me, gains, 0.0), axis=1, keepdims=True)
    gain_full = jnp.broadcast_to(gains, (128, 128)).T

    hits = [jnp.zeros((1, 128), F32) for _ in range(2)]
    for half in range(2):
        data = rbuf[pl.ds(half, 128, stride=8), :]
        good = slot + 128.0 * half < count
        residual = jnp.where(good, data - gain_full * look[0, half], 0.0)
        for c, weight in enumerate((residual, residual * cos_s[half], residual * sin_s[half])):
            upper = weight.astype(BF16).astype(F32)
            wsplit[c, half] = upper
            wsplit[3 + c, half] = weight - upper
        late = jnp.where(hi_s[half] >= 128.0, 1.0, 0.0)
        valid = jnp.where(good, 1.0, 0.0)
        hits[1] = hits[1] + jnp.sum(valid * late, axis=0, keepdims=True)
        hits[0] = hits[0] + jnp.sum(valid * (1.0 - late), axis=0, keepdims=True)

    low_index = lax.broadcasted_iota(jnp.int32, (64, 128), 0).astype(F32).astype(BF16).reshape(4, 16, 128)

    @pl.loop(0, NDEV // UNROLL_S)
    def _(step):
        lefts = []
        rights = []
        for u in range(UNROLL_S):
            s = step * UNROLL_S + u
            for half in range(2):
                rights.append(one_hot(hi_s[half, pl.ds(s, 1), :], 256))
                low = jnp.broadcast_to(lo_s[half, pl.ds(s, 1), :], (16, 128)).astype(BF16)
                same = low_index == low[None]
                rows = []
                for w in range(6):
                    value = jnp.broadcast_to(wsplit[w, half, pl.ds(s, 1), :], (16, 128)).astype(BF16)
                    rows.append(jnp.where(same, value[None], jnp.zeros((), BF16)).reshape(64, 128))
                lefts.append(jnp.concatenate(rows, axis=0))
        acc[...] += lax.dot_general(
            jnp.concatenate(lefts, axis=1), jnp.concatenate(rights, axis=1),
            (((1,), (1,)), ((), ())), preferred_element_type=F32,
        )

    field = acc[:192] + acc[192:]

    z_parts = []
    for cyc in range(2):
        y = jnp.dot(
            field[:, cyc * 128 : cyc * 128 + 128], first[...],
            precision=HIGHEST, preferred_element_type=F32,
        )
        for c in range(3):
            y_re = y[c * 64 : c * 64 + 64, :128]
            y_im = y[c * 64 : c * 64 + 64, 128:]
            z_re = y_re * twist[0] + y_im * twist[1]
            z_im = y_im * twist[0] - y_re * twist[1]
            z_parts.append(jnp.concatenate([z_re, z_im], axis=0))
    x = jnp.dot(
        last[...], jnp.concatenate(z_parts, axis=1), precision=HIGHEST, preferred_element_type=F32
    )
    for cyc in range(2):
        for c in range(3):
            block = x[:, (cyc * 3 + c) * 128 : (cyc * 3 + c) * 128 + 128]
            spec_s[pl.ds(4 * c + cyc, 32, stride=16), :] = block[:32]
            spec_s[pl.ds(4 * c + 2 + cyc, 32, stride=16), :] = block[32:]
        weight = jnp.sum(hits[cyc], axis=1, keepdims=True) * (1.0 / 8192)
        spec_s[pl.ds(12 + cyc, 32, stride=16), :] = jnp.broadcast_to(weight, (32, 128))
        spec_s[pl.ds(14 + cyc, 32, stride=16), :] = jnp.broadcast_to(weight, (32, 128))

    @pl.loop(1, NTM)
    def _(o):
        to = (tm + o) % NTM
        pltpu.make_async_remote_copy(
            spec_s.at[pl.ds(to * 16, 16)], spec_r.at[pl.ds(tm * 16, 16)],
            spec_send, spec_recv, device_id=(det, to), device_id_type=MESH,
        ).start()

    spec_r[pl.ds(tm * 16, 16), :] = spec_s[pl.ds(tm * 16, 16), :]
    for c in range(3):
        for cyc in range(2):
            part = field[c * 64 : c * 64 + 64, cyc * 128 : cyc * 128 + 128]
            part = jnp.concatenate([part[:, :64], part[:, 64:]], axis=0)
            map_out[c, pl.ds(cyc, 64, stride=2), :] = part.T

    span = spec_r.at[pl.ds(0, (NTM - 1) * 16)]
    pltpu.make_async_copy(span, span, spec_recv).wait()

    for cyc in range(2):
        for j in range(7):
            bw[j, pl.ds(8 + cyc, 32, stride=2), :] = spec_r[pl.ds(2 * j + cyc, 32, stride=16), :]
    noise_root = jnp.sqrt(bw[6, 8:72, :])
    for c in range(3):
        root = jnp.sqrt(prec[c])
        for p in range(2):
            j = 2 * c + p
            bw[j, 8:72, :] = bw[j, 8:72, :] + noise_root * onoise[j] + root * oprior[j]
    rhs_down = edge_copy(bw.at[:, 64:72, :], bw.at[:, 0:8, :], 2, ((det + 1) % NDET, tm))
    rhs_up = edge_copy(bw.at[:, 8:16, :], bw.at[:, 72:80, :], 3, ((det + NDET - 1) % NDET, tm))

    @pl.when(det < NDET - 1)
    def _():
        rhs_down.start()

    @pl.when(det > 0)
    def _():
        rhs_up.start()

    @pl.when(det > 0)
    def _():
        prec_down.wait_recv()
        rhs_down.wait_recv()

    @pl.when(det < NDET - 1)
    def _():
        prec_up.wait_recv()
        rhs_up.wait_recv()

    moments = [jnp.zeros((8, 128), F32) for _ in range(6)]
    for c in range(3):
        precision = pp[c]
        root = jnp.sqrt(precision)
        side = root * (0.45 / SCALE)
        diagonal = (precision + bw[6] - SHIFT) * (1.0 / SCALE)

        def step(v):
            u = root * v
            beside = pltpu.roll(u, 1, 0) + pltpu.roll(u, 79, 0)
            return diagonal * v - side * beside

        for p in range(2):
            j = 2 * c + p
            v0 = bw[j]
            v1 = step(v0)
            v2 = step(v1)
            v3 = step(v2)
            own = [v[8:72] for v in (v0, v1, v2, v3)]
            v1_s[j] = own[1]
            v2_s[j] = own[2]
            for m, (a, b) in enumerate(((0, 0), (0, 1), (1, 1), (1, 2), (2, 2), (2, 3))):
                moments[m] = moments[m] + jnp.sum((own[a] * own[b]).reshape(8, 8, 128), axis=0)
    message = jnp.zeros((1, 128), F32)
    for m in range(6):
        value = jnp.sum(jnp.sum(moments[m], axis=0, keepdims=True), axis=1, keepdims=True)
        message = jnp.where(lane == m, jnp.broadcast_to(value, (1, 128)), message)
    mom_r[me] = message

    @pl.loop(1, NDEV)
    def _(o):
        pltpu.make_async_remote_copy(
            mom_r.at[me], mom_r.at[me], mom_send, mom_recv,
            device_id=place((me + o) % NDEV), device_id_type=MESH,
        ).start()

    rest = mom_r.at[pl.ds(0, NDEV - 1)]
    pltpu.make_async_copy(rest, rest, mom_recv).wait()
    sums = jnp.sum(mom_r[...], axis=0)
    nu = [jnp.sum(jnp.where(lane == m, sums, 0.0), axis=1, keepdims=True) for m in range(6)]

    zero = jnp.zeros((1, 1), F32)

    def inner(a, b):
        terms = {}
        for i, x_i in enumerate(a):
            for j, y_j in enumerate(b):
                terms[i + j] = terms.get(i + j, zero) + x_i * y_j
        out = zero
        for power, value in terms.items():
            out = out + value * nu[power]
        return out

    def image_of(a):
        longer = list(a) + [zero]
        return [SHIFT * longer[i] + (SCALE * longer[i - 1] if i else zero) for i in range(len(longer))]

    resid = [zero + 1.0]
    direction = [zero + 1.0]
    answer = [zero, zero, zero]
    norm_now = nu[0]
    for iteration in range(3):
        image = image_of(direction)
        alpha = norm_now / inner(direction, image)
        alpha = jnp.minimum(jnp.maximum(alpha, 0.0), STEP_MAX)
        for i, value in enumerate(direction):
            answer[i] = answer[i] + alpha * value
        if iteration < 2:
            resid = resid + [zero]
            resid = [r - alpha * w for r, w in zip(resid, image)]
            norm_next = jnp.maximum(inner(resid, resid), 0.0)
            beta = norm_next / norm_now
            direction = [r + beta * d for r, d in zip(resid, direction + [zero])]
            norm_now = norm_next
    for j in range(6):
        sol_out[j] = answer[0] * bw[j, 8:72, :] + answer[1] * v1_s[j] + answer[2] * v2_s[j]

    span = sbuf.at[pl.ds(0, (NDEV - 1) * 8)]
    pltpu.make_async_copy(span, span, send_sem).wait()
    rest = stat_r.at[pl.ds(0, NDEV - 1)]
    pltpu.make_async_copy(rest, rest, stat_send).wait()
    span = spec_s.at[pl.ds(0, (NTM - 1) * 16)]
    pltpu.make_async_copy(span, span, spec_send).wait()
    rest = mom_r.at[pl.ds(0, NDEV - 1)]
    pltpu.make_async_copy(rest, rest, mom_send).wait()

    @pl.when(det < NDET - 1)
    def _():
        prec_down.wait_send()
        rhs_down.wait_send()

    @pl.when(det > 0)
    def _():
        prec_up.wait_send()
        rhs_up.wait_send()


def per_device(
    samples, pointing, angles, counts, sky_map, prior_precision, omega_noise, omega_prior
):
    sky = sky_map.reshape(3, 2, 64, 128).transpose(0, 2, 1, 3).reshape(3, 128, 128)
    vmem = pl.BlockSpec(memory_space=pltpu.VMEM)
    dma = pltpu.SemaphoreType.DMA
    gain, binned, solved = pl.pallas_call(
        kernel,
        name="gibbs_step",
        out_shape=(
            jax.ShapeDtypeStruct((1, 1), F32),
            jax.ShapeDtypeStruct((3, 128, 128), F32),
            jax.ShapeDtypeStruct((6, 64, 128), F32),
        ),
        in_specs=[vmem] * 11,
        out_specs=(vmem, vmem, vmem),
        scratch_shapes=[
            pltpu.VMEM((1024, 128), F32),
            pltpu.VMEM((1024, 128), F32),
            pltpu.VMEM((384, 256), BF16),
            pltpu.VMEM((2, 128, 128), F32),
            pltpu.VMEM((2, 128, 128), F32),
            pltpu.VMEM((2, 128, 128), F32),
            pltpu.VMEM((2, 128, 128), F32),
            pltpu.VMEM((3, 2, 128, 128), F32),
            pltpu.VMEM((6, 2, 128, 128), F32),
            pltpu.VMEM((384, 256), F32),
            pltpu.VMEM((NDEV, 2, 128), F32),
            pltpu.VMEM((NTM * 16, 128), F32),
            pltpu.VMEM((NTM * 16, 128), F32),
            pltpu.VMEM((3, 80, 128), F32),
            pltpu.VMEM((7, 80, 128), F32),
            pltpu.VMEM((6, 64, 128), F32),
            pltpu.VMEM((6, 64, 128), F32),
            pltpu.VMEM((NDEV, 1, 128), F32),
            dma, dma((NGROUP,)), dma, dma, dma, dma, dma((4,)), dma((4,)), dma, dma,
        ],
        compiler_params=pltpu.CompilerParams(collective_id=0, has_side_effects=True),
    )(
        samples.reshape(128, 256),
        pointing.reshape(128, 256),
        angles.reshape(128, 256),
        counts.reshape(1, 128),
        sky,
        prior_precision,
        omega_noise,
        omega_prior,
        *(jnp.asarray(t) for t in tables()),
    )
    binned = binned.reshape(3, 64, 2, 128).transpose(0, 2, 1, 3).reshape(3, 2, 8192)
    return (gain, binned, solved)


def solution(mesh):
    return jax.shard_map(
        per_device,
        mesh=mesh,
        in_specs=(
            P("det", "tm", None, None),
            P("det", "tm", None, None),
            P("det", "tm", None, None),
            P("det", "tm", None),
            P(None, ("det", "tm"), None),
            P(None, "det", "tm"),
            P(None, "det", "tm"),
            P(None, "det", "tm"),
        ),
        out_specs=(P("det", "tm"), P(None, ("det", "tm"), None), P(None, "det", "tm")),
        check_vma=False,
    )
```

```python
import math

import jax
import jax.numpy as jnp
import numpy as np
from jax import lax
from jax.experimental import pallas as pl
from jax.experimental.pallas import tpu as pltpu
from jax.sharding import PartitionSpec as P

MESH = pl.DeviceIdType.MESH
F32 = jnp.float32
BF16 = jnp.bfloat16
NDET = 4
NTM = 32
NDEV = NDET * NTM
GROUP = 16
NGROUP = NDEV // GROUP
UNROLL = 16
SHIFT = 4.0
SCALE = 4.0
STEP_MAX = 20.0


def tables():
    h, i = np.divmod(np.arange(128), 64)
    a = 2 * i + h
    k = np.arange(128)
    ang = 2.0 * np.pi * (np.outer(a, k) % 128) / 128
    first = np.concatenate([np.cos(ang), -np.sin(ang)], axis=1)
    b = np.arange(64)
    ang = 2.0 * np.pi * np.outer(b, k) / 8192
    twist = np.stack([np.cos(ang), np.sin(ang)])
    q = np.arange(32)
    ang = 2.0 * np.pi * (np.outer(q, b) % 64) / 64
    c, s = np.cos(ang), np.sin(ang)
    last = np.concatenate([np.concatenate([c, s], axis=1), np.concatenate([-s, c], axis=1)], axis=0)
    last = last / math.sqrt(8192)
    def split(x):
        upper = x.astype(np.float32).astype(jnp.bfloat16)
        return np.stack([upper, (x - upper.astype(np.float64)).astype(jnp.bfloat16)])

    return [split(first), twist.astype(np.float32), split(last)]


def split_parts(x):
    upper = x.astype(BF16)
    return upper, (x - upper.astype(F32)).astype(BF16)


def dot3(a, b):
    out = jnp.dot(a[0], b[0], preferred_element_type=F32)
    out = out + jnp.dot(a[0], b[1], preferred_element_type=F32)
    return out + jnp.dot(a[1], b[0], preferred_element_type=F32)


def sine_cosine(x):
    k = jnp.floor(x * (2.0 / math.pi) + 0.5)
    r = ((x - k * 1.5703125) - k * 4.837512969970703125e-4) - k * 7.549789948768648e-8
    z = r * r
    sine = r + r * z * (-1.6666654611e-1 + z * (8.3321608736e-3 - z * 1.9515295891e-4))
    cosine = 1.0 - 0.5 * z + z * z * (
        4.166664568298827e-2 + z * (-1.388731625493765e-3 + z * 2.443315711809948e-5)
    )
    q = k.astype(jnp.int32) & 3
    odd = (q & 1) == 1
    s = jnp.where(odd, cosine, sine)
    c = jnp.where(odd, sine, cosine)
    s = jnp.where(q >= 2, -s, s)
    c = jnp.where((q == 1) | (q == 2), -c, c)
    return s, c


def one_hot(row, rows):
    value = jnp.broadcast_to(row, (16, 128)).astype(BF16)
    index = lax.broadcasted_iota(jnp.int32, (rows, 128), 0).astype(F32).astype(BF16)
    same = index.reshape(rows // 16, 16, 128) == value[None]
    return jnp.where(same, jnp.ones((), BF16), jnp.zeros((), BF16)).reshape(rows, 128)


def kernel(
    samples, pointing, angles, counts, sky, prec, onoise, oprior, first, twist, last,
    gain_out, map_out, sol_out,
    sbuf, rbuf, table, hi_s, lo_s, cos_s, sin_s, look, sums_s, wsplit, acc,
    stat_r, spec_s, spec_r, pp, root_s, edge, bw, v1_s, v2_s, mom_r,
    send_sem, recv_sem, stat_send, stat_recv, spec_send, spec_recv,
    rim_send, rim_recv, edge_send, edge_recv, mom_send, mom_recv,
):
    det = lax.axis_index("det")
    tm = lax.axis_index("tm")
    me = det * NTM + tm

    ty, tz, tc = tm // 8, (tm // 2) % 4, tm % 2

    def hop(d):
        return jnp.where(d == 0, 2, jnp.where(d == 1, 1, jnp.where(d == 2, 3, 0)))

    def other_tm(e):
        y = (ty + hop(e // 8)) % 4
        z = (tz + hop((e // 2) % 4)) % 4
        return y * 8 + z * 2 + (tc + 1 - e % 2) % 2

    def to_all(act):
        @pl.loop(0, NTM - 1)
        def _(e):
            to = other_tm(e)
            for x in (2, 1, 3, 0):
                act(((det + x) % NDET, to))

        for x in (2, 1, 3):
            act(((det + x) % NDET, tm))

    barrier = pltpu.get_barrier_semaphore()
    to_all(lambda to: pl.semaphore_signal(barrier, inc=1, device_id=to, device_id_type=MESH))

    row_i = lax.broadcasted_iota(jnp.int32, (128, 128), 0)
    col_i = lax.broadcasted_iota(jnp.int32, (128, 128), 1)
    for half in range(2):
        lanes = slice(half * 128, half * 128 + 128)
        sbuf[pl.ds(half, 128, stride=8), :] = samples[:, lanes]
        sbuf[pl.ds(2 + half, 128, stride=8), :] = angles[:, lanes]
        sbuf[pl.ds(4 + half, 128, stride=8), :] = pointing[:, lanes].astype(F32)
    count_row = jnp.broadcast_to(counts[...].astype(F32), (128, 128))
    count_col = jnp.sum(jnp.where(row_i == col_i, count_row, 0.0), axis=1, keepdims=True)
    count_full = jnp.broadcast_to(count_col, (128, 128))
    sbuf[pl.ds(6, 128, stride=8), :] = count_full
    sbuf[pl.ds(7, 128, stride=8), :] = count_full

    for c in range(3):
        blocks = []
        for cyc in range(2):
            turned = sky[c, pl.ds(cyc, 64, stride=2), :].T
            blocks.append(jnp.concatenate([turned[:64], turned[64:]], axis=1))
        full = jnp.concatenate(blocks, axis=1)
        upper = full.astype(BF16)
        table[pl.ds(c * 64, 64), :] = upper
        table[pl.ds(192 + c * 64, 64), :] = (full - upper.astype(F32)).astype(BF16)

    pp[:, 8:72, :] = prec[...]
    bw[:, 0:8, :] = jnp.zeros((7, 8, 128), F32)
    bw[:, 72:80, :] = jnp.zeros((7, 8, 128), F32)

    @pl.when(det == 0)
    def _():
        pp[:, 0:8, :] = jnp.zeros((3, 8, 128), F32)
        edge[0] = jnp.zeros((12, 8, 128), F32)
        spec_r[0:32, :] = jnp.zeros((32, 128), F32)

    @pl.when(det == NDET - 1)
    def _():
        pp[:, 72:80, :] = jnp.zeros((3, 8, 128), F32)
        edge[1] = jnp.zeros((12, 8, 128), F32)
        spec_r[34 * 16 : 36 * 16, :] = jnp.zeros((32, 128), F32)

    acc[...] = jnp.zeros_like(acc)
    pl.semaphore_wait(barrier, NDEV - 1)

    my_group = me // GROUP
    my_slot = me % GROUP
    my_tile = rbuf.at[pl.ds(me * 8, 8)]

    def send_samples(group, v):
        slot = (my_slot + v) % GROUP
        pltpu.make_async_remote_copy(
            sbuf.at[pl.ds((group * GROUP + slot) * 8, 8)], my_tile, send_sem, recv_sem.at[my_group],
            device_id=(group // 2, (group % 2) * GROUP + slot), device_id_type=MESH,
        ).start()

    for v in range(1, GROUP):
        send_samples(my_group, v)

    @pl.loop(1, NGROUP)
    def _(t):
        group = (my_group + NGROUP - t) % NGROUP
        for v in range(GROUP):
            send_samples(group, v)

    rbuf[pl.ds(me * 8, 8), :] = sbuf[pl.ds(me * 8, 8), :]

    down = ((det + 1) % NDET, tm)
    up = ((det + NDET - 1) % NDET, tm)

    def edge_copies(rows, side, padded, to):
        pairs = (
            (prec.at[:, rows, :], pp.at[:, padded, :]),
            (onoise.at[:, rows, :], edge.at[side, 0:6]),
            (oprior.at[:, rows, :], edge.at[side, 6:12]),
        )
        return [
            pltpu.make_async_remote_copy(
                src, dst, edge_send.at[side, i], edge_recv.at[side, i], device_id=to, device_id_type=MESH
            )
            for i, (src, dst) in enumerate(pairs)
        ]

    go_down = edge_copies(slice(56, 64), 0, slice(0, 8), down)
    go_up = edge_copies(slice(0, 8), 1, slice(72, 80), up)

    @pl.when(det < NDET - 1)
    def _():
        for copy in go_down:
            copy.start()

    @pl.when(det > 0)
    def _():
        for copy in go_up:
            copy.start()

    col_index = lax.broadcasted_iota(jnp.int32, (64, 128), 0).astype(F32)

    slot_index = lax.broadcasted_iota(jnp.int32, (GROUP, 128), 1).astype(F32)

    def gather_group(group):
        base = group * GROUP
        here = pl.ds(base, GROUP)

        def row(r):
            return rbuf[pl.ds(base * 8 + r, GROUP, stride=8), :]

        for half in range(2):
            pixel = row(4 + half).astype(jnp.int32)
            upper = (pixel >> 13) * 128 + ((pixel >> 6) & 1) * 64 + ((pixel >> 7) & 63)
            hi_s[half, here, :] = upper.astype(F32)
            lo_s[half, here, :] = (pixel & 63).astype(F32)
            sine, cosine = sine_cosine(2.0 * row(2 + half))
            sin_s[half, here, :] = sine
            cos_s[half, here, :] = cosine
        for first_s in range(0, GROUP, UNROLL):
            for u in range(UNROLL):
                s = base + first_s + u
                hots = [one_hot(hi_s[half, pl.ds(s, 1), :], 256) for half in range(2)]
                got = jnp.dot(table[...], jnp.concatenate(hots, axis=1), preferred_element_type=F32)
                got = got[:192] + got[192:]
                for half in range(2):
                    low = lo_s[half, pl.ds(s, 1), :]
                    same = col_index == low
                    for c in range(3):
                        part = got[c * 64 : c * 64 + 64, half * 128 : half * 128 + 128]
                        look[c, half, pl.ds(s, 1), :] = jnp.sum(
                            jnp.where(same, part, 0.0), axis=0, keepdims=True
                        )
        count = row(6)
        cross = jnp.zeros((GROUP, 128), F32)
        square = jnp.zeros((GROUP, 128), F32)
        for half in range(2):
            signal = (
                look[0, half, here, :]
                + look[1, half, here, :] * cos_s[half, here, :]
                + look[2, half, here, :] * sin_s[half, here, :]
            )
            look[0, half, here, :] = signal
            masked = jnp.where(slot_index + 128.0 * half < count, signal, 0.0)
            cross = cross + masked * row(half)
            square = square + masked * signal
        sums_s[0, here, :] = cross
        sums_s[1, here, :] = square

    @pl.loop(0, NGROUP)
    def _(t):
        group = (my_group + t) % NGROUP

        @pl.when(t == 0)
        def _():
            span = rbuf.at[pl.ds(0, (GROUP - 1) * 8)]
            pltpu.make_async_copy(span, span, recv_sem.at[my_group]).wait()

        @pl.when(t > 0)
        def _():
            span = rbuf.at[pl.ds(0, GROUP * 8)]
            pltpu.make_async_copy(span, span, recv_sem.at[group]).wait()

        gather_group(group)

    cross = jnp.sum(sums_s[0].T, axis=0, keepdims=True)
    square = jnp.sum(sums_s[1].T, axis=0, keepdims=True)
    mine = stat_r.at[me]
    mine[...] = jnp.concatenate([cross, square], axis=0)
    to_all(
        lambda to: pltpu.make_async_remote_copy(
            mine, mine, stat_send, stat_recv, device_id=to, device_id_type=MESH
        ).start()
    )
    count = rbuf[pl.ds(6, 128, stride=8), :]
    slot = col_i.astype(F32)
    rest = stat_r.at[pl.ds(0, NDEV - 1)]
    pltpu.make_async_copy(rest, rest, stat_recv).wait()
    total = jnp.sum(stat_r[...], axis=0)
    gains = total[0:1] / (total[1:2] + 1e-06)
    lane = lax.broadcasted_iota(jnp.int32, (1, 128), 1)
    gain_out[...] = jnp.sum(jnp.where(lane == me, gains, 0.0), axis=1, keepdims=True)
    gain_full = jnp.broadcast_to(gains, (128, 128)).T

    hits = [jnp.zeros((1, 128), F32) for _ in range(2)]
    for half in range(2):
        data = rbuf[pl.ds(half, 128, stride=8), :]
        good = slot + 128.0 * half < count
        residual = jnp.where(good, data - gain_full * look[0, half], 0.0)
        for c, weight in enumerate((residual, residual * cos_s[half], residual * sin_s[half])):
            upper = weight.astype(BF16).astype(F32)
            wsplit[c, half] = upper
            wsplit[3 + c, half] = weight - upper
        late = jnp.where(hi_s[half] >= 128.0, 1.0, 0.0)
        valid = jnp.where(good, 1.0, 0.0)
        hits[1] = hits[1] + jnp.sum(valid * late, axis=0, keepdims=True)
        hits[0] = hits[0] + jnp.sum(valid * (1.0 - late), axis=0, keepdims=True)

    low_index = lax.broadcasted_iota(jnp.int32, (64, 128), 0).astype(F32).astype(BF16).reshape(4, 16, 128)

    @pl.loop(0, NDEV // UNROLL)
    def _(step):
        lefts = []
        rights = []
        for u in range(UNROLL):
            s = step * UNROLL + u
            for half in range(2):
                rights.append(one_hot(hi_s[half, pl.ds(s, 1), :], 256))
                low = jnp.broadcast_to(lo_s[half, pl.ds(s, 1), :], (16, 128)).astype(BF16)
                same = low_index == low[None]
                rows = []
                for w in range(6):
                    value = jnp.broadcast_to(wsplit[w, half, pl.ds(s, 1), :], (16, 128)).astype(BF16)
                    rows.append(jnp.where(same, value[None], jnp.zeros((), BF16)).reshape(64, 128))
                lefts.append(jnp.concatenate(rows, axis=0))
        acc[...] += lax.dot_general(
            jnp.concatenate(lefts, axis=1), jnp.concatenate(rights, axis=1),
            (((1,), (1,)), ((), ())), preferred_element_type=F32,
        )

    field = acc[:192] + acc[192:]

    z_parts = []
    for cyc in range(2):
        y = dot3(split_parts(field[:, cyc * 128 : cyc * 128 + 128]), (first[0], first[1]))
        for c in range(3):
            y_re = y[c * 64 : c * 64 + 64, :128]
            y_im = y[c * 64 : c * 64 + 64, 128:]
            z_re = y_re * twist[0] + y_im * twist[1]
            z_im = y_im * twist[0] - y_re * twist[1]
            z_parts.append(jnp.concatenate([z_re, z_im], axis=0))
    x = dot3((last[0], last[1]), split_parts(jnp.concatenate(z_parts, axis=1)))
    for cyc in range(2):
        for c in range(3):
            block = x[:, (cyc * 3 + c) * 128 : (cyc * 3 + c) * 128 + 128]
            spec_s[pl.ds(4 * c + cyc, 32, stride=16), :] = block[:32]
            spec_s[pl.ds(4 * c + 2 + cyc, 32, stride=16), :] = block[32:]
        weight = jnp.sum(hits[cyc], axis=1, keepdims=True) * (1.0 / 8192)
        spec_s[pl.ds(12 + cyc, 32, stride=16), :] = jnp.broadcast_to(weight, (32, 128))
        spec_s[pl.ds(14 + cyc, 32, stride=16), :] = jnp.broadcast_to(weight, (32, 128))

    def send_spectrum(where, to, slot, send, recv):
        pltpu.make_async_remote_copy(
            spec_s.at[pl.ds(to * 16, 16)], spec_r.at[pl.ds(slot * 16, 16)],
            send, recv, device_id=(where, to), device_id_type=MESH,
        ).start()

    low_end = jnp.logical_and(tm < 2, det > 0)
    high_end = jnp.logical_and(tm >= NTM - 2, det < NDET - 1)

    @pl.when(low_end)
    def _():
        @pl.loop(0, NTM)
        def _(e):
            send_spectrum(det - 1, other_tm(e), 34 + tm, rim_send, rim_recv.at[1])

    @pl.when(high_end)
    def _():
        @pl.loop(0, NTM)
        def _(e):
            send_spectrum(det + 1, other_tm(e), tm - (NTM - 2), rim_send, rim_recv.at[0])

    @pl.loop(0, NTM - 1)
    def _(e):
        send_spectrum(det, other_tm(e), 2 + tm, spec_send, spec_recv)

    spec_r[pl.ds((2 + tm) * 16, 16), :] = spec_s[pl.ds(tm * 16, 16), :]
    for c in range(3):
        for cyc in range(2):
            part = field[c * 64 : c * 64 + 64, cyc * 128 : cyc * 128 + 128]
            part = jnp.concatenate([part[:, :64], part[:, 64:]], axis=0)
            map_out[c, pl.ds(cyc, 64, stride=2), :] = part.T

    @pl.when(det > 0)
    def _():
        for copy in go_down:
            copy.wait_recv()

    @pl.when(det < NDET - 1)
    def _():
        for copy in go_up:
            copy.wait_recv()

    for c in range(3):
        root_s[c] = jnp.sqrt(pp[c])

    @pl.when(det > 0)
    def _():
        span = spec_r.at[pl.ds(0, 32)]
        pltpu.make_async_copy(span, span, rim_recv.at[0]).wait()

    @pl.when(det < NDET - 1)
    def _():
        span = spec_r.at[pl.ds(0, 32)]
        pltpu.make_async_copy(span, span, rim_recv.at[1]).wait()

    span = spec_r.at[pl.ds(0, (NTM - 1) * 16)]
    pltpu.make_async_copy(span, span, spec_recv).wait()

    for cyc in range(2):
        for j in range(7):
            bw[j, pl.ds(4 + cyc, 36, stride=2), :] = spec_r[pl.ds(2 * j + cyc, 36, stride=16), :]
    noise_root = jnp.sqrt(bw[6])
    for j in range(6):
        noise = jnp.concatenate([edge[0, j], onoise[j], edge[1, j]], axis=0)
        prior = jnp.concatenate([edge[0, 6 + j], oprior[j], edge[1, 6 + j]], axis=0)
        bw[j] = bw[j] + noise_root * noise + root_s[j // 2] * prior

    moments = [jnp.zeros((8, 128), F32) for _ in range(6)]
    for c in range(3):
        precision = pp[c]
        root = root_s[c]
        side = root * (0.45 / SCALE)
        diagonal = (precision + bw[6] - SHIFT) * (1.0 / SCALE)

        def step(v):
            u = root * v
            beside = pltpu.roll(u, 1, 0) + pltpu.roll(u, 79, 0)
            return diagonal * v - side * beside

        for p in range(2):
            j = 2 * c + p
            v0 = bw[j]
            v1 = step(v0)
            v2 = step(v1)
            v3 = step(v2)
            own = [v[8:72] for v in (v0, v1, v2, v3)]
            v1_s[j] = own[1]
            v2_s[j] = own[2]
            for m, (a, b) in enumerate(((0, 0), (0, 1), (1, 1), (1, 2), (2, 2), (2, 3))):
                moments[m] = moments[m] + jnp.sum((own[a] * own[b]).reshape(8, 8, 128), axis=0)
    message = jnp.zeros((1, 128), F32)
    for m in range(6):
        value = jnp.sum(jnp.sum(moments[m], axis=0, keepdims=True), axis=1, keepdims=True)
        message = jnp.where(lane == m, jnp.broadcast_to(value, (1, 128)), message)
    own_row = mom_r.at[me]
    own_row[...] = message
    to_all(
        lambda to: pltpu.make_async_remote_copy(
            own_row, own_row, mom_send, mom_recv, device_id=to, device_id_type=MESH
        ).start()
    )
    rest = mom_r.at[pl.ds(0, NDEV - 1)]
    pltpu.make_async_copy(rest, rest, mom_recv).wait()
    sums = jnp.sum(mom_r[...], axis=0)
    nu = [jnp.sum(jnp.where(lane == m, sums, 0.0), axis=1, keepdims=True) for m in range(6)]

    zero = jnp.zeros((1, 1), F32)

    def inner(a, b):
        terms = {}
        for i, x_i in enumerate(a):
            for j, y_j in enumerate(b):
                terms[i + j] = terms.get(i + j, zero) + x_i * y_j
        out = zero
        for power, value in terms.items():
            out = out + value * nu[power]
        return out

    def image_of(a):
        longer = list(a) + [zero]
        return [SHIFT * longer[i] + (SCALE * longer[i - 1] if i else zero) for i in range(len(longer))]

    resid = [zero + 1.0]
    direction = [zero + 1.0]
    answer = [zero, zero, zero]
    norm_now = nu[0]
    for iteration in range(3):
        image = image_of(direction)
        alpha = norm_now / inner(direction, image)
        alpha = jnp.minimum(jnp.maximum(alpha, 0.0), STEP_MAX)
        for i, value in enumerate(direction):
            answer[i] = answer[i] + alpha * value
        if iteration < 2:
            resid = resid + [zero]
            resid = [r - alpha * w for r, w in zip(resid, image)]
            norm_next = jnp.maximum(inner(resid, resid), 0.0)
            beta = norm_next / norm_now
            direction = [r + beta * d for r, d in zip(resid, direction + [zero])]
            norm_now = norm_next
    for j in range(6):
        sol_out[j] = answer[0] * bw[j, 8:72, :] + answer[1] * v1_s[j] + answer[2] * v2_s[j]

    span = sbuf.at[pl.ds(0, (NDEV - 1) * 8)]
    pltpu.make_async_copy(span, span, send_sem).wait()
    rest = stat_r.at[pl.ds(0, NDEV - 1)]
    pltpu.make_async_copy(rest, rest, stat_send).wait()
    span = spec_s.at[pl.ds(0, (NTM - 1) * 16)]
    pltpu.make_async_copy(span, span, spec_send).wait()
    rest = mom_r.at[pl.ds(0, NDEV - 1)]
    pltpu.make_async_copy(rest, rest, mom_send).wait()

    @pl.when(jnp.logical_or(low_end, high_end))
    def _():
        span = spec_s.at[pl.ds(0, NTM * 16)]
        pltpu.make_async_copy(span, span, rim_send).wait()

    @pl.when(det < NDET - 1)
    def _():
        for copy in go_down:
            copy.wait_send()

    @pl.when(det > 0)
    def _():
        for copy in go_up:
            copy.wait_send()


def per_device(
    samples, pointing, angles, counts, sky_map, prior_precision, omega_noise, omega_prior
):
    sky = sky_map.reshape(3, 2, 64, 128).transpose(0, 2, 1, 3).reshape(3, 128, 128)
    vmem = pl.BlockSpec(memory_space=pltpu.VMEM)
    dma = pltpu.SemaphoreType.DMA
    gain, binned, solved = pl.pallas_call(
        kernel,
        name="gibbs_step",
        out_shape=(
            jax.ShapeDtypeStruct((1, 1), F32),
            jax.ShapeDtypeStruct((3, 128, 128), F32),
            jax.ShapeDtypeStruct((6, 64, 128), F32),
        ),
        in_specs=[vmem] * 11,
        out_specs=(vmem, vmem, vmem),
        scratch_shapes=[
            pltpu.VMEM((1024, 128), F32),
            pltpu.VMEM((1024, 128), F32),
            pltpu.VMEM((384, 256), BF16),
            pltpu.VMEM((2, 128, 128), F32),
            pltpu.VMEM((2, 128, 128), F32),
            pltpu.VMEM((2, 128, 128), F32),
            pltpu.VMEM((2, 128, 128), F32),
            pltpu.VMEM((3, 2, 128, 128), F32),
            pltpu.VMEM((2, 128, 128), F32),
            pltpu.VMEM((6, 2, 128, 128), F32),
            pltpu.VMEM((384, 256), F32),
            pltpu.VMEM((NDEV, 2, 128), F32),
            pltpu.VMEM((NTM * 16, 128), F32),
            pltpu.VMEM(((NTM + 4) * 16, 128), F32),
            pltpu.VMEM((3, 80, 128), F32),
            pltpu.VMEM((3, 80, 128), F32),
            pltpu.VMEM((2, 12, 8, 128), F32),
            pltpu.VMEM((7, 80, 128), F32),
            pltpu.VMEM((6, 64, 128), F32),
            pltpu.VMEM((6, 64, 128), F32),
            pltpu.VMEM((NDEV, 1, 128), F32),
            dma, dma((NGROUP,)), dma, dma, dma, dma,
            dma, dma((2,)), dma((2, 3)), dma((2, 3)), dma, dma,
        ],
        compiler_params=pltpu.CompilerParams(collective_id=0, has_side_effects=True),
    )(
        samples.reshape(128, 256),
        pointing.reshape(128, 256),
        angles.reshape(128, 256),
        counts.reshape(1, 128),
        sky,
        prior_precision,
        omega_noise,
        omega_prior,
        *(jnp.asarray(t) for t in tables()),
    )
    binned = binned.reshape(3, 64, 2, 128).transpose(0, 2, 1, 3).reshape(3, 2, 8192)
    return (gain, binned, solved)


def solution(mesh):
    return jax.shard_map(
        per_device,
        mesh=mesh,
        in_specs=(
            P("det", "tm", None, None),
            P("det", "tm", None, None),
            P("det", "tm", None, None),
            P("det", "tm", None),
            P(None, ("det", "tm"), None),
            P(None, "det", "tm"),
            P(None, "det", "tm"),
            P(None, "det", "tm"),
        ),
        out_specs=(P("det", "tm"), P(None, ("det", "tm"), None), P(None, "det", "tm")),
        check_vma=False,
    )
```

```python
import math

import jax
import jax.numpy as jnp
import numpy as np
from jax import lax
from jax.experimental import pallas as pl
from jax.experimental.pallas import tpu as pltpu
from jax.sharding import PartitionSpec as P

MESH = pl.DeviceIdType.MESH
F32 = jnp.float32
BF16 = jnp.bfloat16
NDET = 4
NTM = 32
NDEV = NDET * NTM
GROUP = 16
NGROUP = NDEV // GROUP
UNROLL = 16
SHIFT = 4.0
SCALE = 4.0
STEP_MAX = 20.0


def tables():
    h, i = np.divmod(np.arange(128), 64)
    a = 2 * i + h
    k = np.arange(128)
    ang = 2.0 * np.pi * (np.outer(a, k) % 128) / 128
    first = np.concatenate([np.cos(ang), -np.sin(ang)], axis=1)
    b = np.arange(64)
    ang = 2.0 * np.pi * np.outer(b, k) / 8192
    twist = np.stack([np.cos(ang), np.sin(ang)])
    q = np.arange(32)
    ang = 2.0 * np.pi * (np.outer(q, b) % 64) / 64
    c, s = np.cos(ang), np.sin(ang)
    last = np.concatenate([np.concatenate([c, s], axis=1), np.concatenate([-s, c], axis=1)], axis=0)
    last = last / math.sqrt(8192)
    def split(x):
        upper = x.astype(np.float32).astype(jnp.bfloat16)
        return np.stack([upper, (x - upper.astype(np.float64)).astype(jnp.bfloat16)])

    return [split(first), twist.astype(np.float32), split(last)]


def split_parts(x):
    upper = x.astype(BF16)
    return upper, (x - upper.astype(F32)).astype(BF16)


def dot3(a, b):
    out = jnp.dot(a[0], b[0], preferred_element_type=F32)
    out = out + jnp.dot(a[0], b[1], preferred_element_type=F32)
    return out + jnp.dot(a[1], b[0], preferred_element_type=F32)


def sine_cosine(x):
    k = jnp.floor(x * (2.0 / math.pi) + 0.5)
    r = ((x - k * 1.5703125) - k * 4.837512969970703125e-4) - k * 7.549789948768648e-8
    z = r * r
    sine = r + r * z * (-1.6666654611e-1 + z * (8.3321608736e-3 - z * 1.9515295891e-4))
    cosine = 1.0 - 0.5 * z + z * z * (
        4.166664568298827e-2 + z * (-1.388731625493765e-3 + z * 2.443315711809948e-5)
    )
    q = k.astype(jnp.int32) & 3
    odd = (q & 1) == 1
    s = jnp.where(odd, cosine, sine)
    c = jnp.where(odd, sine, cosine)
    s = jnp.where(q >= 2, -s, s)
    c = jnp.where((q == 1) | (q == 2), -c, c)
    return s, c


def one_hot(row, rows):
    value = jnp.broadcast_to(row, (16, 128)).astype(BF16)
    index = lax.broadcasted_iota(jnp.int32, (rows, 128), 0).astype(F32).astype(BF16)
    same = index.reshape(rows // 16, 16, 128) == value[None]
    return jnp.where(same, jnp.ones((), BF16), jnp.zeros((), BF16)).reshape(rows, 128)


def kernel(
    samples_in, pointing_in, angles_in, counts_in, sky_in, prec, onoise_in, oprior_in,
    first_in, twist_in, last_in,
    gain_out, map_upper_out, map_lower_out, sol_out,
    samples, pointing, angles, counts, sky, onoise, oprior, first, twist, last, map_s, sol_s,
    sbuf, rbuf, table, hi_s, lo_s, cos_s, sin_s, look, sums_s, wsplit, acc,
    stat_r, spec_s, spec_r, pp, root_s, edge, bw, v1_s, v2_s, mom_r,
    send_sem, recv_sem, stat_send, stat_recv, spec_send, spec_recv,
    rim_send, rim_recv, edge_send, edge_recv, mom_send, mom_recv, in_sem, out_sem,
):
    det = lax.axis_index("det")
    tm = lax.axis_index("tm")
    me = det * NTM + tm

    loads = [
        pltpu.make_async_copy(src, dst, in_sem.at[i])
        for i, (src, dst) in enumerate((
            (samples_in, samples), (pointing_in, pointing), (angles_in, angles), (counts_in, counts),
            (sky_in, sky), (prec, pp.at[:, 8:72, :]), (first_in, first), (twist_in, twist),
            (last_in, last), (onoise_in, onoise), (oprior_in, oprior),
        ))
    ]
    for load in loads:
        load.start()

    ty, tz, tc = tm // 8, (tm // 2) % 4, tm % 2
    at_z = [(tz + o) % 4 * 2 for o in range(4)]
    at_c = [tc, 1 - tc]
    at_det = [(det + o) % NDET for o in range(NDET)]

    def to_tm(act):
        def row(y, own):
            for z in (2, 1, 3, 0):
                for c in (1, 0):
                    if not (own and z == 0 and c == 0):
                        act(y * 8 + at_z[z] + at_c[c])

        @pl.loop(0, 3)
        def _(d):
            row((ty + jnp.where(d == 0, 2, jnp.where(d == 1, 1, 3))) % 4, False)

        row(ty, True)

    def to_all(act):
        to_tm(lambda to: [act((at_det[x], to)) for x in (2, 1, 3, 0)])
        for x in (2, 1, 3):
            act((at_det[x], tm))

    barrier = pltpu.get_barrier_semaphore()
    to_all(lambda to: pl.semaphore_signal(barrier, inc=1, device_id=to, device_id_type=MESH))

    for load in loads[:4]:
        load.wait()

    row_i = lax.broadcasted_iota(jnp.int32, (128, 128), 0)
    col_i = lax.broadcasted_iota(jnp.int32, (128, 128), 1)
    for half in range(2):
        lanes = slice(half * 128, half * 128 + 128)
        sbuf[pl.ds(half, 128, stride=8), :] = samples[:, lanes]
        sbuf[pl.ds(2 + half, 128, stride=8), :] = angles[:, lanes]
        sbuf[pl.ds(4 + half, 128, stride=8), :] = pointing[:, lanes].astype(F32)
    count_row = jnp.broadcast_to(counts[...].astype(F32), (128, 128))
    count_col = jnp.sum(jnp.where(row_i == col_i, count_row, 0.0), axis=1, keepdims=True)
    count_full = jnp.broadcast_to(count_col, (128, 128))
    sbuf[pl.ds(6, 128, stride=8), :] = count_full
    sbuf[pl.ds(7, 128, stride=8), :] = count_full

    loads[4].wait()

    for c in range(3):
        blocks = []
        for cyc in range(2):
            turned = sky[c, pl.ds(cyc, 64, stride=2), :].T
            blocks.append(jnp.concatenate([turned[:64], turned[64:]], axis=1))
        full = jnp.concatenate(blocks, axis=1)
        upper = full.astype(BF16)
        table[pl.ds(c * 64, 64), :] = upper
        table[pl.ds(192 + c * 64, 64), :] = (full - upper.astype(F32)).astype(BF16)

    bw[:, 0:8, :] = jnp.zeros((7, 8, 128), F32)
    bw[:, 72:80, :] = jnp.zeros((7, 8, 128), F32)

    @pl.when(det == 0)
    def _():
        pp[:, 0:8, :] = jnp.zeros((3, 8, 128), F32)
        edge[0] = jnp.zeros((12, 8, 128), F32)
        spec_r[0:32, :] = jnp.zeros((32, 128), F32)

    @pl.when(det == NDET - 1)
    def _():
        pp[:, 72:80, :] = jnp.zeros((3, 8, 128), F32)
        edge[1] = jnp.zeros((12, 8, 128), F32)
        spec_r[34 * 16 : 36 * 16, :] = jnp.zeros((32, 128), F32)

    acc[...] = jnp.zeros_like(acc)
    pl.semaphore_wait(barrier, NDEV - 1)

    my_group = me // GROUP
    my_slot = me % GROUP
    my_tile = rbuf.at[pl.ds(me * 8, 8)]

    def send_samples(group, v):
        slot = (my_slot + v) % GROUP
        pltpu.make_async_remote_copy(
            sbuf.at[pl.ds((group * GROUP + slot) * 8, 8)], my_tile, send_sem, recv_sem.at[my_group],
            device_id=(group // 2, (group % 2) * GROUP + slot), device_id_type=MESH,
        ).start()

    for v in range(1, GROUP):
        send_samples(my_group, v)

    @pl.loop(1, NGROUP)
    def _(t):
        group = (my_group + NGROUP - t) % NGROUP
        for v in range(GROUP):
            send_samples(group, v)

    rbuf[pl.ds(me * 8, 8), :] = sbuf[pl.ds(me * 8, 8), :]

    down = ((det + 1) % NDET, tm)
    up = ((det + NDET - 1) % NDET, tm)

    def edge_copies(rows, side, padded, to):
        pairs = (
            (prec.at[:, rows, :], pp.at[:, padded, :]),
            (onoise_in.at[:, rows, :], edge.at[side, 0:6]),
            (oprior_in.at[:, rows, :], edge.at[side, 6:12]),
        )
        return [
            pltpu.make_async_remote_copy(
                src, dst, edge_send.at[side, i], edge_recv.at[side, i], device_id=to, device_id_type=MESH
            )
            for i, (src, dst) in enumerate(pairs)
        ]

    go_down = edge_copies(slice(56, 64), 0, slice(0, 8), down)
    go_up = edge_copies(slice(0, 8), 1, slice(72, 80), up)

    @pl.when(det < NDET - 1)
    def _():
        for copy in go_down:
            copy.start()

    @pl.when(det > 0)
    def _():
        for copy in go_up:
            copy.start()

    col_index = lax.broadcasted_iota(jnp.int32, (64, 128), 0).astype(F32)

    slot_index = lax.broadcasted_iota(jnp.int32, (GROUP, 128), 1).astype(F32)

    def gather_group(group):
        base = group * GROUP
        here = pl.ds(base, GROUP)

        def row(r):
            return rbuf[pl.ds(base * 8 + r, GROUP, stride=8), :]

        for half in range(2):
            pixel = row(4 + half).astype(jnp.int32)
            upper = (pixel >> 13) * 128 + ((pixel >> 6) & 1) * 64 + ((pixel >> 7) & 63)
            hi_s[half, here, :] = upper.astype(F32)
            lo_s[half, here, :] = (pixel & 63).astype(F32)
            sine, cosine = sine_cosine(2.0 * row(2 + half))
            sin_s[half, here, :] = sine
            cos_s[half, here, :] = cosine
        for first_s in range(0, GROUP, UNROLL):
            for u in range(UNROLL):
                s = base + first_s + u
                hots = [one_hot(hi_s[half, pl.ds(s, 1), :], 256) for half in range(2)]
                got = jnp.dot(table[...], jnp.concatenate(hots, axis=1), preferred_element_type=F32)
                got = got[:192] + got[192:]
                for half in range(2):
                    low = lo_s[half, pl.ds(s, 1), :]
                    same = col_index == low
                    for c in range(3):
                        part = got[c * 64 : c * 64 + 64, half * 128 : half * 128 + 128]
                        look[c, half, pl.ds(s, 1), :] = jnp.sum(
                            jnp.where(same, part, 0.0), axis=0, keepdims=True
                        )
        count = row(6)
        cross = jnp.zeros((GROUP, 128), F32)
        square = jnp.zeros((GROUP, 128), F32)
        for half in range(2):
            signal = (
                look[0, half, here, :]
                + look[1, half, here, :] * cos_s[half, here, :]
                + look[2, half, here, :] * sin_s[half, here, :]
            )
            look[0, half, here, :] = signal
            masked = jnp.where(slot_index + 128.0 * half < count, signal, 0.0)
            cross = cross + masked * row(half)
            square = square + masked * signal
        sums_s[0, here, :] = cross
        sums_s[1, here, :] = square

    @pl.loop(0, NGROUP)
    def _(t):
        group = (my_group + t) % NGROUP

        @pl.when(t == 0)
        def _():
            span = rbuf.at[pl.ds(0, (GROUP - 1) * 8)]
            pltpu.make_async_copy(span, span, recv_sem.at[my_group]).wait()

        @pl.when(t > 0)
        def _():
            span = rbuf.at[pl.ds(0, GROUP * 8)]
            pltpu.make_async_copy(span, span, recv_sem.at[group]).wait()

        gather_group(group)

    cross = jnp.sum(sums_s[0].T, axis=0, keepdims=True)
    square = jnp.sum(sums_s[1].T, axis=0, keepdims=True)
    mine = stat_r.at[me]
    mine[...] = jnp.concatenate([cross, square], axis=0)
    to_all(
        lambda to: pltpu.make_async_remote_copy(
            mine, mine, stat_send, stat_recv, device_id=to, device_id_type=MESH
        ).start()
    )
    count = rbuf[pl.ds(6, 128, stride=8), :]
    slot = col_i.astype(F32)
    rest = stat_r.at[pl.ds(0, NDEV - 1)]
    pltpu.make_async_copy(rest, rest, stat_recv).wait()
    total = jnp.sum(stat_r[...], axis=0)
    gains = total[0:1] / (total[1:2] + 1e-06)
    lane = lax.broadcasted_iota(jnp.int32, (1, 128), 1)
    gain_out[...] = jnp.sum(jnp.where(lane == me, gains, 0.0), axis=1, keepdims=True)
    gain_full = jnp.broadcast_to(gains, (128, 128)).T

    hits = [jnp.zeros((1, 128), F32) for _ in range(2)]
    for half in range(2):
        data = rbuf[pl.ds(half, 128, stride=8), :]
        good = slot + 128.0 * half < count
        residual = jnp.where(good, data - gain_full * look[0, half], 0.0)
        for c, weight in enumerate((residual, residual * cos_s[half], residual * sin_s[half])):
            upper = weight.astype(BF16).astype(F32)
            wsplit[c, half] = upper
            wsplit[3 + c, half] = weight - upper
        late = jnp.where(hi_s[half] >= 128.0, 1.0, 0.0)
        valid = jnp.where(good, 1.0, 0.0)
        hits[1] = hits[1] + jnp.sum(valid * late, axis=0, keepdims=True)
        hits[0] = hits[0] + jnp.sum(valid * (1.0 - late), axis=0, keepdims=True)

    low_index = lax.broadcasted_iota(jnp.int32, (64, 128), 0).astype(F32).astype(BF16).reshape(4, 16, 128)

    @pl.loop(0, NDEV // UNROLL)
    def _(step):
        lefts = []
        rights = []
        for u in range(UNROLL):
            s = step * UNROLL + u
            for half in range(2):
                rights.append(one_hot(hi_s[half, pl.ds(s, 1), :], 256))
                low = jnp.broadcast_to(lo_s[half, pl.ds(s, 1), :], (16, 128)).astype(BF16)
                same = low_index == low[None]
                rows = []
                for w in range(6):
                    value = jnp.broadcast_to(wsplit[w, half, pl.ds(s, 1), :], (16, 128)).astype(BF16)
                    rows.append(jnp.where(same, value[None], jnp.zeros((), BF16)).reshape(64, 128))
                lefts.append(jnp.concatenate(rows, axis=0))
        acc[...] += lax.dot_general(
            jnp.concatenate(lefts, axis=1), jnp.concatenate(rights, axis=1),
            (((1,), (1,)), ((), ())), preferred_element_type=F32,
        )

    field = acc[:192] + acc[192:]

    for load in loads[6:9]:
        load.wait()
    z_parts = []
    for cyc in range(2):
        y = dot3(split_parts(field[:, cyc * 128 : cyc * 128 + 128]), (first[0], first[1]))
        for c in range(3):
            y_re = y[c * 64 : c * 64 + 64, :128]
            y_im = y[c * 64 : c * 64 + 64, 128:]
            z_re = y_re * twist[0] + y_im * twist[1]
            z_im = y_im * twist[0] - y_re * twist[1]
            z_parts.append(jnp.concatenate([z_re, z_im], axis=0))
    x = dot3((last[0], last[1]), split_parts(jnp.concatenate(z_parts, axis=1)))
    for cyc in range(2):
        for c in range(3):
            block = x[:, (cyc * 3 + c) * 128 : (cyc * 3 + c) * 128 + 128]
            spec_s[pl.ds(4 * c + cyc, 32, stride=16), :] = block[:32]
            spec_s[pl.ds(4 * c + 2 + cyc, 32, stride=16), :] = block[32:]
        weight = jnp.sum(hits[cyc], axis=1, keepdims=True) * (1.0 / 8192)
        spec_s[pl.ds(12 + cyc, 32, stride=16), :] = jnp.broadcast_to(weight, (32, 128))
        spec_s[pl.ds(14 + cyc, 32, stride=16), :] = jnp.broadcast_to(weight, (32, 128))

    def send_spectrum(where, to, slot, send, recv):
        pltpu.make_async_remote_copy(
            spec_s.at[pl.ds(to * 16, 16)], spec_r.at[pl.ds(slot * 16, 16)],
            send, recv, device_id=(where, to), device_id_type=MESH,
        ).start()

    low_end = jnp.logical_and(tm < 2, det > 0)
    high_end = jnp.logical_and(tm >= NTM - 2, det < NDET - 1)

    @pl.when(low_end)
    def _():
        send = lambda to: send_spectrum(det - 1, to, 34 + tm, rim_send, rim_recv.at[1])
        to_tm(send)
        send(tm)

    @pl.when(high_end)
    def _():
        send = lambda to: send_spectrum(det + 1, to, tm - (NTM - 2), rim_send, rim_recv.at[0])
        to_tm(send)
        send(tm)

    to_tm(lambda to: send_spectrum(det, to, 2 + tm, spec_send, spec_recv))

    spec_r[pl.ds((2 + tm) * 16, 16), :] = spec_s[pl.ds(tm * 16, 16), :]
    for c in range(3):
        for cyc in range(2):
            for part in range(2):
                rows = pl.ds(part * 192 + c * 64, 64)
                block = acc[rows, cyc * 128 : cyc * 128 + 128]
                block = jnp.concatenate([block[:, :64], block[:, 64:]], axis=0)
                map_s[part, c, pl.ds(cyc, 64, stride=2), :] = block.T
    stores = [
        pltpu.make_async_copy(map_s.at[0], map_upper_out, out_sem.at[0]),
        pltpu.make_async_copy(map_s.at[1], map_lower_out, out_sem.at[1]),
        pltpu.make_async_copy(sol_s, sol_out, out_sem.at[2]),
    ]
    stores[0].start()
    stores[1].start()
    loads[5].wait()
    loads[9].wait()
    loads[10].wait()

    @pl.when(det > 0)
    def _():
        for copy in go_down:
            copy.wait_recv()

    @pl.when(det < NDET - 1)
    def _():
        for copy in go_up:
            copy.wait_recv()

    for c in range(3):
        root_s[c] = jnp.sqrt(pp[c])

    @pl.when(det > 0)
    def _():
        span = spec_r.at[pl.ds(0, 32)]
        pltpu.make_async_copy(span, span, rim_recv.at[0]).wait()

    @pl.when(det < NDET - 1)
    def _():
        span = spec_r.at[pl.ds(0, 32)]
        pltpu.make_async_copy(span, span, rim_recv.at[1]).wait()

    span = spec_r.at[pl.ds(0, (NTM - 1) * 16)]
    pltpu.make_async_copy(span, span, spec_recv).wait()

    for cyc in range(2):
        for j in range(7):
            bw[j, pl.ds(4 + cyc, 36, stride=2), :] = spec_r[pl.ds(2 * j + cyc, 36, stride=16), :]
    noise_root = jnp.sqrt(bw[6])
    for j in range(6):
        noise = jnp.concatenate([edge[0, j], onoise[j], edge[1, j]], axis=0)
        prior = jnp.concatenate([edge[0, 6 + j], oprior[j], edge[1, 6 + j]], axis=0)
        bw[j] = bw[j] + noise_root * noise + root_s[j // 2] * prior

    moments = [jnp.zeros((8, 128), F32) for _ in range(6)]
    for c in range(3):
        precision = pp[c]
        root = root_s[c]
        side = root * (0.45 / SCALE)
        diagonal = (precision + bw[6] - SHIFT) * (1.0 / SCALE)

        def step(v):
            u = root * v
            beside = pltpu.roll(u, 1, 0) + pltpu.roll(u, 79, 0)
            return diagonal * v - side * beside

        for p in range(2):
            j = 2 * c + p
            v0 = bw[j]
            v1 = step(v0)
            v2 = step(v1)
            v3 = step(v2)
            own = [v[8:72] for v in (v0, v1, v2, v3)]
            v1_s[j] = own[1]
            v2_s[j] = own[2]
            for m, (a, b) in enumerate(((0, 0), (0, 1), (1, 1), (1, 2), (2, 2), (2, 3))):
                moments[m] = moments[m] + jnp.sum((own[a] * own[b]).reshape(8, 8, 128), axis=0)
    message = jnp.zeros((1, 128), F32)
    for m in range(6):
        value = jnp.sum(jnp.sum(moments[m], axis=0, keepdims=True), axis=1, keepdims=True)
        message = jnp.where(lane == m, jnp.broadcast_to(value, (1, 128)), message)
    own_row = mom_r.at[me]
    own_row[...] = message
    to_all(
        lambda to: pltpu.make_async_remote_copy(
            own_row, own_row, mom_send, mom_recv, device_id=to, device_id_type=MESH
        ).start()
    )
    rest = mom_r.at[pl.ds(0, NDEV - 1)]
    pltpu.make_async_copy(rest, rest, mom_recv).wait()
    sums = jnp.sum(mom_r[...], axis=0)
    nu = [jnp.sum(jnp.where(lane == m, sums, 0.0), axis=1, keepdims=True) for m in range(6)]

    zero = jnp.zeros((1, 1), F32)

    def inner(a, b):
        terms = {}
        for i, x_i in enumerate(a):
            for j, y_j in enumerate(b):
                terms[i + j] = terms.get(i + j, zero) + x_i * y_j
        out = zero
        for power, value in terms.items():
            out = out + value * nu[power]
        return out

    def image_of(a):
        longer = list(a) + [zero]
        return [SHIFT * longer[i] + (SCALE * longer[i - 1] if i else zero) for i in range(len(longer))]

    resid = [zero + 1.0]
    direction = [zero + 1.0]
    answer = [zero, zero, zero]
    norm_now = nu[0]
    for iteration in range(3):
        image = image_of(direction)
        alpha = norm_now / inner(direction, image)
        alpha = jnp.minimum(jnp.maximum(alpha, 0.0), STEP_MAX)
        for i, value in enumerate(direction):
            answer[i] = answer[i] + alpha * value
        if iteration < 2:
            resid = resid + [zero]
            resid = [r - alpha * w for r, w in zip(resid, image)]
            norm_next = jnp.maximum(inner(resid, resid), 0.0)
            beta = norm_next / norm_now
            direction = [r + beta * d for r, d in zip(resid, direction + [zero])]
            norm_now = norm_next
    for j in range(6):
        sol_s[j] = answer[0] * bw[j, 8:72, :] + answer[1] * v1_s[j] + answer[2] * v2_s[j]

    stores[2].start()

    span = sbuf.at[pl.ds(0, (NDEV - 1) * 8)]
    pltpu.make_async_copy(span, span, send_sem).wait()
    rest = stat_r.at[pl.ds(0, NDEV - 1)]
    pltpu.make_async_copy(rest, rest, stat_send).wait()
    span = spec_s.at[pl.ds(0, (NTM - 1) * 16)]
    pltpu.make_async_copy(span, span, spec_send).wait()
    rest = mom_r.at[pl.ds(0, NDEV - 1)]
    pltpu.make_async_copy(rest, rest, mom_send).wait()

    @pl.when(jnp.logical_or(low_end, high_end))
    def _():
        span = spec_s.at[pl.ds(0, NTM * 16)]
        pltpu.make_async_copy(span, span, rim_send).wait()

    @pl.when(det < NDET - 1)
    def _():
        for copy in go_down:
            copy.wait_send()

    @pl.when(det > 0)
    def _():
        for copy in go_up:
            copy.wait_send()
    for store in stores:
        store.wait()


def per_device(
    samples, pointing, angles, counts, sky_map, prior_precision, omega_noise, omega_prior
):
    sky = sky_map.reshape(3, 2, 64, 128).transpose(0, 2, 1, 3).reshape(3, 128, 128)
    vmem = pl.BlockSpec(memory_space=pltpu.VMEM)
    dma = pltpu.SemaphoreType.DMA
    anywhere = pl.BlockSpec(memory_space=pl.ANY)
    gain, upper, lower, solved = pl.pallas_call(
        kernel,
        name="gibbs_step",
        out_shape=(
            jax.ShapeDtypeStruct((1, 1), F32),
            jax.ShapeDtypeStruct((3, 128, 128), F32),
            jax.ShapeDtypeStruct((3, 128, 128), F32),
            jax.ShapeDtypeStruct((6, 64, 128), F32),
        ),
        in_specs=[anywhere] * 11,
        out_specs=(vmem, anywhere, anywhere, anywhere),
        scratch_shapes=[
            pltpu.VMEM((128, 256), F32),
            pltpu.VMEM((128, 256), jnp.int32),
            pltpu.VMEM((128, 256), F32),
            pltpu.VMEM((1, 128), jnp.int32),
            pltpu.VMEM((3, 128, 128), F32),
            pltpu.VMEM((6, 64, 128), F32),
            pltpu.VMEM((6, 64, 128), F32),
            pltpu.VMEM((2, 128, 256), BF16),
            pltpu.VMEM((2, 64, 128), F32),
            pltpu.VMEM((2, 64, 128), BF16),
            pltpu.VMEM((2, 3, 128, 128), F32),
            pltpu.VMEM((6, 64, 128), F32),
            pltpu.VMEM((1024, 128), F32),
            pltpu.VMEM((1024, 128), F32),
            pltpu.VMEM((384, 256), BF16),
            pltpu.VMEM((2, 128, 128), F32),
            pltpu.VMEM((2, 128, 128), F32),
            pltpu.VMEM((2, 128, 128), F32),
            pltpu.VMEM((2, 128, 128), F32),
            pltpu.VMEM((3, 2, 128, 128), F32),
            pltpu.VMEM((2, 128, 128), F32),
            pltpu.VMEM((6, 2, 128, 128), F32),
            pltpu.VMEM((384, 256), F32),
            pltpu.VMEM((NDEV, 2, 128), F32),
            pltpu.VMEM((NTM * 16, 128), F32),
            pltpu.VMEM(((NTM + 4) * 16, 128), F32),
            pltpu.VMEM((3, 80, 128), F32),
            pltpu.VMEM((3, 80, 128), F32),
            pltpu.VMEM((2, 12, 8, 128), F32),
            pltpu.VMEM((7, 80, 128), F32),
            pltpu.VMEM((6, 64, 128), F32),
            pltpu.VMEM((6, 64, 128), F32),
            pltpu.VMEM((NDEV, 1, 128), F32),
            dma, dma((NGROUP,)), dma, dma, dma, dma,
            dma, dma((2,)), dma((2, 3)), dma((2, 3)), dma, dma,
            dma((11,)), dma((3,)),
        ],
        compiler_params=pltpu.CompilerParams(collective_id=0, has_side_effects=True),
    )(
        samples.reshape(128, 256),
        pointing.reshape(128, 256),
        angles.reshape(128, 256),
        counts.reshape(1, 128),
        sky,
        prior_precision,
        omega_noise,
        omega_prior,
        *(jnp.asarray(t) for t in tables()),
    )
    binned = (upper + lower).reshape(3, 64, 2, 128).transpose(0, 2, 1, 3).reshape(3, 2, 8192)
    return (gain, binned, solved)


def solution(mesh):
    return jax.shard_map(
        per_device,
        mesh=mesh,
        in_specs=(
            P("det", "tm", None, None),
            P("det", "tm", None, None),
            P("det", "tm", None, None),
            P("det", "tm", None),
            P(None, ("det", "tm"), None),
            P(None, "det", "tm"),
            P(None, "det", "tm"),
            P(None, "det", "tm"),
        ),
        out_specs=(P("det", "tm"), P(None, ("det", "tm"), None), P(None, "det", "tm")),
        check_vma=False,
    )
```

```python
import math

import jax
import jax.numpy as jnp
import numpy as np
from jax import lax
from jax.experimental import pallas as pl
from jax.experimental.pallas import tpu as pltpu
from jax.sharding import PartitionSpec as P

MESH = pl.DeviceIdType.MESH
F32 = jnp.float32
BF16 = jnp.bfloat16
NDET = 4
NTM = 32
NDEV = NDET * NTM
GROUP = 16
NGROUP = NDEV // GROUP
UNROLL = 32
SHIFT = 4.0
SCALE = 4.0
STEP_MAX = 20.0


def near_first():
    ring = (0, 1, 2, 1)
    return sorted(
        ((x, y, z, c) for x in range(4) for y in range(4) for z in range(4) for c in range(2)),
        key=lambda o: 4 * (ring[o[0]] + ring[o[1]] + ring[o[2]]) + o[3],
    )


NEAR = near_first()


def tables():
    h, i = np.divmod(np.arange(128), 64)
    a = 2 * i + h
    k = np.arange(128)
    ang = 2.0 * np.pi * (np.outer(a, k) % 128) / 128
    first = np.concatenate([np.cos(ang), -np.sin(ang)], axis=1)
    b = np.arange(64)
    ang = 2.0 * np.pi * np.outer(b, k) / 8192
    twist = np.stack([np.cos(ang), np.sin(ang)])
    q = np.arange(32)
    ang = 2.0 * np.pi * (np.outer(q, b) % 64) / 64
    c, s = np.cos(ang), np.sin(ang)
    last = np.concatenate([np.concatenate([c, s], axis=1), np.concatenate([-s, c], axis=1)], axis=0)
    last = last / math.sqrt(8192)
    def split(x):
        upper = x.astype(np.float32).astype(jnp.bfloat16)
        return np.stack([upper, (x - upper.astype(np.float64)).astype(jnp.bfloat16)])

    codes = np.asarray([o[0] + 4 * o[1] + 16 * o[2] + 64 * o[3] for o in NEAR], np.int32)
    codes = np.ascontiguousarray(np.broadcast_to(codes[:, None], (NDEV, 128)))
    return [split(first), twist.astype(np.float32), split(last), codes]


def split_parts(x):
    upper = x.astype(BF16)
    return upper, (x - upper.astype(F32)).astype(BF16)


def dot3(a, b):
    out = jnp.dot(a[0], b[0], preferred_element_type=F32)
    out = out + jnp.dot(a[0], b[1], preferred_element_type=F32)
    return out + jnp.dot(a[1], b[0], preferred_element_type=F32)


def sine_cosine(x):
    k = jnp.floor(x * (2.0 / math.pi) + 0.5)
    r = ((x - k * 1.5703125) - k * 4.837512969970703125e-4) - k * 7.549789948768648e-8
    z = r * r
    sine = r + r * z * (-1.6666654611e-1 + z * (8.3321608736e-3 - z * 1.9515295891e-4))
    cosine = 1.0 - 0.5 * z + z * z * (
        4.166664568298827e-2 + z * (-1.388731625493765e-3 + z * 2.443315711809948e-5)
    )
    q = k.astype(jnp.int32) & 3
    odd = (q & 1) == 1
    s = jnp.where(odd, cosine, sine)
    c = jnp.where(odd, sine, cosine)
    s = jnp.where(q >= 2, -s, s)
    c = jnp.where((q == 1) | (q == 2), -c, c)
    return s, c


def one_hot(row, rows):
    value = jnp.broadcast_to(row, (16, 128)).astype(BF16)
    index = lax.broadcasted_iota(jnp.int32, (rows, 128), 0).astype(F32).astype(BF16)
    same = index.reshape(rows // 16, 16, 128) == value[None]
    return jnp.where(same, jnp.ones((), BF16), jnp.zeros((), BF16)).reshape(rows, 128)


def kernel(
    samples_in, pointing_in, angles_in, counts_in, sky_in, prec, onoise_in, oprior_in,
    first_in, twist_in, last_in, codes_in,
    small_out, map_out, basis_out,
    samples, pointing, angles, counts, sky, onoise, oprior, first, twist, last, codes, map_s, match_s,
    sbuf, rbuf, table, hi_s, lo_s, cos_s, sin_s, look, sums_s, wsplit, acc,
    stat_r, spec_s, spec_r, pp, root_s, edge, bw, v1_s, v2_s, mom_r,
    send_sem, recv_sem, stat_send, stat_recv, spec_send, spec_recv,
    rim_send, rim_recv, edge_send, edge_recv, mom_send, mom_recv, in_sem, out_sem,
):
    det = lax.axis_index("det")
    tm = lax.axis_index("tm")
    me = det * NTM + tm

    loads = [
        pltpu.make_async_copy(src, dst, in_sem.at[i])
        for i, (src, dst) in enumerate((
            (samples_in, samples), (pointing_in, pointing), (angles_in, angles), (counts_in, counts),
            (sky_in, sky), (prec, pp.at[:, 8:72, :]), (first_in, first), (twist_in, twist),
            (last_in, last), (onoise_in, onoise), (oprior_in, oprior), (codes_in, codes),
        ))
    ]
    for load in loads:
        load.start()

    ty, tz, tc = tm // 8, (tm // 2) % 4, tm % 2
    at_z = [(tz + o) % 4 * 2 for o in range(4)]
    at_c = [tc, 1 - tc]
    at_y = [(ty + o) % 4 * 8 for o in range(4)]
    at_det = [(det + o) % NDET for o in range(NDET)]

    def to_tm(act):
        def row(y, own):
            for z in (2, 1, 3, 0):
                for c in (1, 0):
                    if not (own and z == 0 and c == 0):
                        act(y * 8 + at_z[z] + at_c[c])

        @pl.loop(0, 3)
        def _(d):
            row((ty + jnp.where(d == 0, 2, jnp.where(d == 1, 1, 3))) % 4, False)

        row(ty, True)

    def to_all(act):
        to_tm(lambda to: [act((at_det[x], to)) for x in (2, 1, 3, 0)])
        for x in (2, 1, 3):
            act((at_det[x], tm))

    barrier = pltpu.get_barrier_semaphore()
    to_all(lambda to: pl.semaphore_signal(barrier, inc=1, device_id=to, device_id_type=MESH))

    for load in loads[:4]:
        load.wait()

    row_i = lax.broadcasted_iota(jnp.int32, (128, 128), 0)
    col_i = lax.broadcasted_iota(jnp.int32, (128, 128), 1)
    for half in range(2):
        lanes = slice(half * 128, half * 128 + 128)
        sbuf[pl.ds(half, 128, stride=8), :] = samples[:, lanes]
        sbuf[pl.ds(2 + half, 128, stride=8), :] = angles[:, lanes]
        sbuf[pl.ds(4 + half, 128, stride=8), :] = pointing[:, lanes].astype(F32)
    count_row = jnp.broadcast_to(counts[...].astype(F32), (128, 128))
    count_col = jnp.sum(jnp.where(row_i == col_i, count_row, 0.0), axis=1, keepdims=True)
    count_full = jnp.broadcast_to(count_col, (128, 128))
    sbuf[pl.ds(6, 128, stride=8), :] = count_full
    sbuf[pl.ds(7, 128, stride=8), :] = count_full

    loads[4].wait()

    for c in range(3):
        blocks = []
        for cyc in range(2):
            turned = sky[c, pl.ds(cyc, 64, stride=2), :].T
            blocks.append(jnp.concatenate([turned[:64], turned[64:]], axis=1))
        full = jnp.concatenate(blocks, axis=1)
        upper = full.astype(BF16)
        table[pl.ds(c * 64, 64), :] = upper
        table[pl.ds(192 + c * 64, 64), :] = (full - upper.astype(F32)).astype(BF16)

    bw[:, 0:8, :] = jnp.zeros((7, 8, 128), F32)
    bw[:, 72:80, :] = jnp.zeros((7, 8, 128), F32)

    @pl.when(det == 0)
    def _():
        pp[:, 0:8, :] = jnp.zeros((3, 8, 128), F32)
        edge[0] = jnp.zeros((12, 8, 128), F32)
        spec_r[0:24, :] = jnp.zeros((24, 128), F32)

    @pl.when(det == NDET - 1)
    def _():
        pp[:, 72:80, :] = jnp.zeros((3, 8, 128), F32)
        edge[1] = jnp.zeros((12, 8, 128), F32)
        spec_r[67 * 8 : 70 * 8, :] = jnp.zeros((24, 128), F32)

    loads[11].wait()
    code = codes[...]
    source = ((code & 3) + det) % 4 * 32 + (((code >> 2) & 3) + ty) % 4 * 8
    source = source + (((code >> 4) & 3) + tz) % 4 * 2 + ((code >> 6) + tc) % 2
    match_s[...] = jnp.where(source == col_i, 1.0, 0.0)
    acc[...] = jnp.zeros_like(acc)
    pl.semaphore_wait(barrier, NDEV - 1)

    for s, (x, y, z, c) in enumerate(NEAR):
        if s == 0:
            continue
        where = at_det[-x % 4]
        to = at_y[-y % 4] + at_z[-z % 4] + at_c[c]
        pltpu.make_async_remote_copy(
            sbuf.at[pl.ds((where * NTM + to) * 8, 8)], rbuf.at[s * 8 : s * 8 + 8],
            send_sem, recv_sem.at[s // GROUP], device_id=(where, to), device_id_type=MESH,
        ).start()
    rbuf[0:8, :] = sbuf[pl.ds(me * 8, 8), :]

    down = ((det + 1) % NDET, tm)
    up = ((det + NDET - 1) % NDET, tm)

    def edge_copies(rows, side, padded, to):
        pairs = (
            (prec.at[:, rows, :], pp.at[:, padded, :]),
            (onoise_in.at[:, rows, :], edge.at[side, 0:6]),
            (oprior_in.at[:, rows, :], edge.at[side, 6:12]),
        )
        return [
            pltpu.make_async_remote_copy(
                src, dst, edge_send.at[side, i], edge_recv.at[side, i], device_id=to, device_id_type=MESH
            )
            for i, (src, dst) in enumerate(pairs)
        ]

    go_down = edge_copies(slice(56, 64), 0, slice(0, 8), down)
    go_up = edge_copies(slice(0, 8), 1, slice(72, 80), up)

    @pl.when(det < NDET - 1)
    def _():
        for copy in go_down:
            copy.start()

    @pl.when(det > 0)
    def _():
        for copy in go_up:
            copy.start()

    col_index = lax.broadcasted_iota(jnp.int32, (64, 128), 0).astype(F32)

    slot_index = lax.broadcasted_iota(jnp.int32, (GROUP, 128), 1).astype(F32)

    def gather_group(group):
        base = group * GROUP
        here = pl.ds(base, GROUP)

        def row(r):
            return rbuf[pl.ds(base * 8 + r, GROUP, stride=8), :]

        for half in range(2):
            pixel = row(4 + half).astype(jnp.int32)
            upper = (pixel >> 13) * 128 + ((pixel >> 6) & 1) * 64 + ((pixel >> 7) & 63)
            hi_s[half, here, :] = upper.astype(F32)
            lo_s[half, here, :] = (pixel & 63).astype(F32)
        for u in range(GROUP):
            s = base + u
            hots = [one_hot(hi_s[half, pl.ds(s, 1), :], 256) for half in range(2)]
            got = jnp.dot(table[...], jnp.concatenate(hots, axis=1), preferred_element_type=F32)
            got = got[:192] + got[192:]
            for half in range(2):
                low = lo_s[half, pl.ds(s, 1), :]
                same = col_index == low
                for c in range(3):
                    part = got[c * 64 : c * 64 + 64, half * 128 : half * 128 + 128]
                    look[c, half, pl.ds(s, 1), :] = jnp.sum(
                        jnp.where(same, part, 0.0), axis=0, keepdims=True
                    )
        count = row(6)
        cross = jnp.zeros((GROUP, 128), F32)
        square = jnp.zeros((GROUP, 128), F32)
        for half in range(2):
            sine, cosine = sine_cosine(2.0 * row(2 + half))
            sin_s[half, here, :] = sine
            cos_s[half, here, :] = cosine
            signal = look[0, half, here, :] + look[1, half, here, :] * cosine + look[2, half, here, :] * sine
            look[0, half, here, :] = signal
            masked = jnp.where(slot_index + 128.0 * half < count, signal, 0.0)
            cross = cross + masked * row(half)
            square = square + masked * signal
        sums_s[0, here, :] = cross
        sums_s[1, here, :] = square

    @pl.loop(0, NGROUP)
    def _(group):
        @pl.when(group == 0)
        def _():
            span = rbuf.at[pl.ds(0, (GROUP - 1) * 8)]
            pltpu.make_async_copy(span, span, recv_sem.at[0]).wait()

        @pl.when(group > 0)
        def _():
            span = rbuf.at[pl.ds(0, GROUP * 8)]
            pltpu.make_async_copy(span, span, recv_sem.at[group]).wait()

        gather_group(group)

    match = match_s[...] > 0.5
    cross, square = (
        jnp.sum(
            jnp.where(match, jnp.sum(sums_s[k], axis=1, keepdims=True), 0.0), axis=0, keepdims=True
        )
        for k in range(2)
    )
    mine = stat_r.at[me]
    mine[...] = jnp.concatenate([cross, square], axis=0)
    to_all(
        lambda to: pltpu.make_async_remote_copy(
            mine, mine, stat_send, stat_recv, device_id=to, device_id_type=MESH
        ).start()
    )
    count = rbuf[pl.ds(6, 128, stride=8), :]
    slot = col_i.astype(F32)
    rest = stat_r.at[pl.ds(0, NDEV - 1)]
    pltpu.make_async_copy(rest, rest, stat_recv).wait()
    total = jnp.sum(stat_r[...], axis=0)
    gains = total[0:1] / (total[1:2] + 1e-06)
    lane = lax.broadcasted_iota(jnp.int32, (1, 128), 1)
    own_gain = jnp.sum(jnp.where(lane == me, gains, 0.0), axis=1, keepdims=True)
    gain_col = jnp.sum(jnp.where(match, gains, 0.0), axis=1, keepdims=True)
    gain_full = jnp.broadcast_to(gain_col, (128, 128))

    hits = [jnp.zeros((1, 128), F32) for _ in range(2)]
    for half in range(2):
        data = rbuf[pl.ds(half, 128, stride=8), :]
        good = slot + 128.0 * half < count
        residual = jnp.where(good, data - gain_full * look[0, half], 0.0)
        for c, weight in enumerate((residual, residual * cos_s[half], residual * sin_s[half])):
            upper = weight.astype(BF16).astype(F32)
            wsplit[c, half] = upper
            wsplit[3 + c, half] = weight - upper
        late = jnp.where(hi_s[half] >= 128.0, 1.0, 0.0)
        valid = jnp.where(good, 1.0, 0.0)
        hits[1] = hits[1] + jnp.sum(valid * late, axis=0, keepdims=True)
        hits[0] = hits[0] + jnp.sum(valid * (1.0 - late), axis=0, keepdims=True)

    low_index = lax.broadcasted_iota(jnp.int32, (64, 128), 0).astype(F32).astype(BF16).reshape(4, 16, 128)

    @pl.loop(0, NDEV // UNROLL)
    def _(step):
        lefts = []
        rights = []
        for u in range(UNROLL):
            s = step * UNROLL + u
            for half in range(2):
                rights.append(one_hot(hi_s[half, pl.ds(s, 1), :], 256))
                low = jnp.broadcast_to(lo_s[half, pl.ds(s, 1), :], (16, 128)).astype(BF16)
                same = low_index == low[None]
                rows = []
                for w in range(6):
                    value = jnp.broadcast_to(wsplit[w, half, pl.ds(s, 1), :], (16, 128)).astype(BF16)
                    rows.append(jnp.where(same, value[None], jnp.zeros((), BF16)).reshape(64, 128))
                lefts.append(jnp.concatenate(rows, axis=0))
        acc[...] += lax.dot_general(
            jnp.concatenate(lefts, axis=1), jnp.concatenate(rights, axis=1),
            (((1,), (1,)), ((), ())), preferred_element_type=F32,
        )

    field = acc[:192] + acc[192:]

    for load in loads[6:9]:
        load.wait()
    z_parts = []
    for cyc in range(2):
        y = dot3(split_parts(field[:, cyc * 128 : cyc * 128 + 128]), (first[0], first[1]))
        for c in range(3):
            y_re = y[c * 64 : c * 64 + 64, :128]
            y_im = y[c * 64 : c * 64 + 64, 128:]
            z_re = y_re * twist[0] + y_im * twist[1]
            z_im = y_im * twist[0] - y_re * twist[1]
            z_parts.append(jnp.concatenate([z_re, z_im], axis=0))
    x = dot3((last[0], last[1]), split_parts(jnp.concatenate(z_parts, axis=1)))
    for cyc in range(2):
        for c in range(3):
            block = x[:, (cyc * 3 + c) * 128 : (cyc * 3 + c) * 128 + 128]
            spec_s[pl.ds(cyc * 8 + 2 * c, 32, stride=16), :] = block[:32]
            spec_s[pl.ds(cyc * 8 + 2 * c + 1, 32, stride=16), :] = block[32:]
        weight = jnp.sum(hits[cyc], axis=1, keepdims=True) * (1.0 / 8192)
        for r in (6, 7):
            spec_s[pl.ds(cyc * 8 + r, 32, stride=16), :] = jnp.broadcast_to(weight, (32, 128))

    def send_spectrum(where, to, skip, tiles, slot, send, recv):
        pltpu.make_async_remote_copy(
            spec_s.at[pl.ds(to * 16 + skip * 8, tiles * 8)], spec_r.at[pl.ds(slot * 8, tiles * 8)],
            send, recv, device_id=(where, to), device_id_type=MESH,
        ).start()

    def send_rim(where, skip, tiles, slot, recv):
        send = lambda to: send_spectrum(where, to, skip, tiles, slot, rim_send, recv)
        to_tm(send)
        send(tm)

    rims = []
    for at, bound, step, skip, tiles, slot, side in (
        (0, det > 0, -1, 0, 2, 67, 1),
        (1, det > 0, -1, 0, 1, 69, 1),
        (NTM - 2, det < NDET - 1, 1, 1, 1, 0, 0),
        (NTM - 1, det < NDET - 1, 1, 0, 2, 1, 0),
    ):
        here = jnp.logical_and(tm == at, bound)
        rims.append((here, tiles))

        @pl.when(here)
        def _():
            send_rim(det + step, skip, tiles, slot, rim_recv.at[side])

    to_tm(lambda to: send_spectrum(det, to, 0, 2, 3 + 2 * tm, spec_send, spec_recv))
    spec_r[pl.ds((3 + 2 * tm) * 8, 16), :] = spec_s[pl.ds(tm * 16, 16), :]
    for c in range(3):
        for cyc in range(2):
            block = field[c * 64 : c * 64 + 64, cyc * 128 : cyc * 128 + 128]
            block = jnp.concatenate([block[:, :64], block[:, 64:]], axis=0)
            map_s[c, pl.ds(cyc, 64, stride=2), :] = block.T
    stores = [
        pltpu.make_async_copy(map_s, map_out, out_sem.at[0]),
        pltpu.make_async_copy(bw.at[0:6, 8:72, :], basis_out.at[0], out_sem.at[1]),
        pltpu.make_async_copy(v1_s, basis_out.at[1], out_sem.at[2]),
        pltpu.make_async_copy(v2_s, basis_out.at[2], out_sem.at[3]),
    ]
    stores[0].start()
    loads[5].wait()
    loads[9].wait()
    loads[10].wait()

    @pl.when(det > 0)
    def _():
        for copy in go_down:
            copy.wait_recv()

    @pl.when(det < NDET - 1)
    def _():
        for copy in go_up:
            copy.wait_recv()

    for c in range(3):
        root_s[c] = jnp.sqrt(pp[c])

    @pl.when(det > 0)
    def _():
        span = spec_r.at[pl.ds(0, 24)]
        pltpu.make_async_copy(span, span, rim_recv.at[0]).wait()

    @pl.when(det < NDET - 1)
    def _():
        span = spec_r.at[pl.ds(0, 24)]
        pltpu.make_async_copy(span, span, rim_recv.at[1]).wait()

    span = spec_r.at[pl.ds(0, (NTM - 1) * 16)]
    pltpu.make_async_copy(span, span, spec_recv).wait()

    for j in range(7):
        bw[j, 5:75, :] = spec_r[pl.ds(j, 70, stride=8), :]
    noise_root = jnp.sqrt(bw[6])
    for j in range(6):
        noise = jnp.concatenate([edge[0, j], onoise[j], edge[1, j]], axis=0)
        prior = jnp.concatenate([edge[0, 6 + j], oprior[j], edge[1, 6 + j]], axis=0)
        bw[j] = bw[j] + noise_root * noise + root_s[j // 2] * prior

    moments = [jnp.zeros((8, 128), F32) for _ in range(6)]
    for c in range(3):
        precision = pp[c]
        root = root_s[c]
        side = root * (0.45 / SCALE)
        diagonal = (precision + bw[6] - SHIFT) * (1.0 / SCALE)

        def step(v):
            u = root * v
            beside = pltpu.roll(u, 1, 0) + pltpu.roll(u, 79, 0)
            return diagonal * v - side * beside

        for p in range(2):
            j = 2 * c + p
            v0 = bw[j]
            v1 = step(v0)
            v2 = step(v1)
            v3 = step(v2)
            own = [v[8:72] for v in (v0, v1, v2, v3)]
            v1_s[j] = own[1]
            v2_s[j] = own[2]
            for m, (a, b) in enumerate(((0, 0), (0, 1), (1, 1), (1, 2), (2, 2), (2, 3))):
                moments[m] = moments[m] + jnp.sum((own[a] * own[b]).reshape(8, 8, 128), axis=0)
    message = jnp.zeros((1, 128), F32)
    for m in range(6):
        value = jnp.sum(jnp.sum(moments[m], axis=0, keepdims=True), axis=1, keepdims=True)
        message = jnp.where(lane == m, jnp.broadcast_to(value, (1, 128)), message)
    own_row = mom_r.at[me]
    own_row[...] = message
    to_all(
        lambda to: pltpu.make_async_remote_copy(
            own_row, own_row, mom_send, mom_recv, device_id=to, device_id_type=MESH
        ).start()
    )
    for store in stores[1:]:
        store.start()
    rest = mom_r.at[pl.ds(0, NDEV - 1)]
    pltpu.make_async_copy(rest, rest, mom_recv).wait()
    sums = jnp.sum(mom_r[...], axis=0)
    nu = [jnp.sum(jnp.where(lane == m, sums, 0.0), axis=1, keepdims=True) for m in range(6)]

    zero = jnp.zeros((1, 1), F32)

    def inner(a, b):
        terms = {}
        for i, x_i in enumerate(a):
            for j, y_j in enumerate(b):
                terms[i + j] = terms.get(i + j, zero) + x_i * y_j
        out = zero
        for power, value in terms.items():
            out = out + value * nu[power]
        return out

    def image_of(a):
        longer = list(a) + [zero]
        return [SHIFT * longer[i] + (SCALE * longer[i - 1] if i else zero) for i in range(len(longer))]

    resid = [zero + 1.0]
    direction = [zero + 1.0]
    answer = [zero, zero, zero]
    norm_now = nu[0]
    for iteration in range(3):
        image = image_of(direction)
        alpha = norm_now / inner(direction, image)
        alpha = jnp.minimum(jnp.maximum(alpha, 0.0), STEP_MAX)
        for i, value in enumerate(direction):
            answer[i] = answer[i] + alpha * value
        if iteration < 2:
            resid = resid + [zero]
            resid = [r - alpha * w for r, w in zip(resid, image)]
            norm_next = jnp.maximum(inner(resid, resid), 0.0)
            beta = norm_next / norm_now
            direction = [r + beta * d for r, d in zip(resid, direction + [zero])]
            norm_now = norm_next
    for i, value in enumerate(answer + [own_gain]):
        small_out[i : i + 1, :] = jnp.broadcast_to(value, (1, 128))

    span = sbuf.at[pl.ds(0, (NDEV - 1) * 8)]
    pltpu.make_async_copy(span, span, send_sem).wait()
    rest = stat_r.at[pl.ds(0, NDEV - 1)]
    pltpu.make_async_copy(rest, rest, stat_send).wait()
    span = spec_s.at[pl.ds(0, (NTM - 1) * 16)]
    pltpu.make_async_copy(span, span, spec_send).wait()
    rest = mom_r.at[pl.ds(0, NDEV - 1)]
    pltpu.make_async_copy(rest, rest, mom_send).wait()

    for here, tiles in rims:
        @pl.when(here)
        def _():
            span = spec_s.at[pl.ds(0, NTM * tiles * 8)]
            pltpu.make_async_copy(span, span, rim_send).wait()

    @pl.when(det < NDET - 1)
    def _():
        for copy in go_down:
            copy.wait_send()

    @pl.when(det > 0)
    def _():
        for copy in go_up:
            copy.wait_send()
    for store in stores:
        store.wait()


def finish(small, map_in, basis_in, gain_out, map_out, sol_out, map_s, basis, sol_s, in_sem, out_sem):
    loads = [pltpu.make_async_copy(basis_in.at[i], basis.at[i], in_sem.at[i]) for i in range(3)]
    loads.append(pltpu.make_async_copy(map_in, map_s, in_sem.at[3]))
    for load in loads:
        load.start()
    gain_out[...] = small[3:4, 0:1]
    for load in loads[:3]:
        load.wait()
    parts = [jnp.broadcast_to(small[i : i + 1, :], (64, 128)) for i in range(3)]
    for j in range(6):
        sol_s[j] = parts[0] * basis[0, j] + parts[1] * basis[1, j] + parts[2] * basis[2, j]
    stores = [
        pltpu.make_async_copy(sol_s, sol_out, out_sem.at[0]),
        pltpu.make_async_copy(map_s, map_out, out_sem.at[1]),
    ]
    stores[0].start()
    loads[3].wait()
    stores[1].start()
    for store in stores:
        store.wait()


def per_device(
    samples, pointing, angles, counts, sky_map, prior_precision, omega_noise, omega_prior
):
    sky = sky_map.reshape(3, 2, 64, 128).transpose(0, 2, 1, 3).reshape(3, 128, 128)
    vmem = pl.BlockSpec(memory_space=pltpu.VMEM)
    dma = pltpu.SemaphoreType.DMA
    anywhere = pl.BlockSpec(memory_space=pl.ANY)
    small, binned, basis = pl.pallas_call(
        kernel,
        name="gibbs_step",
        out_shape=(
            jax.ShapeDtypeStruct((8, 128), F32),
            jax.ShapeDtypeStruct((3, 128, 128), F32),
            jax.ShapeDtypeStruct((3, 6, 64, 128), F32),
        ),
        in_specs=[anywhere] * 12,
        out_specs=(vmem, anywhere, anywhere),
        scratch_shapes=[
            pltpu.VMEM((128, 256), F32),
            pltpu.VMEM((128, 256), jnp.int32),
            pltpu.VMEM((128, 256), F32),
            pltpu.VMEM((1, 128), jnp.int32),
            pltpu.VMEM((3, 128, 128), F32),
            pltpu.VMEM((6, 64, 128), F32),
            pltpu.VMEM((6, 64, 128), F32),
            pltpu.VMEM((2, 128, 256), BF16),
            pltpu.VMEM((2, 64, 128), F32),
            pltpu.VMEM((2, 64, 128), BF16),
            pltpu.VMEM((NDEV, 128), jnp.int32),
            pltpu.VMEM((3, 128, 128), F32),
            pltpu.VMEM((NDEV, 128), F32),
            pltpu.VMEM((1024, 128), F32),
            pltpu.VMEM((1024, 128), F32),
            pltpu.VMEM((384, 256), BF16),
            pltpu.VMEM((2, 128, 128), F32),
            pltpu.VMEM((2, 128, 128), F32),
            pltpu.VMEM((2, 128, 128), F32),
            pltpu.VMEM((2, 128, 128), F32),
            pltpu.VMEM((3, 2, 128, 128), F32),
            pltpu.VMEM((2, 128, 128), F32),
            pltpu.VMEM((6, 2, 128, 128), F32),
            pltpu.VMEM((384, 256), F32),
            pltpu.VMEM((NDEV, 2, 128), F32),
            pltpu.VMEM((NTM * 16, 128), F32),
            pltpu.VMEM((70 * 8, 128), F32),
            pltpu.VMEM((3, 80, 128), F32),
            pltpu.VMEM((3, 80, 128), F32),
            pltpu.VMEM((2, 12, 8, 128), F32),
            pltpu.VMEM((7, 80, 128), F32),
            pltpu.VMEM((6, 64, 128), F32),
            pltpu.VMEM((6, 64, 128), F32),
            pltpu.VMEM((NDEV, 1, 128), F32),
            dma, dma((NGROUP,)), dma, dma, dma, dma,
            dma, dma((2,)), dma((2, 3)), dma((2, 3)), dma, dma,
            dma((12,)), dma((4,)),
        ],
        compiler_params=pltpu.CompilerParams(collective_id=0, has_side_effects=True),
    )(
        samples.reshape(128, 256),
        pointing.reshape(128, 256),
        angles.reshape(128, 256),
        counts.reshape(1, 128),
        sky,
        prior_precision,
        omega_noise,
        omega_prior,
        *(jnp.asarray(t) for t in tables()),
    )
    gain, binned, solved = pl.pallas_call(
        finish,
        name="finish",
        out_shape=(
            jax.ShapeDtypeStruct((1, 1), F32),
            jax.ShapeDtypeStruct((3, 128, 128), F32),
            jax.ShapeDtypeStruct((6, 64, 128), F32),
        ),
        in_specs=[vmem, anywhere, anywhere],
        out_specs=(vmem, anywhere, anywhere),
        scratch_shapes=[
            pltpu.VMEM((3, 128, 128), F32),
            pltpu.VMEM((3, 6, 64, 128), F32),
            pltpu.VMEM((6, 64, 128), F32),
            dma((4,)), dma((2,)),
        ],
    )(small, binned, basis)
    binned = binned.reshape(3, 64, 2, 128).transpose(0, 2, 1, 3).reshape(3, 2, 8192)
    return (gain, binned, solved)


def solution(mesh):
    return jax.shard_map(
        per_device,
        mesh=mesh,
        in_specs=(
            P("det", "tm", None, None),
            P("det", "tm", None, None),
            P("det", "tm", None, None),
            P("det", "tm", None),
            P(None, ("det", "tm"), None),
            P(None, "det", "tm"),
            P(None, "det", "tm"),
            P(None, "det", "tm"),
        ),
        out_specs=(P("det", "tm"), P(None, ("det", "tm"), None), P(None, "det", "tm")),
        check_vma=False,
    )
```

```python
import math

import jax
import jax.numpy as jnp
import numpy as np
from jax import lax
from jax.experimental import pallas as pl
from jax.experimental.pallas import tpu as pltpu
from jax.sharding import PartitionSpec as P

MESH = pl.DeviceIdType.MESH
F32 = jnp.float32
BF16 = jnp.bfloat16
NDET = 4
NTM = 32
NDEV = NDET * NTM
GROUP = 16
NGROUP = NDEV // GROUP
UNROLL = 32
SHIFT = 4.0
SCALE = 4.0
STEP_MAX = 20.0


def near_first():
    ring = (0, 1, 2, 1)
    return sorted(
        ((x, y, z, c) for x in range(4) for y in range(4) for z in range(4) for c in range(2)),
        key=lambda o: 4 * (ring[o[0]] + ring[o[1]] + ring[o[2]]) + o[3],
    )


NEAR = near_first()


def tables():
    h, i = np.divmod(np.arange(128), 64)
    a = 2 * i + h
    k = np.arange(128)
    ang = 2.0 * np.pi * (np.outer(a, k) % 128) / 128
    first = np.concatenate([np.cos(ang), -np.sin(ang)], axis=1)
    b = np.arange(64)
    ang = 2.0 * np.pi * np.outer(b, k) / 8192
    twist = np.stack([np.cos(ang), np.sin(ang)])
    q = np.arange(32)
    ang = 2.0 * np.pi * (np.outer(q, b) % 64) / 64
    c, s = np.cos(ang), np.sin(ang)
    last = np.concatenate([np.concatenate([c, s], axis=1), np.concatenate([-s, c], axis=1)], axis=0)
    last = last / math.sqrt(8192)
    def split(x):
        upper = x.astype(np.float32).astype(jnp.bfloat16)
        return np.stack([upper, (x - upper.astype(np.float64)).astype(jnp.bfloat16)])

    codes = np.asarray([o[0] + 4 * o[1] + 16 * o[2] + 64 * o[3] for o in NEAR], np.int32)
    codes = np.ascontiguousarray(np.broadcast_to(codes[:, None], (NDEV, 128)))
    return [split(first), twist.astype(np.float32), split(last), codes]


def split_parts(x):
    upper = x.astype(BF16)
    return upper, (x - upper.astype(F32)).astype(BF16)


def dot3(a, b):
    out = jnp.dot(a[0], b[0], preferred_element_type=F32)
    out = out + jnp.dot(a[0], b[1], preferred_element_type=F32)
    return out + jnp.dot(a[1], b[0], preferred_element_type=F32)


def sine_cosine(x):
    k = jnp.floor(x * (2.0 / math.pi) + 0.5)
    r = ((x - k * 1.5703125) - k * 4.837512969970703125e-4) - k * 7.549789948768648e-8
    z = r * r
    sine = r + r * z * (-1.6666654611e-1 + z * (8.3321608736e-3 - z * 1.9515295891e-4))
    cosine = 1.0 - 0.5 * z + z * z * (
        4.166664568298827e-2 + z * (-1.388731625493765e-3 + z * 2.443315711809948e-5)
    )
    q = k.astype(jnp.int32) & 3
    odd = (q & 1) == 1
    s = jnp.where(odd, cosine, sine)
    c = jnp.where(odd, sine, cosine)
    s = jnp.where(q >= 2, -s, s)
    c = jnp.where((q == 1) | (q == 2), -c, c)
    return s, c


def one_hot(row, rows):
    value = jnp.broadcast_to(row, (16, 128)).astype(BF16)
    index = lax.broadcasted_iota(jnp.int32, (rows, 128), 0).astype(F32).astype(BF16)
    same = index.reshape(rows // 16, 16, 128) == value[None]
    return jnp.where(same, jnp.ones((), BF16), jnp.zeros((), BF16)).reshape(rows, 128)


def kernel(
    samples_in, pointing_in, angles_in, counts_in, sky_in, prec, onoise_in, oprior_in,
    first_in, twist_in, last_in, codes_in,
    small_out, map_s, sol_out,
    samples, pointing, angles, counts, sky, onoise, oprior, first, twist, last, codes, match_s,
    sbuf, rbuf, table, hi_s, lo_s, cos_s, sin_s, look, sums_s, wsplit, acc,
    stat_r, spec_s, spec_r, pp, root_s, edge, bw, v1_s, v2_s, mom_r,
    send_sem, recv_sem, stat_send, stat_recv, spec_send, spec_recv,
    rim_send, rim_recv, edge_send, edge_recv, mom_send, mom_recv, in_sem,
):
    det = lax.axis_index("det")
    tm = lax.axis_index("tm")
    me = det * NTM + tm

    loads = [
        pltpu.make_async_copy(src, dst, in_sem.at[i])
        for i, (src, dst) in enumerate((
            (samples_in, samples), (pointing_in, pointing), (angles_in, angles), (counts_in, counts),
            (sky_in, sky), (prec, pp.at[:, 8:72, :]), (first_in, first), (twist_in, twist),
            (last_in, last), (onoise_in, onoise), (oprior_in, oprior), (codes_in, codes),
        ))
    ]
    for load in loads:
        load.start()

    ty, tz, tc = tm // 8, (tm // 2) % 4, tm % 2
    at_z = [(tz + o) % 4 * 2 for o in range(4)]
    at_c = [tc, 1 - tc]
    at_y = [(ty + o) % 4 * 8 for o in range(4)]
    at_det = [(det + o) % NDET for o in range(NDET)]

    def to_tm(act):
        def row(y, own):
            for z in (2, 1, 3, 0):
                for c in (1, 0):
                    if not (own and z == 0 and c == 0):
                        act(y * 8 + at_z[z] + at_c[c])

        @pl.loop(0, 3)
        def _(d):
            row((ty + jnp.where(d == 0, 2, jnp.where(d == 1, 1, 3))) % 4, False)

        row(ty, True)

    def to_all(act):
        to_tm(lambda to: [act((at_det[x], to)) for x in (2, 1, 3, 0)])
        for x in (2, 1, 3):
            act((at_det[x], tm))

    barrier = pltpu.get_barrier_semaphore()
    to_all(lambda to: pl.semaphore_signal(barrier, inc=1, device_id=to, device_id_type=MESH))

    for load in loads[:4]:
        load.wait()

    row_i = lax.broadcasted_iota(jnp.int32, (128, 128), 0)
    col_i = lax.broadcasted_iota(jnp.int32, (128, 128), 1)
    for half in range(2):
        lanes = slice(half * 128, half * 128 + 128)
        sbuf[pl.ds(half, 128, stride=8), :] = samples[:, lanes]
        sbuf[pl.ds(2 + half, 128, stride=8), :] = angles[:, lanes]
        sbuf[pl.ds(4 + half, 128, stride=8), :] = pointing[:, lanes].astype(F32)
    count_row = jnp.broadcast_to(counts[...].astype(F32), (128, 128))
    count_col = jnp.sum(jnp.where(row_i == col_i, count_row, 0.0), axis=1, keepdims=True)
    count_full = jnp.broadcast_to(count_col, (128, 128))
    sbuf[pl.ds(6, 128, stride=8), :] = count_full
    sbuf[pl.ds(7, 128, stride=8), :] = count_full

    loads[4].wait()

    for c in range(3):
        blocks = []
        for cyc in range(2):
            turned = sky[c, pl.ds(cyc, 64, stride=2), :].T
            blocks.append(jnp.concatenate([turned[:64], turned[64:]], axis=1))
        full = jnp.concatenate(blocks, axis=1)
        upper = full.astype(BF16)
        table[pl.ds(c * 64, 64), :] = upper
        table[pl.ds(192 + c * 64, 64), :] = (full - upper.astype(F32)).astype(BF16)

    bw[:, 0:8, :] = jnp.zeros((7, 8, 128), F32)
    bw[:, 72:80, :] = jnp.zeros((7, 8, 128), F32)

    @pl.when(det == 0)
    def _():
        pp[:, 0:8, :] = jnp.zeros((3, 8, 128), F32)
        edge[0] = jnp.zeros((12, 8, 128), F32)
        spec_r[0:24, :] = jnp.zeros((24, 128), F32)

    @pl.when(det == NDET - 1)
    def _():
        pp[:, 72:80, :] = jnp.zeros((3, 8, 128), F32)
        edge[1] = jnp.zeros((12, 8, 128), F32)
        spec_r[67 * 8 : 70 * 8, :] = jnp.zeros((24, 128), F32)

    loads[11].wait()
    code = codes[...]
    source = ((code & 3) + det) % 4 * 32 + (((code >> 2) & 3) + ty) % 4 * 8
    source = source + (((code >> 4) & 3) + tz) % 4 * 2 + ((code >> 6) + tc) % 2
    match_s[...] = jnp.where(source == col_i, 1.0, 0.0)
    acc[...] = jnp.zeros_like(acc)
    pl.semaphore_wait(barrier, NDEV - 1)

    for s, (x, y, z, c) in enumerate(NEAR):
        if s == 0:
            continue
        where = at_det[-x % 4]
        to = at_y[-y % 4] + at_z[-z % 4] + at_c[c]
        pltpu.make_async_remote_copy(
            sbuf.at[pl.ds((where * NTM + to) * 8, 8)], rbuf.at[s * 8 : s * 8 + 8],
            send_sem, recv_sem.at[s // GROUP], device_id=(where, to), device_id_type=MESH,
        ).start()
    rbuf[0:8, :] = sbuf[pl.ds(me * 8, 8), :]

    down = ((det + 1) % NDET, tm)
    up = ((det + NDET - 1) % NDET, tm)

    def edge_copies(rows, side, padded, to):
        pairs = (
            (prec.at[:, rows, :], pp.at[:, padded, :]),
            (onoise_in.at[:, rows, :], edge.at[side, 0:6]),
            (oprior_in.at[:, rows, :], edge.at[side, 6:12]),
        )
        return [
            pltpu.make_async_remote_copy(
                src, dst, edge_send.at[side, i], edge_recv.at[side, i], device_id=to, device_id_type=MESH
            )
            for i, (src, dst) in enumerate(pairs)
        ]

    go_down = edge_copies(slice(56, 64), 0, slice(0, 8), down)
    go_up = edge_copies(slice(0, 8), 1, slice(72, 80), up)

    @pl.when(det < NDET - 1)
    def _():
        for copy in go_down:
            copy.start()

    @pl.when(det > 0)
    def _():
        for copy in go_up:
            copy.start()

    col_index = lax.broadcasted_iota(jnp.int32, (64, 128), 0).astype(F32)

    slot_index = lax.broadcasted_iota(jnp.int32, (GROUP, 128), 1).astype(F32)

    def gather_group(group):
        base = group * GROUP
        here = pl.ds(base, GROUP)

        def row(r):
            return rbuf[pl.ds(base * 8 + r, GROUP, stride=8), :]

        for half in range(2):
            pixel = row(4 + half).astype(jnp.int32)
            upper = (pixel >> 13) * 128 + ((pixel >> 6) & 1) * 64 + ((pixel >> 7) & 63)
            hi_s[half, here, :] = upper.astype(F32)
            lo_s[half, here, :] = (pixel & 63).astype(F32)
        for u in range(GROUP):
            s = base + u
            hots = [one_hot(hi_s[half, pl.ds(s, 1), :], 256) for half in range(2)]
            got = jnp.dot(table[...], jnp.concatenate(hots, axis=1), preferred_element_type=F32)
            got = got[:192] + got[192:]
            for half in range(2):
                low = lo_s[half, pl.ds(s, 1), :]
                same = col_index == low
                for c in range(3):
                    part = got[c * 64 : c * 64 + 64, half * 128 : half * 128 + 128]
                    look[c, half, pl.ds(s, 1), :] = jnp.sum(
                        jnp.where(same, part, 0.0), axis=0, keepdims=True
                    )
        count = row(6)
        cross = jnp.zeros((GROUP, 128), F32)
        square = jnp.zeros((GROUP, 128), F32)
        for half in range(2):
            sine, cosine = sine_cosine(2.0 * row(2 + half))
            sin_s[half, here, :] = sine
            cos_s[half, here, :] = cosine
            signal = look[0, half, here, :] + look[1, half, here, :] * cosine + look[2, half, here, :] * sine
            look[0, half, here, :] = signal
            masked = jnp.where(slot_index + 128.0 * half < count, signal, 0.0)
            cross = cross + masked * row(half)
            square = square + masked * signal
        sums_s[0, here, :] = cross
        sums_s[1, here, :] = square

    @pl.loop(0, NGROUP)
    def _(group):
        @pl.when(group == 0)
        def _():
            span = rbuf.at[pl.ds(0, (GROUP - 1) * 8)]
            pltpu.make_async_copy(span, span, recv_sem.at[0]).wait()

        @pl.when(group > 0)
        def _():
            span = rbuf.at[pl.ds(0, GROUP * 8)]
            pltpu.make_async_copy(span, span, recv_sem.at[group]).wait()

        gather_group(group)

    match = match_s[...] > 0.5
    cross, square = (
        jnp.sum(
            jnp.where(match, jnp.sum(sums_s[k], axis=1, keepdims=True), 0.0), axis=0, keepdims=True
        )
        for k in range(2)
    )
    mine = stat_r.at[me]
    mine[...] = jnp.concatenate([cross, square], axis=0)
    to_all(
        lambda to: pltpu.make_async_remote_copy(
            mine, mine, stat_send, stat_recv, device_id=to, device_id_type=MESH
        ).start()
    )
    count = rbuf[pl.ds(6, 128, stride=8), :]
    slot = col_i.astype(F32)
    rest = stat_r.at[pl.ds(0, NDEV - 1)]
    pltpu.make_async_copy(rest, rest, stat_recv).wait()
    total = jnp.sum(stat_r[...], axis=0)
    gains = total[0:1] / (total[1:2] + 1e-06)
    lane = lax.broadcasted_iota(jnp.int32, (1, 128), 1)
    own_gain = jnp.sum(jnp.where(lane == me, gains, 0.0), axis=1, keepdims=True)
    gain_col = jnp.sum(jnp.where(match, gains, 0.0), axis=1, keepdims=True)
    gain_full = jnp.broadcast_to(gain_col, (128, 128))

    hits = [jnp.zeros((1, 128), F32) for _ in range(2)]
    for half in range(2):
        data = rbuf[pl.ds(half, 128, stride=8), :]
        good = slot + 128.0 * half < count
        residual = jnp.where(good, data - gain_full * look[0, half], 0.0)
        for c, weight in enumerate((residual, residual * cos_s[half], residual * sin_s[half])):
            upper = weight.astype(BF16).astype(F32)
            wsplit[c, half] = upper
            wsplit[3 + c, half] = weight - upper
        late = jnp.where(hi_s[half] >= 128.0, 1.0, 0.0)
        valid = jnp.where(good, 1.0, 0.0)
        hits[1] = hits[1] + jnp.sum(valid * late, axis=0, keepdims=True)
        hits[0] = hits[0] + jnp.sum(valid * (1.0 - late), axis=0, keepdims=True)

    low_index = lax.broadcasted_iota(jnp.int32, (64, 128), 0).astype(F32).astype(BF16).reshape(4, 16, 128)

    @pl.loop(0, NDEV // UNROLL)
    def _(step):
        lefts = []
        rights = []
        for u in range(UNROLL):
            s = step * UNROLL + u
            for half in range(2):
                rights.append(one_hot(hi_s[half, pl.ds(s, 1), :], 256))
                low = jnp.broadcast_to(lo_s[half, pl.ds(s, 1), :], (16, 128)).astype(BF16)
                same = low_index == low[None]
                rows = []
                for w in range(6):
                    value = jnp.broadcast_to(wsplit[w, half, pl.ds(s, 1), :], (16, 128)).astype(BF16)
                    rows.append(jnp.where(same, value[None], jnp.zeros((), BF16)).reshape(64, 128))
                lefts.append(jnp.concatenate(rows, axis=0))
        acc[...] += lax.dot_general(
            jnp.concatenate(lefts, axis=1), jnp.concatenate(rights, axis=1),
            (((1,), (1,)), ((), ())), preferred_element_type=F32,
        )

    field = acc[:192] + acc[192:]

    for load in loads[6:9]:
        load.wait()
    z_parts = []
    for cyc in range(2):
        y = dot3(split_parts(field[:, cyc * 128 : cyc * 128 + 128]), (first[0], first[1]))
        for c in range(3):
            y_re = y[c * 64 : c * 64 + 64, :128]
            y_im = y[c * 64 : c * 64 + 64, 128:]
            z_re = y_re * twist[0] + y_im * twist[1]
            z_im = y_im * twist[0] - y_re * twist[1]
            z_parts.append(jnp.concatenate([z_re, z_im], axis=0))
    x = dot3((last[0], last[1]), split_parts(jnp.concatenate(z_parts, axis=1)))
    for cyc in range(2):
        for c in range(3):
            block = x[:, (cyc * 3 + c) * 128 : (cyc * 3 + c) * 128 + 128]
            spec_s[pl.ds(cyc * 8 + 2 * c, 32, stride=16), :] = block[:32]
            spec_s[pl.ds(cyc * 8 + 2 * c + 1, 32, stride=16), :] = block[32:]
        weight = jnp.sum(hits[cyc], axis=1, keepdims=True) * (1.0 / 8192)
        for r in (6, 7):
            spec_s[pl.ds(cyc * 8 + r, 32, stride=16), :] = jnp.broadcast_to(weight, (32, 128))

    def send_spectrum(where, to, skip, tiles, slot, send, recv):
        pltpu.make_async_remote_copy(
            spec_s.at[pl.ds(to * 16 + skip * 8, tiles * 8)], spec_r.at[pl.ds(slot * 8, tiles * 8)],
            send, recv, device_id=(where, to), device_id_type=MESH,
        ).start()

    def send_rim(where, skip, tiles, slot, recv):
        send = lambda to: send_spectrum(where, to, skip, tiles, slot, rim_send, recv)
        to_tm(send)
        send(tm)

    rims = []
    for at, bound, step, skip, tiles, slot, side in (
        (0, det > 0, -1, 0, 2, 67, 1),
        (1, det > 0, -1, 0, 1, 69, 1),
        (NTM - 2, det < NDET - 1, 1, 1, 1, 0, 0),
        (NTM - 1, det < NDET - 1, 1, 0, 2, 1, 0),
    ):
        here = jnp.logical_and(tm == at, bound)
        rims.append((here, tiles))

        @pl.when(here)
        def _():
            send_rim(det + step, skip, tiles, slot, rim_recv.at[side])

    to_tm(lambda to: send_spectrum(det, to, 0, 2, 3 + 2 * tm, spec_send, spec_recv))
    spec_r[pl.ds((3 + 2 * tm) * 8, 16), :] = spec_s[pl.ds(tm * 16, 16), :]
    for c in range(3):
        for cyc in range(2):
            block = field[c * 64 : c * 64 + 64, cyc * 128 : cyc * 128 + 128]
            block = jnp.concatenate([block[:, :64], block[:, 64:]], axis=0)
            map_s[c, pl.ds(cyc, 64, stride=2), :] = block.T
    loads[5].wait()
    loads[9].wait()
    loads[10].wait()

    @pl.when(det > 0)
    def _():
        for copy in go_down:
            copy.wait_recv()

    @pl.when(det < NDET - 1)
    def _():
        for copy in go_up:
            copy.wait_recv()

    for c in range(3):
        root_s[c] = jnp.sqrt(pp[c])

    @pl.when(det > 0)
    def _():
        span = spec_r.at[pl.ds(0, 24)]
        pltpu.make_async_copy(span, span, rim_recv.at[0]).wait()

    @pl.when(det < NDET - 1)
    def _():
        span = spec_r.at[pl.ds(0, 24)]
        pltpu.make_async_copy(span, span, rim_recv.at[1]).wait()

    span = spec_r.at[pl.ds(0, (NTM - 1) * 16)]
    pltpu.make_async_copy(span, span, spec_recv).wait()

    for j in range(7):
        bw[j, 5:75, :] = spec_r[pl.ds(j, 70, stride=8), :]
    noise_root = jnp.sqrt(bw[6])
    for j in range(6):
        noise = jnp.concatenate([edge[0, j], onoise[j], edge[1, j]], axis=0)
        prior = jnp.concatenate([edge[0, 6 + j], oprior[j], edge[1, 6 + j]], axis=0)
        bw[j] = bw[j] + noise_root * noise + root_s[j // 2] * prior

    moments = [jnp.zeros((8, 128), F32) for _ in range(6)]
    for c in range(3):
        precision = pp[c]
        root = root_s[c]
        side = root * (0.45 / SCALE)
        diagonal = (precision + bw[6] - SHIFT) * (1.0 / SCALE)

        def step(v):
            u = root * v
            beside = pltpu.roll(u, 1, 0) + pltpu.roll(u, 79, 0)
            return diagonal * v - side * beside

        for p in range(2):
            j = 2 * c + p
            v0 = bw[j]
            v1 = step(v0)
            v2 = step(v1)
            v3 = step(v2)
            own = [v[8:72] for v in (v0, v1, v2, v3)]
            v1_s[j] = own[1]
            v2_s[j] = own[2]
            for m, (a, b) in enumerate(((0, 0), (0, 1), (1, 1), (1, 2), (2, 2), (2, 3))):
                moments[m] = moments[m] + jnp.sum((own[a] * own[b]).reshape(8, 8, 128), axis=0)
    message = jnp.zeros((1, 128), F32)
    for m in range(6):
        value = jnp.sum(jnp.sum(moments[m], axis=0, keepdims=True), axis=1, keepdims=True)
        message = jnp.where(lane == m, jnp.broadcast_to(value, (1, 128)), message)
    own_row = mom_r.at[me]
    own_row[...] = message
    to_all(
        lambda to: pltpu.make_async_remote_copy(
            own_row, own_row, mom_send, mom_recv, device_id=to, device_id_type=MESH
        ).start()
    )
    rest = mom_r.at[pl.ds(0, NDEV - 1)]
    pltpu.make_async_copy(rest, rest, mom_recv).wait()
    sums = jnp.sum(mom_r[...], axis=0)
    nu = [jnp.sum(jnp.where(lane == m, sums, 0.0), axis=1, keepdims=True) for m in range(6)]

    zero = jnp.zeros((1, 1), F32)

    def inner(a, b):
        terms = {}
        for i, x_i in enumerate(a):
            for j, y_j in enumerate(b):
                terms[i + j] = terms.get(i + j, zero) + x_i * y_j
        out = zero
        for power, value in terms.items():
            out = out + value * nu[power]
        return out

    def image_of(a):
        longer = list(a) + [zero]
        return [SHIFT * longer[i] + (SCALE * longer[i - 1] if i else zero) for i in range(len(longer))]

    resid = [zero + 1.0]
    direction = [zero + 1.0]
    answer = [zero, zero, zero]
    norm_now = nu[0]
    for iteration in range(3):
        image = image_of(direction)
        alpha = norm_now / inner(direction, image)
        alpha = jnp.minimum(jnp.maximum(alpha, 0.0), STEP_MAX)
        for i, value in enumerate(direction):
            answer[i] = answer[i] + alpha * value
        if iteration < 2:
            resid = resid + [zero]
            resid = [r - alpha * w for r, w in zip(resid, image)]
            norm_next = jnp.maximum(inner(resid, resid), 0.0)
            beta = norm_next / norm_now
            direction = [r + beta * d for r, d in zip(resid, direction + [zero])]
            norm_now = norm_next
    small_out[...] = jnp.broadcast_to(own_gain, (8, 128))
    for j in range(6):
        sol_out[j] = answer[0] * bw[j, 8:72, :] + answer[1] * v1_s[j] + answer[2] * v2_s[j]

    span = sbuf.at[pl.ds(0, (NDEV - 1) * 8)]
    pltpu.make_async_copy(span, span, send_sem).wait()
    rest = stat_r.at[pl.ds(0, NDEV - 1)]
    pltpu.make_async_copy(rest, rest, stat_send).wait()
    span = spec_s.at[pl.ds(0, (NTM - 1) * 16)]
    pltpu.make_async_copy(span, span, spec_send).wait()
    rest = mom_r.at[pl.ds(0, NDEV - 1)]
    pltpu.make_async_copy(rest, rest, mom_send).wait()

    for here, tiles in rims:
        @pl.when(here)
        def _():
            span = spec_s.at[pl.ds(0, NTM * tiles * 8)]
            pltpu.make_async_copy(span, span, rim_send).wait()

    @pl.when(det < NDET - 1)
    def _():
        for copy in go_down:
            copy.wait_send()

    @pl.when(det > 0)
    def _():
        for copy in go_up:
            copy.wait_send()


def finish(small, map_in, sol_in, gain_out, map_out, sol_out, out_sem):
    stores = [
        pltpu.make_async_copy(sol_in, sol_out, out_sem.at[0]),
        pltpu.make_async_copy(map_in, map_out, out_sem.at[1]),
    ]
    for store in stores:
        store.start()
    gain_out[...] = small[0:1, 0:1]
    for store in stores:
        store.wait()


def per_device(
    samples, pointing, angles, counts, sky_map, prior_precision, omega_noise, omega_prior
):
    sky = sky_map.reshape(3, 2, 64, 128).transpose(0, 2, 1, 3).reshape(3, 128, 128)
    vmem = pl.BlockSpec(memory_space=pltpu.VMEM)
    dma = pltpu.SemaphoreType.DMA
    anywhere = pl.BlockSpec(memory_space=pl.ANY)
    small, binned, solved = pl.pallas_call(
        kernel,
        name="gibbs_step",
        out_shape=(
            pltpu.VMEM((8, 128), F32),
            pltpu.VMEM((3, 128, 128), F32),
            pltpu.VMEM((6, 64, 128), F32),
        ),
        in_specs=[anywhere] * 12,
        out_specs=(vmem, vmem, vmem),
        scratch_shapes=[
            pltpu.VMEM((128, 256), F32),
            pltpu.VMEM((128, 256), jnp.int32),
            pltpu.VMEM((128, 256), F32),
            pltpu.VMEM((1, 128), jnp.int32),
            pltpu.VMEM((3, 128, 128), F32),
            pltpu.VMEM((6, 64, 128), F32),
            pltpu.VMEM((6, 64, 128), F32),
            pltpu.VMEM((2, 128, 256), BF16),
            pltpu.VMEM((2, 64, 128), F32),
            pltpu.VMEM((2, 64, 128), BF16),
            pltpu.VMEM((NDEV, 128), jnp.int32),
            pltpu.VMEM((NDEV, 128), F32),
            pltpu.VMEM((1024, 128), F32),
            pltpu.VMEM((1024, 128), F32),
            pltpu.VMEM((384, 256), BF16),
            pltpu.VMEM((2, 128, 128), F32),
            pltpu.VMEM((2, 128, 128), F32),
            pltpu.VMEM((2, 128, 128), F32),
            pltpu.VMEM((2, 128, 128), F32),
            pltpu.VMEM((3, 2, 128, 128), F32),
            pltpu.VMEM((2, 128, 128), F32),
            pltpu.VMEM((6, 2, 128, 128), F32),
            pltpu.VMEM((384, 256), F32),
            pltpu.VMEM((NDEV, 2, 128), F32),
            pltpu.VMEM((NTM * 16, 128), F32),
            pltpu.VMEM((70 * 8, 128), F32),
            pltpu.VMEM((3, 80, 128), F32),
            pltpu.VMEM((3, 80, 128), F32),
            pltpu.VMEM((2, 12, 8, 128), F32),
            pltpu.VMEM((7, 80, 128), F32),
            pltpu.VMEM((6, 64, 128), F32),
            pltpu.VMEM((6, 64, 128), F32),
            pltpu.VMEM((NDEV, 1, 128), F32),
            dma, dma((NGROUP,)), dma, dma, dma, dma,
            dma, dma((2,)), dma((2, 3)), dma((2, 3)), dma, dma,
            dma((12,)),
        ],
        compiler_params=pltpu.CompilerParams(collective_id=0, has_side_effects=True),
    )(
        samples.reshape(128, 256),
        pointing.reshape(128, 256),
        angles.reshape(128, 256),
        counts.reshape(1, 128),
        sky,
        prior_precision,
        omega_noise,
        omega_prior,
        *(jnp.asarray(t) for t in tables()),
    )
    gain, binned, solved = pl.pallas_call(
        finish,
        name="finish",
        out_shape=(
            jax.ShapeDtypeStruct((1, 1), F32),
            jax.ShapeDtypeStruct((3, 128, 128), F32),
            jax.ShapeDtypeStruct((6, 64, 128), F32),
        ),
        in_specs=[vmem, vmem, vmem],
        out_specs=(vmem, anywhere, anywhere),
        scratch_shapes=[dma((2,))],
    )(*(pltpu.with_memory_space_constraint(x, pltpu.VMEM) for x in (small, binned, solved)))
    binned = binned.reshape(3, 64, 2, 128).transpose(0, 2, 1, 3).reshape(3, 2, 8192)
    return (gain, binned, solved)


def solution(mesh):
    return jax.shard_map(
        per_device,
        mesh=mesh,
        in_specs=(
            P("det", "tm", None, None),
            P("det", "tm", None, None),
            P("det", "tm", None, None),
            P("det", "tm", None),
            P(None, ("det", "tm"), None),
            P(None, "det", "tm"),
            P(None, "det", "tm"),
            P(None, "det", "tm"),
        ),
        out_specs=(P("det", "tm"), P(None, ("det", "tm"), None), P(None, "det", "tm")),
        check_vma=False,
    )
```

```python
import math

import jax
import jax.numpy as jnp
import numpy as np
from jax import lax
from jax.experimental import pallas as pl
from jax.experimental.pallas import tpu as pltpu
from jax.sharding import PartitionSpec as P

MESH = pl.DeviceIdType.MESH
F32 = jnp.float32
BF16 = jnp.bfloat16
NDET = 4
NTM = 32
NDEV = NDET * NTM
GROUP = 16
NGROUP = NDEV // GROUP
LOWER = 12
UNROLL = 32
SHIFT = 4.0
SCALE = 4.0
STEP_MAX = 20.0


def near_first():
    ring = (0, 1, 2, 1)
    return sorted(
        ((x, y, z, c) for x in range(4) for y in range(4) for z in range(4) for c in range(2)),
        key=lambda o: 4 * (ring[o[0]] + ring[o[1]] + ring[o[2]]) + o[3],
    )


NEAR = near_first()


def tables():
    h, i = np.divmod(np.arange(128), 64)
    a = 2 * i + h
    k = np.arange(128)
    ang = 2.0 * np.pi * (np.outer(a, k) % 128) / 128
    first = np.concatenate([np.cos(ang), -np.sin(ang)], axis=1)
    b = np.arange(64)
    ang = 2.0 * np.pi * np.outer(b, k) / 8192
    twist = np.stack([np.cos(ang), np.sin(ang)])
    q = np.arange(32)
    ang = 2.0 * np.pi * (np.outer(q, b) % 64) / 64
    c, s = np.cos(ang), np.sin(ang)
    last = np.concatenate([np.concatenate([c, s], axis=1), np.concatenate([-s, c], axis=1)], axis=0)
    last = last / math.sqrt(8192)
    def split(x):
        upper = x.astype(np.float32).astype(jnp.bfloat16)
        return np.stack([upper, (x - upper.astype(np.float64)).astype(jnp.bfloat16)])

    codes = np.asarray([o[0] + 4 * o[1] + 16 * o[2] + 64 * o[3] for o in NEAR], np.int32)
    codes = np.ascontiguousarray(np.broadcast_to(codes[:, None], (NDEV, 128)))
    return [split(first), twist.astype(np.float32), split(last), codes]


def split_parts(x):
    upper = x.astype(BF16)
    return upper, (x - upper.astype(F32)).astype(BF16)


def dot3(a, b):
    out = jnp.dot(a[0], b[0], preferred_element_type=F32)
    out = out + jnp.dot(a[0], b[1], preferred_element_type=F32)
    return out + jnp.dot(a[1], b[0], preferred_element_type=F32)


def sine_cosine(x):
    k = jnp.floor(x * (2.0 / math.pi) + 0.5)
    r = ((x - k * 1.5703125) - k * 4.837512969970703125e-4) - k * 7.549789948768648e-8
    z = r * r
    sine = r + r * z * (-1.6666654611e-1 + z * (8.3321608736e-3 - z * 1.9515295891e-4))
    cosine = 1.0 - 0.5 * z + z * z * (
        4.166664568298827e-2 + z * (-1.388731625493765e-3 + z * 2.443315711809948e-5)
    )
    q = k.astype(jnp.int32) & 3
    odd = (q & 1) == 1
    s = jnp.where(odd, cosine, sine)
    c = jnp.where(odd, sine, cosine)
    s = jnp.where(q >= 2, -s, s)
    c = jnp.where((q == 1) | (q == 2), -c, c)
    return s, c


def one_hot(row, rows):
    value = jnp.broadcast_to(row, (16, 128)).astype(BF16)
    index = lax.broadcasted_iota(jnp.int32, (rows, 128), 0).astype(F32).astype(BF16)
    same = index.reshape(rows // 16, 16, 128) == value[None]
    return jnp.where(same, jnp.ones((), BF16), jnp.zeros((), BF16)).reshape(rows, 128)


def kernel(
    samples_in, pointing_in, angles_in, counts_in, sky_in, prec, onoise_in, oprior_in,
    first_in, twist_in, last_in, codes_in,
    small_out, map_s, sol_out,
    samples, pointing, angles, counts, sky, onoise, oprior, first, twist, last, codes, match_s,
    sbuf, rbuf, table, hi_s, lo_s, cos_s, sin_s, look, sums_s, wsplit, acc,
    stat_r, spec_s, spec_r, pp, root_s, edge, bw, v1_s, v2_s, mom_r,
    send_sem, recv_sem, stat_send, stat_recv, spec_send, spec_recv,
    rim_send, rim_recv, edge_send, edge_recv, mom_send, mom_recv, in_sem,
):
    det = lax.axis_index("det")
    tm = lax.axis_index("tm")
    me = det * NTM + tm

    loads = [
        pltpu.make_async_copy(src, dst, in_sem.at[i])
        for i, (src, dst) in enumerate((
            (samples_in, samples), (pointing_in, pointing), (angles_in, angles), (counts_in, counts),
            (sky_in, sky), (prec, pp.at[:, 8:72, :]), (first_in, first), (twist_in, twist),
            (last_in, last), (onoise_in, onoise), (oprior_in, oprior), (codes_in, codes),
        ))
    ]
    for load in loads:
        load.start()

    ty, tz, tc = tm // 8, (tm // 2) % 4, tm % 2
    at_z = [(tz + o) % 4 * 2 for o in range(4)]
    at_c = [tc, 1 - tc]
    at_y = [(ty + o) % 4 * 8 for o in range(4)]
    at_det = [(det + o) % NDET for o in range(NDET)]

    def to_tm(act):
        def row(y, own):
            for z in (2, 1, 3, 0):
                for c in (1, 0):
                    if not (own and z == 0 and c == 0):
                        act(y * 8 + at_z[z] + at_c[c])

        @pl.loop(0, 3)
        def _(d):
            row((ty + jnp.where(d == 0, 2, jnp.where(d == 1, 1, 3))) % 4, False)

        row(ty, True)

    def to_all(act):
        to_tm(lambda to: [act((at_det[x], to)) for x in (2, 1, 3, 0)])
        for x in (2, 1, 3):
            act((at_det[x], tm))

    barrier = pltpu.get_barrier_semaphore()
    to_all(lambda to: pl.semaphore_signal(barrier, inc=1, device_id=to, device_id_type=MESH))

    for load in loads[:4]:
        load.wait()

    row_i = lax.broadcasted_iota(jnp.int32, (128, 128), 0)
    col_i = lax.broadcasted_iota(jnp.int32, (128, 128), 1)
    for half in range(2):
        lanes = slice(half * 128, half * 128 + 128)
        sbuf[pl.ds(half, 128, stride=8), :] = samples[:, lanes]
        sbuf[pl.ds(2 + half, 128, stride=8), :] = angles[:, lanes]
        sbuf[pl.ds(4 + half, 128, stride=8), :] = pointing[:, lanes].astype(F32)
    count_row = jnp.broadcast_to(counts[...].astype(F32), (128, 128))
    count_col = jnp.sum(jnp.where(row_i == col_i, count_row, 0.0), axis=1, keepdims=True)
    count_full = jnp.broadcast_to(count_col, (128, 128))
    sbuf[pl.ds(6, 128, stride=8), :] = count_full
    sbuf[pl.ds(7, 128, stride=8), :] = count_full

    loads[4].wait()

    for c in range(3):
        blocks = []
        for cyc in range(2):
            turned = sky[c, pl.ds(cyc, 64, stride=2), :].T
            blocks.append(jnp.concatenate([turned[:64], turned[64:]], axis=1))
        full = jnp.concatenate(blocks, axis=1)
        upper = full.astype(BF16)
        table[pl.ds(c * 64, 64), :] = upper
        table[pl.ds(192 + c * 64, 64), :] = (full - upper.astype(F32)).astype(BF16)

    bw[:, 0:8, :] = jnp.zeros((7, 8, 128), F32)
    bw[:, 72:80, :] = jnp.zeros((7, 8, 128), F32)

    @pl.when(det == 0)
    def _():
        pp[:, 0:8, :] = jnp.zeros((3, 8, 128), F32)
        edge[0] = jnp.zeros((12, 8, 128), F32)
        spec_r[0:24, :] = jnp.zeros((24, 128), F32)

    @pl.when(det == NDET - 1)
    def _():
        pp[:, 72:80, :] = jnp.zeros((3, 8, 128), F32)
        edge[1] = jnp.zeros((12, 8, 128), F32)
        spec_r[67 * 8 : 70 * 8, :] = jnp.zeros((24, 128), F32)

    loads[11].wait()
    code = codes[...]
    source = ((code & 3) + det) % 4 * 32 + (((code >> 2) & 3) + ty) % 4 * 8
    source = source + (((code >> 4) & 3) + tz) % 4 * 2 + ((code >> 6) + tc) % 2
    match_s[...] = jnp.where(source == col_i, 1.0, 0.0)
    acc[...] = jnp.zeros_like(acc)
    pl.semaphore_wait(barrier, NDEV - 1)

    for s, (x, y, z, c) in enumerate(NEAR):
        if s == 0:
            continue
        where = at_det[-x % 4]
        to = at_y[-y % 4] + at_z[-z % 4] + at_c[c]
        pltpu.make_async_remote_copy(
            sbuf.at[pl.ds((where * NTM + to) * 8, 8)], rbuf.at[s * 8 : s * 8 + 8],
            send_sem, recv_sem.at[s // GROUP], device_id=(where, to), device_id_type=MESH,
        ).start()
    rbuf[0:8, :] = sbuf[pl.ds(me * 8, 8), :]

    down = ((det + 1) % NDET, tm)
    up = ((det + NDET - 1) % NDET, tm)

    def edge_copies(rows, side, padded, to):
        pairs = (
            (prec.at[:, rows, :], pp.at[:, padded, :]),
            (onoise_in.at[:, rows, :], edge.at[side, 0:6]),
            (oprior_in.at[:, rows, :], edge.at[side, 6:12]),
        )
        return [
            pltpu.make_async_remote_copy(
                src, dst, edge_send.at[side, i], edge_recv.at[side, i], device_id=to, device_id_type=MESH
            )
            for i, (src, dst) in enumerate(pairs)
        ]

    go_down = edge_copies(slice(56, 64), 0, slice(0, 8), down)
    go_up = edge_copies(slice(0, 8), 1, slice(72, 80), up)

    @pl.when(det < NDET - 1)
    def _():
        for copy in go_down:
            copy.start()

    @pl.when(det > 0)
    def _():
        for copy in go_up:
            copy.start()

    col_index = lax.broadcasted_iota(jnp.int32, (64, 128), 0).astype(F32)

    slot_index = lax.broadcasted_iota(jnp.int32, (GROUP, 128), 1).astype(F32)

    def gather_group(group):
        base = group * GROUP
        here = pl.ds(base, GROUP)

        def row(r):
            return rbuf[pl.ds(base * 8 + r, GROUP, stride=8), :]

        for half in range(2):
            pixel = row(4 + half).astype(jnp.int32)
            upper = (pixel >> 13) * 128 + ((pixel >> 6) & 1) * 64 + ((pixel >> 7) & 63)
            hi_s[half, here, :] = upper.astype(F32)
            lo_s[half, here, :] = (pixel & 63).astype(F32)
        pixel = jnp.concatenate(
            [rbuf[pl.ds((base + LOWER) * 8 + 4 + half, GROUP - LOWER, stride=8), :] for half in range(2)], axis=0
        ).astype(jnp.int32)
        in_row, at_lane = ((pixel >> 7) & 63) * 2 + (pixel >> 13), pixel & 127
        picked = [jnp.zeros((8, 128), F32) for _ in range(3)]

        def permute_rows(first_r, last_r):
            for r in range(first_r, last_r):
                same = in_row == r
                for c in range(3):
                    line = jnp.broadcast_to(sky[c, r : r + 1, :], (8, 128))
                    taken = jnp.take_along_axis(line, at_lane, axis=1)
                    picked[c] = jnp.where(same, taken, picked[c])

        for u in range(LOWER):
            s = base + u
            hots = [one_hot(hi_s[half, pl.ds(s, 1), :], 256) for half in range(2)]
            got = jnp.dot(table[...], jnp.concatenate(hots, axis=1), preferred_element_type=F32)
            got = got[:192] + got[192:]
            for half in range(2):
                low = lo_s[half, pl.ds(s, 1), :]
                same = col_index == low
                for c in range(3):
                    part = got[c * 64 : c * 64 + 64, half * 128 : half * 128 + 128]
                    look[c, half, pl.ds(s, 1), :] = jnp.sum(
                        jnp.where(same, part, 0.0), axis=0, keepdims=True
                    )
            permute_rows(u * 128 // LOWER, (u + 1) * 128 // LOWER)
        for half in range(2):
            for c in range(3):
                look[c, half, pl.ds(base + LOWER, GROUP - LOWER), :] = picked[c][half * 4 : half * 4 + 4]
        count = row(6)
        cross = jnp.zeros((GROUP, 128), F32)
        square = jnp.zeros((GROUP, 128), F32)
        for half in range(2):
            sine, cosine = sine_cosine(2.0 * row(2 + half))
            sin_s[half, here, :] = sine
            cos_s[half, here, :] = cosine
            signal = look[0, half, here, :] + look[1, half, here, :] * cosine + look[2, half, here, :] * sine
            look[0, half, here, :] = signal
            masked = jnp.where(slot_index + 128.0 * half < count, signal, 0.0)
            cross = cross + masked * row(half)
            square = square + masked * signal
        sums_s[0, here, :] = cross
        sums_s[1, here, :] = square

    @pl.loop(0, NGROUP)
    def _(group):
        @pl.when(group == 0)
        def _():
            span = rbuf.at[pl.ds(0, (GROUP - 1) * 8)]
            pltpu.make_async_copy(span, span, recv_sem.at[0]).wait()

        @pl.when(group > 0)
        def _():
            span = rbuf.at[pl.ds(0, GROUP * 8)]
            pltpu.make_async_copy(span, span, recv_sem.at[group]).wait()

        gather_group(group)

    match = match_s[...] > 0.5
    cross, square = (
        jnp.sum(
            jnp.where(match, jnp.sum(sums_s[k], axis=1, keepdims=True), 0.0), axis=0, keepdims=True
        )
        for k in range(2)
    )
    mine = stat_r.at[me]
    mine[...] = jnp.concatenate([cross, square], axis=0)
    to_all(
        lambda to: pltpu.make_async_remote_copy(
            mine, mine, stat_send, stat_recv, device_id=to, device_id_type=MESH
        ).start()
    )
    count = rbuf[pl.ds(6, 128, stride=8), :]
    slot = col_i.astype(F32)
    hits = [jnp.zeros((1, 128), F32) for _ in range(2)]
    for half in range(2):
        good = slot + 128.0 * half < count
        for first_w, value in ((0, rbuf[pl.ds(half, 128, stride=8), :]), (3, look[0, half])):
            value = jnp.where(good, value, 0.0)
            wsplit[first_w, half] = value
            wsplit[first_w + 1, half] = value * cos_s[half]
            wsplit[first_w + 2, half] = value * sin_s[half]
        late = jnp.where(hi_s[half] >= 128.0, 1.0, 0.0)
        valid = jnp.where(good, 1.0, 0.0)
        hits[1] = hits[1] + jnp.sum(valid * late, axis=0, keepdims=True)
        hits[0] = hits[0] + jnp.sum(valid * (1.0 - late), axis=0, keepdims=True)
    rest = stat_r.at[pl.ds(0, NDEV - 1)]
    pltpu.make_async_copy(rest, rest, stat_recv).wait()
    total = jnp.sum(stat_r[...], axis=0)
    gains = total[0:1] / (total[1:2] + 1e-06)
    lane = lax.broadcasted_iota(jnp.int32, (1, 128), 1)
    own_gain = jnp.sum(jnp.where(lane == me, gains, 0.0), axis=1, keepdims=True)
    gain_col = jnp.sum(jnp.where(match, gains, 0.0), axis=1, keepdims=True)
    gain_full = jnp.broadcast_to(gain_col, (128, 128))

    for half in range(2):
        for c in range(3):
            weight = wsplit[c, half] - gain_full * wsplit[3 + c, half]
            upper = weight.astype(BF16).astype(F32)
            wsplit[c, half] = upper
            wsplit[3 + c, half] = weight - upper

    low_index = lax.broadcasted_iota(jnp.int32, (64, 128), 0).astype(F32).astype(BF16).reshape(4, 16, 128)

    @pl.loop(0, NDEV // UNROLL)
    def _(step):
        lefts = []
        rights = []
        for u in range(UNROLL):
            s = step * UNROLL + u
            for half in range(2):
                rights.append(one_hot(hi_s[half, pl.ds(s, 1), :], 256))
                low = jnp.broadcast_to(lo_s[half, pl.ds(s, 1), :], (16, 128)).astype(BF16)
                same = low_index == low[None]
                rows = []
                for w in range(6):
                    value = jnp.broadcast_to(wsplit[w, half, pl.ds(s, 1), :], (16, 128)).astype(BF16)
                    rows.append(jnp.where(same, value[None], jnp.zeros((), BF16)).reshape(64, 128))
                lefts.append(jnp.concatenate(rows, axis=0))
        acc[...] += lax.dot_general(
            jnp.concatenate(lefts, axis=1), jnp.concatenate(rights, axis=1),
            (((1,), (1,)), ((), ())), preferred_element_type=F32,
        )

    field = acc[:192] + acc[192:]

    for load in loads[6:9]:
        load.wait()
    z_parts = []
    for cyc in range(2):
        y = dot3(split_parts(field[:, cyc * 128 : cyc * 128 + 128]), (first[0], first[1]))
        for c in range(3):
            y_re = y[c * 64 : c * 64 + 64, :128]
            y_im = y[c * 64 : c * 64 + 64, 128:]
            z_re = y_re * twist[0] + y_im * twist[1]
            z_im = y_im * twist[0] - y_re * twist[1]
            z_parts.append(jnp.concatenate([z_re, z_im], axis=0))
    x = dot3((last[0], last[1]), split_parts(jnp.concatenate(z_parts, axis=1)))
    for cyc in range(2):
        for c in range(3):
            block = x[:, (cyc * 3 + c) * 128 : (cyc * 3 + c) * 128 + 128]
            spec_s[pl.ds(cyc * 8 + 2 * c, 32, stride=16), :] = block[:32]
            spec_s[pl.ds(cyc * 8 + 2 * c + 1, 32, stride=16), :] = block[32:]
        weight = jnp.sum(hits[cyc], axis=1, keepdims=True) * (1.0 / 8192)
        for r in (6, 7):
            spec_s[pl.ds(cyc * 8 + r, 32, stride=16), :] = jnp.broadcast_to(weight, (32, 128))

    def send_spectrum(where, to, skip, tiles, slot, send, recv):
        pltpu.make_async_remote_copy(
            spec_s.at[pl.ds(to * 16 + skip * 8, tiles * 8)], spec_r.at[pl.ds(slot * 8, tiles * 8)],
            send, recv, device_id=(where, to), device_id_type=MESH,
        ).start()

    def send_rim(where, skip, tiles, slot, recv):
        send = lambda to: send_spectrum(where, to, skip, tiles, slot, rim_send, recv)
        to_tm(send)
        send(tm)

    rims = []
    for at, bound, step, skip, tiles, slot, side in (
        (0, det > 0, -1, 0, 2, 67, 1),
        (1, det > 0, -1, 0, 1, 69, 1),
        (NTM - 2, det < NDET - 1, 1, 1, 1, 0, 0),
        (NTM - 1, det < NDET - 1, 1, 0, 2, 1, 0),
    ):
        here = jnp.logical_and(tm == at, bound)
        rims.append((here, tiles))

        @pl.when(here)
        def _():
            send_rim(det + step, skip, tiles, slot, rim_recv.at[side])

    to_tm(lambda to: send_spectrum(det, to, 0, 2, 3 + 2 * tm, spec_send, spec_recv))
    spec_r[pl.ds((3 + 2 * tm) * 8, 16), :] = spec_s[pl.ds(tm * 16, 16), :]
    for c in range(3):
        for cyc in range(2):
            block = field[c * 64 : c * 64 + 64, cyc * 128 : cyc * 128 + 128]
            block = jnp.concatenate([block[:, :64], block[:, 64:]], axis=0)
            map_s[c, pl.ds(cyc, 64, stride=2), :] = block.T
    loads[5].wait()
    loads[9].wait()
    loads[10].wait()

    @pl.when(det > 0)
    def _():
        for copy in go_down:
            copy.wait_recv()

    @pl.when(det < NDET - 1)
    def _():
        for copy in go_up:
            copy.wait_recv()

    for c in range(3):
        root_s[c] = jnp.sqrt(pp[c])

    @pl.when(det > 0)
    def _():
        span = spec_r.at[pl.ds(0, 24)]
        pltpu.make_async_copy(span, span, rim_recv.at[0]).wait()

    @pl.when(det < NDET - 1)
    def _():
        span = spec_r.at[pl.ds(0, 24)]
        pltpu.make_async_copy(span, span, rim_recv.at[1]).wait()

    span = spec_r.at[pl.ds(0, (NTM - 1) * 16)]
    pltpu.make_async_copy(span, span, spec_recv).wait()

    for j in range(7):
        bw[j, 5:75, :] = spec_r[pl.ds(j, 70, stride=8), :]
    noise_root = jnp.sqrt(bw[6])
    for j in range(6):
        noise = jnp.concatenate([edge[0, j], onoise[j], edge[1, j]], axis=0)
        prior = jnp.concatenate([edge[0, 6 + j], oprior[j], edge[1, 6 + j]], axis=0)
        bw[j] = bw[j] + noise_root * noise + root_s[j // 2] * prior

    moments = [jnp.zeros((8, 128), F32) for _ in range(6)]
    for c in range(3):
        precision = pp[c]
        root = root_s[c]
        side = root * (0.45 / SCALE)
        diagonal = (precision + bw[6] - SHIFT) * (1.0 / SCALE)

        def step(v):
            u = root * v
            beside = pltpu.roll(u, 1, 0) + pltpu.roll(u, 79, 0)
            return diagonal * v - side * beside

        for p in range(2):
            j = 2 * c + p
            v0 = bw[j]
            v1 = step(v0)
            v2 = step(v1)
            v3 = step(v2)
            own = [v[8:72] for v in (v0, v1, v2, v3)]
            v1_s[j] = own[1]
            v2_s[j] = own[2]
            for m, (a, b) in enumerate(((0, 0), (0, 1), (1, 1), (1, 2), (2, 2), (2, 3))):
                moments[m] = moments[m] + jnp.sum((own[a] * own[b]).reshape(8, 8, 128), axis=0)
    message = jnp.zeros((1, 128), F32)
    for m in range(6):
        value = jnp.sum(jnp.sum(moments[m], axis=0, keepdims=True), axis=1, keepdims=True)
        message = jnp.where(lane == m, jnp.broadcast_to(value, (1, 128)), message)
    own_row = mom_r.at[me]
    own_row[...] = message
    to_all(
        lambda to: pltpu.make_async_remote_copy(
            own_row, own_row, mom_send, mom_recv, device_id=to, device_id_type=MESH
        ).start()
    )
    rest = mom_r.at[pl.ds(0, NDEV - 1)]
    pltpu.make_async_copy(rest, rest, mom_recv).wait()
    sums = jnp.sum(mom_r[...], axis=0)
    nu = [jnp.sum(jnp.where(lane == m, sums, 0.0), axis=1, keepdims=True) for m in range(6)]

    zero = jnp.zeros((1, 1), F32)

    def inner(a, b):
        terms = {}
        for i, x_i in enumerate(a):
            for j, y_j in enumerate(b):
                terms[i + j] = terms.get(i + j, zero) + x_i * y_j
        out = zero
        for power, value in terms.items():
            out = out + value * nu[power]
        return out

    def image_of(a):
        longer = list(a) + [zero]
        return [SHIFT * longer[i] + (SCALE * longer[i - 1] if i else zero) for i in range(len(longer))]

    resid = [zero + 1.0]
    direction = [zero + 1.0]
    answer = [zero, zero, zero]
    norm_now = nu[0]
    for iteration in range(3):
        image = image_of(direction)
        alpha = norm_now / inner(direction, image)
        alpha = jnp.minimum(jnp.maximum(alpha, 0.0), STEP_MAX)
        for i, value in enumerate(direction):
            answer[i] = answer[i] + alpha * value
        if iteration < 2:
            resid = resid + [zero]
            resid = [r - alpha * w for r, w in zip(resid, image)]
            norm_next = jnp.maximum(inner(resid, resid), 0.0)
            beta = norm_next / norm_now
            direction = [r + beta * d for r, d in zip(resid, direction + [zero])]
            norm_now = norm_next
    small_out[...] = jnp.broadcast_to(own_gain, (8, 128))
    for j in range(6):
        sol_out[j] = answer[0] * bw[j, 8:72, :] + answer[1] * v1_s[j] + answer[2] * v2_s[j]

    span = sbuf.at[pl.ds(0, (NDEV - 1) * 8)]
    pltpu.make_async_copy(span, span, send_sem).wait()
    rest = stat_r.at[pl.ds(0, NDEV - 1)]
    pltpu.make_async_copy(rest, rest, stat_send).wait()
    span = spec_s.at[pl.ds(0, (NTM - 1) * 16)]
    pltpu.make_async_copy(span, span, spec_send).wait()
    rest = mom_r.at[pl.ds(0, NDEV - 1)]
    pltpu.make_async_copy(rest, rest, mom_send).wait()

    for here, tiles in rims:
        @pl.when(here)
        def _():
            span = spec_s.at[pl.ds(0, NTM * tiles * 8)]
            pltpu.make_async_copy(span, span, rim_send).wait()

    @pl.when(det < NDET - 1)
    def _():
        for copy in go_down:
            copy.wait_send()

    @pl.when(det > 0)
    def _():
        for copy in go_up:
            copy.wait_send()


def finish(small, map_in, sol_in, gain_out, map_out, sol_out, out_sem):
    stores = [
        pltpu.make_async_copy(sol_in, sol_out, out_sem.at[0]),
        pltpu.make_async_copy(map_in, map_out, out_sem.at[1]),
    ]
    for store in stores:
        store.start()
    gain_out[...] = small[0:1, 0:1]
    for store in stores:
        store.wait()


def per_device(
    samples, pointing, angles, counts, sky_map, prior_precision, omega_noise, omega_prior
):
    sky = sky_map.reshape(3, 2, 64, 128).transpose(0, 2, 1, 3).reshape(3, 128, 128)
    vmem = pl.BlockSpec(memory_space=pltpu.VMEM)
    dma = pltpu.SemaphoreType.DMA
    anywhere = pl.BlockSpec(memory_space=pl.ANY)
    small, binned, solved = pl.pallas_call(
        kernel,
        name="gibbs_step",
        out_shape=(
            pltpu.VMEM((8, 128), F32),
            pltpu.VMEM((3, 128, 128), F32),
            pltpu.VMEM((6, 64, 128), F32),
        ),
        in_specs=[anywhere] * 12,
        out_specs=(vmem, vmem, vmem),
        scratch_shapes=[
            pltpu.VMEM((128, 256), F32),
            pltpu.VMEM((128, 256), jnp.int32),
            pltpu.VMEM((128, 256), F32),
            pltpu.VMEM((1, 128), jnp.int32),
            pltpu.VMEM((3, 128, 128), F32),
            pltpu.VMEM((6, 64, 128), F32),
            pltpu.VMEM((6, 64, 128), F32),
            pltpu.VMEM((2, 128, 256), BF16),
            pltpu.VMEM((2, 64, 128), F32),
            pltpu.VMEM((2, 64, 128), BF16),
            pltpu.VMEM((NDEV, 128), jnp.int32),
            pltpu.VMEM((NDEV, 128), F32),
            pltpu.VMEM((1024, 128), F32),
            pltpu.VMEM((1024, 128), F32),
            pltpu.VMEM((384, 256), BF16),
            pltpu.VMEM((2, 128, 128), F32),
            pltpu.VMEM((2, 128, 128), F32),
            pltpu.VMEM((2, 128, 128), F32),
            pltpu.VMEM((2, 128, 128), F32),
            pltpu.VMEM((3, 2, 128, 128), F32),
            pltpu.VMEM((2, 128, 128), F32),
            pltpu.VMEM((6, 2, 128, 128), F32),
            pltpu.VMEM((384, 256), F32),
            pltpu.VMEM((NDEV, 2, 128), F32),
            pltpu.VMEM((NTM * 16, 128), F32),
            pltpu.VMEM((70 * 8, 128), F32),
            pltpu.VMEM((3, 80, 128), F32),
            pltpu.VMEM((3, 80, 128), F32),
            pltpu.VMEM((2, 12, 8, 128), F32),
            pltpu.VMEM((7, 80, 128), F32),
            pltpu.VMEM((6, 64, 128), F32),
            pltpu.VMEM((6, 64, 128), F32),
            pltpu.VMEM((NDEV, 1, 128), F32),
            dma, dma((NGROUP,)), dma, dma, dma, dma,
            dma, dma((2,)), dma((2, 3)), dma((2, 3)), dma, dma,
            dma((12,)),
        ],
        compiler_params=pltpu.CompilerParams(collective_id=0, has_side_effects=True),
    )(
        samples.reshape(128, 256),
        pointing.reshape(128, 256),
        angles.reshape(128, 256),
        counts.reshape(1, 128),
        sky,
        prior_precision,
        omega_noise,
        omega_prior,
        *(jnp.asarray(t) for t in tables()),
    )
    gain, binned, solved = pl.pallas_call(
        finish,
        name="finish",
        out_shape=(
            jax.ShapeDtypeStruct((1, 1), F32),
            jax.ShapeDtypeStruct((3, 128, 128), F32),
            jax.ShapeDtypeStruct((6, 64, 128), F32),
        ),
        in_specs=[vmem, vmem, vmem],
        out_specs=(vmem, anywhere, anywhere),
        scratch_shapes=[dma((2,))],
    )(*(pltpu.with_memory_space_constraint(x, pltpu.VMEM) for x in (small, binned, solved)))
    binned = binned.reshape(3, 64, 2, 128).transpose(0, 2, 1, 3).reshape(3, 2, 8192)
    return (gain, binned, solved)


def solution(mesh):
    return jax.shard_map(
        per_device,
        mesh=mesh,
        in_specs=(
            P("det", "tm", None, None),
            P("det", "tm", None, None),
            P("det", "tm", None, None),
            P("det", "tm", None),
            P(None, ("det", "tm"), None),
            P(None, "det", "tm"),
            P(None, "det", "tm"),
            P(None, "det", "tm"),
        ),
        out_specs=(P("det", "tm"), P(None, ("det", "tm"), None), P(None, "det", "tm")),
        check_vma=False,
    )
```

```python
import math

import jax
import jax.numpy as jnp
import numpy as np
from jax import lax
from jax.experimental import pallas as pl
from jax.experimental.pallas import tpu as pltpu
from jax.sharding import PartitionSpec as P

MESH = pl.DeviceIdType.MESH
F32 = jnp.float32
BF16 = jnp.bfloat16
NDET = 4
NTM = 32
NDEV = NDET * NTM
GROUP = 32
NGROUP = NDEV // GROUP
LOWER = 24
UNROLL = 64
SHIFT = 4.0
SCALE = 4.0
STEP_MAX = 20.0


def near_first():
    ring = (0, 1, 2, 1)
    return sorted(
        ((x, y, z, c) for x in range(4) for y in range(4) for z in range(4) for c in range(2)),
        key=lambda o: 4 * (ring[o[0]] + ring[o[1]] + ring[o[2]]) + o[3],
    )


NEAR = near_first()


def tables():
    h, i = np.divmod(np.arange(128), 64)
    a = 2 * i + h
    k = np.arange(128)
    ang = 2.0 * np.pi * (np.outer(a, k) % 128) / 128
    first = np.concatenate([np.cos(ang), -np.sin(ang)], axis=1)
    b = np.arange(64)
    ang = 2.0 * np.pi * np.outer(b, k) / 8192
    twist = np.stack([np.cos(ang), np.sin(ang)])
    q = np.arange(32)
    ang = 2.0 * np.pi * (np.outer(q, b) % 64) / 64
    c, s = np.cos(ang), np.sin(ang)
    last = np.concatenate([np.concatenate([c, s], axis=1), np.concatenate([-s, c], axis=1)], axis=0)
    last = last / math.sqrt(8192)
    def split(x):
        upper = x.astype(np.float32).astype(jnp.bfloat16)
        return np.stack([upper, (x - upper.astype(np.float64)).astype(jnp.bfloat16)])

    codes = np.asarray([o[0] + 4 * o[1] + 16 * o[2] + 64 * o[3] for o in NEAR], np.int32)
    codes = np.ascontiguousarray(np.broadcast_to(codes[:, None], (NDEV, 128)))
    return [split(first), twist.astype(np.float32), split(last), codes]


def split_parts(x):
    upper = x.astype(BF16)
    return upper, (x - upper.astype(F32)).astype(BF16)


def dot3(a, b):
    out = jnp.dot(a[0], b[0], preferred_element_type=F32)
    out = out + jnp.dot(a[0], b[1], preferred_element_type=F32)
    return out + jnp.dot(a[1], b[0], preferred_element_type=F32)


def sine_cosine(x):
    k = jnp.floor(x * (2.0 / math.pi) + 0.5)
    r = ((x - k * 1.5703125) - k * 4.837512969970703125e-4) - k * 7.549789948768648e-8
    z = r * r
    sine = r + r * z * (-1.6666654611e-1 + z * (8.3321608736e-3 - z * 1.9515295891e-4))
    cosine = 1.0 - 0.5 * z + z * z * (
        4.166664568298827e-2 + z * (-1.388731625493765e-3 + z * 2.443315711809948e-5)
    )
    q = k.astype(jnp.int32) & 3
    odd = (q & 1) == 1
    s = jnp.where(odd, cosine, sine)
    c = jnp.where(odd, sine, cosine)
    s = jnp.where(q >= 2, -s, s)
    c = jnp.where((q == 1) | (q == 2), -c, c)
    return s, c


def one_hot(row, rows):
    value = jnp.broadcast_to(row, (16, 128)).astype(BF16)
    index = lax.broadcasted_iota(jnp.int32, (rows, 128), 0).astype(F32).astype(BF16)
    same = index.reshape(rows // 16, 16, 128) == value[None]
    return jnp.where(same, jnp.ones((), BF16), jnp.zeros((), BF16)).reshape(rows, 128)


def kernel(
    samples_in, pointing_in, angles_in, counts_in, sky_in, prec, onoise_in, oprior_in,
    first_in, twist_in, last_in, codes_in,
    small_out, map_s, sol_out,
    samples, pointing, angles, counts, sky, onoise, oprior, first, twist, last, codes, match_s,
    sbuf, rbuf, table, hi_s, lo_s, cos_s, sin_s, look, sums_s, wsplit, acc,
    stat_r, spec_s, spec_r, pp, root_s, edge, bw, v1_s, v2_s, mom_r,
    send_sem, recv_sem, stat_send, stat_recv, spec_send, spec_recv,
    rim_send, rim_recv, edge_send, edge_recv, mom_send, mom_recv, in_sem,
):
    det = lax.axis_index("det")
    tm = lax.axis_index("tm")
    me = det * NTM + tm

    ty, tz, tc = tm // 8, (tm // 2) % 4, tm % 2
    at_z = [(tz + o) % 4 * 2 for o in range(4)]
    at_c = [tc, 1 - tc]
    at_y = [(ty + o) % 4 * 8 for o in range(4)]
    at_det = [(det + o) % NDET for o in range(NDET)]

    def to_tm(act):
        def row(y, own):
            for z in (2, 1, 3, 0):
                for c in (1, 0):
                    if not (own and z == 0 and c == 0):
                        act(y * 8 + at_z[z] + at_c[c])

        @pl.loop(0, 3)
        def _(d):
            row((ty + jnp.where(d == 0, 2, jnp.where(d == 1, 1, 3))) % 4, False)

        row(ty, True)

    def to_all(act):
        to_tm(lambda to: [act((at_det[x], to)) for x in (2, 1, 3, 0)])
        for x in (2, 1, 3):
            act((at_det[x], tm))

    barrier = pltpu.get_barrier_semaphore()
    to_all(lambda to: pl.semaphore_signal(barrier, inc=1, device_id=to, device_id_type=MESH))

    loads = [
        pltpu.make_async_copy(src, dst, in_sem.at[i])
        for i, (src, dst) in enumerate((
            (samples_in, samples), (pointing_in, pointing), (angles_in, angles), (counts_in, counts),
            (sky_in, sky), (prec, pp.at[:, 8:72, :]), (first_in, first), (twist_in, twist),
            (last_in, last), (onoise_in, onoise), (oprior_in, oprior), (codes_in, codes),
        ))
    ]
    for load in loads:
        load.start()

    for load in loads[:4]:
        load.wait()

    row_i = lax.broadcasted_iota(jnp.int32, (128, 128), 0)
    col_i = lax.broadcasted_iota(jnp.int32, (128, 128), 1)
    for half in range(2):
        lanes = slice(half * 128, half * 128 + 128)
        sbuf[pl.ds(half, 128, stride=8), :] = samples[:, lanes]
        sbuf[pl.ds(2 + half, 128, stride=8), :] = angles[:, lanes]
        sbuf[pl.ds(4 + half, 128, stride=8), :] = pointing[:, lanes].astype(F32)
    count_row = jnp.broadcast_to(counts[...].astype(F32), (128, 128))
    count_col = jnp.sum(jnp.where(row_i == col_i, count_row, 0.0), axis=1, keepdims=True)
    count_full = jnp.broadcast_to(count_col, (128, 128))
    sbuf[pl.ds(6, 128, stride=8), :] = count_full
    sbuf[pl.ds(7, 128, stride=8), :] = count_full

    loads[4].wait()

    for c in range(3):
        blocks = []
        for cyc in range(2):
            turned = sky[c, pl.ds(cyc, 64, stride=2), :].T
            blocks.append(jnp.concatenate([turned[:64], turned[64:]], axis=1))
        full = jnp.concatenate(blocks, axis=1)
        upper = full.astype(BF16)
        table[pl.ds(c * 64, 64), :] = upper
        table[pl.ds(192 + c * 64, 64), :] = (full - upper.astype(F32)).astype(BF16)

    bw[:, 0:8, :] = jnp.zeros((7, 8, 128), F32)
    bw[:, 72:80, :] = jnp.zeros((7, 8, 128), F32)

    @pl.when(det == 0)
    def _():
        pp[:, 0:8, :] = jnp.zeros((3, 8, 128), F32)
        edge[0] = jnp.zeros((12, 8, 128), F32)
        spec_r[0:24, :] = jnp.zeros((24, 128), F32)

    @pl.when(det == NDET - 1)
    def _():
        pp[:, 72:80, :] = jnp.zeros((3, 8, 128), F32)
        edge[1] = jnp.zeros((12, 8, 128), F32)
        spec_r[67 * 8 : 70 * 8, :] = jnp.zeros((24, 128), F32)

    loads[11].wait()
    code = codes[...]
    source = ((code & 3) + det) % 4 * 32 + (((code >> 2) & 3) + ty) % 4 * 8
    source = source + (((code >> 4) & 3) + tz) % 4 * 2 + ((code >> 6) + tc) % 2
    match_s[...] = jnp.where(source == col_i, 1.0, 0.0)
    acc[...] = jnp.zeros_like(acc)
    pl.semaphore_wait(barrier, NDEV - 1)

    for s, (x, y, z, c) in enumerate(NEAR):
        if s == 0:
            continue
        where = at_det[-x % 4]
        to = at_y[-y % 4] + at_z[-z % 4] + at_c[c]
        pltpu.make_async_remote_copy(
            sbuf.at[pl.ds((where * NTM + to) * 8, 8)], rbuf.at[s * 8 : s * 8 + 8],
            send_sem, recv_sem.at[s // GROUP], device_id=(where, to), device_id_type=MESH,
        ).start()
    rbuf[0:8, :] = sbuf[pl.ds(me * 8, 8), :]

    down = ((det + 1) % NDET, tm)
    up = ((det + NDET - 1) % NDET, tm)

    def edge_copies(rows, side, padded, to):
        pairs = (
            (prec.at[:, rows, :], pp.at[:, padded, :]),
            (onoise_in.at[:, rows, :], edge.at[side, 0:6]),
            (oprior_in.at[:, rows, :], edge.at[side, 6:12]),
        )
        return [
            pltpu.make_async_remote_copy(
                src, dst, edge_send.at[side, i], edge_recv.at[side, i], device_id=to, device_id_type=MESH
            )
            for i, (src, dst) in enumerate(pairs)
        ]

    go_down = edge_copies(slice(56, 64), 0, slice(0, 8), down)
    go_up = edge_copies(slice(0, 8), 1, slice(72, 80), up)

    @pl.when(det < NDET - 1)
    def _():
        for copy in go_down:
            copy.start()

    @pl.when(det > 0)
    def _():
        for copy in go_up:
            copy.start()

    col_index = lax.broadcasted_iota(jnp.int32, (64, 128), 0).astype(F32)

    slot_index = lax.broadcasted_iota(jnp.int32, (GROUP, 128), 1).astype(F32)

    def gather_group(group):
        base = group * GROUP
        here = pl.ds(base, GROUP)

        def row(r):
            return rbuf[pl.ds(base * 8 + r, GROUP, stride=8), :]

        for half in range(2):
            pixel = row(4 + half).astype(jnp.int32)
            upper = (pixel >> 13) * 128 + ((pixel >> 6) & 1) * 64 + ((pixel >> 7) & 63)
            hi_s[half, here, :] = upper.astype(F32)
            lo_s[half, here, :] = (pixel & 63).astype(F32)
        picked = {}
        places = {}

        def permute_rows(first_step, last_step):
            for step in range(first_step, last_step):
                half, r = divmod(step, 128)
                if r == 0:
                    pixel = rbuf[pl.ds((base + LOWER) * 8 + 4 + half, GROUP - LOWER, stride=8), :].astype(jnp.int32)
                    places[half] = (((pixel >> 7) & 63) * 2 + (pixel >> 13), pixel & 127)
                    picked[half] = [jnp.zeros((GROUP - LOWER, 128), F32) for _ in range(3)]
                in_row, at_lane = places[half]
                same = in_row == r
                for c in range(3):
                    line = jnp.broadcast_to(sky[c, r : r + 1, :], (GROUP - LOWER, 128))
                    taken = jnp.take_along_axis(line, at_lane, axis=1)
                    picked[half][c] = jnp.where(same, taken, picked[half][c])

        for u in range(LOWER):
            s = base + u
            hots = [one_hot(hi_s[half, pl.ds(s, 1), :], 256) for half in range(2)]
            got = jnp.dot(table[...], jnp.concatenate(hots, axis=1), preferred_element_type=F32)
            got = got[:192] + got[192:]
            for half in range(2):
                low = lo_s[half, pl.ds(s, 1), :]
                same = col_index == low
                for c in range(3):
                    part = got[c * 64 : c * 64 + 64, half * 128 : half * 128 + 128]
                    look[c, half, pl.ds(s, 1), :] = jnp.sum(
                        jnp.where(same, part, 0.0), axis=0, keepdims=True
                    )
            permute_rows(u * 256 // LOWER, (u + 1) * 256 // LOWER)
        for half in range(2):
            for c in range(3):
                look[c, half, pl.ds(base + LOWER, GROUP - LOWER), :] = picked[half][c]
        count = row(6)
        cross = jnp.zeros((GROUP, 128), F32)
        square = jnp.zeros((GROUP, 128), F32)
        for half in range(2):
            sine, cosine = sine_cosine(2.0 * row(2 + half))
            sin_s[half, here, :] = sine
            cos_s[half, here, :] = cosine
            signal = look[0, half, here, :] + look[1, half, here, :] * cosine + look[2, half, here, :] * sine
            look[0, half, here, :] = signal
            masked = jnp.where(slot_index + 128.0 * half < count, signal, 0.0)
            cross = cross + masked * row(half)
            square = square + masked * signal
        sums_s[0, here, :] = cross
        sums_s[1, here, :] = square

    @pl.loop(0, NGROUP)
    def _(group):
        @pl.when(group == 0)
        def _():
            span = rbuf.at[pl.ds(0, (GROUP - 1) * 8)]
            pltpu.make_async_copy(span, span, recv_sem.at[0]).wait()

        @pl.when(group > 0)
        def _():
            span = rbuf.at[pl.ds(0, GROUP * 8)]
            pltpu.make_async_copy(span, span, recv_sem.at[group]).wait()

        gather_group(group)

    match = match_s[...] > 0.5
    cross, square = (
        jnp.sum(
            jnp.where(match, jnp.sum(sums_s[k], axis=1, keepdims=True), 0.0), axis=0, keepdims=True
        )
        for k in range(2)
    )
    mine = stat_r.at[me]
    mine[...] = jnp.concatenate([cross, square], axis=0)
    to_all(
        lambda to: pltpu.make_async_remote_copy(
            mine, mine, stat_send, stat_recv, device_id=to, device_id_type=MESH
        ).start()
    )
    count = rbuf[pl.ds(6, 128, stride=8), :]
    slot = col_i.astype(F32)
    hits = [jnp.zeros((1, 128), F32) for _ in range(2)]
    for half in range(2):
        good = slot + 128.0 * half < count
        for first_w, value in ((0, rbuf[pl.ds(half, 128, stride=8), :]), (3, look[0, half])):
            value = jnp.where(good, value, 0.0)
            wsplit[first_w, half] = value
            wsplit[first_w + 1, half] = value * cos_s[half]
            wsplit[first_w + 2, half] = value * sin_s[half]
        late = jnp.where(hi_s[half] >= 128.0, 1.0, 0.0)
        valid = jnp.where(good, 1.0, 0.0)
        hits[1] = hits[1] + jnp.sum(valid * late, axis=0, keepdims=True)
        hits[0] = hits[0] + jnp.sum(valid * (1.0 - late), axis=0, keepdims=True)
    rest = stat_r.at[pl.ds(0, NDEV - 1)]
    pltpu.make_async_copy(rest, rest, stat_recv).wait()
    total = jnp.sum(stat_r[...], axis=0)
    gains = total[0:1] / (total[1:2] + 1e-06)
    lane = lax.broadcasted_iota(jnp.int32, (1, 128), 1)
    own_gain = jnp.sum(jnp.where(lane == me, gains, 0.0), axis=1, keepdims=True)
    gain_col = jnp.sum(jnp.where(match, gains, 0.0), axis=1, keepdims=True)
    gain_full = jnp.broadcast_to(gain_col, (128, 128))

    for half in range(2):
        for c in range(3):
            weight = wsplit[c, half] - gain_full * wsplit[3 + c, half]
            upper = weight.astype(BF16).astype(F32)
            wsplit[c, half] = upper
            wsplit[3 + c, half] = weight - upper

    low_index = lax.broadcasted_iota(jnp.int32, (64, 128), 0).astype(F32).astype(BF16).reshape(4, 16, 128)

    @pl.loop(0, NDEV // UNROLL)
    def _(step):
        lefts = []
        rights = []
        for u in range(UNROLL):
            s = step * UNROLL + u
            for half in range(2):
                rights.append(one_hot(hi_s[half, pl.ds(s, 1), :], 256))
                low = jnp.broadcast_to(lo_s[half, pl.ds(s, 1), :], (16, 128)).astype(BF16)
                same = low_index == low[None]
                rows = []
                for w in range(6):
                    value = jnp.broadcast_to(wsplit[w, half, pl.ds(s, 1), :], (16, 128)).astype(BF16)
                    rows.append(jnp.where(same, value[None], jnp.zeros((), BF16)).reshape(64, 128))
                lefts.append(jnp.concatenate(rows, axis=0))
        acc[...] += lax.dot_general(
            jnp.concatenate(lefts, axis=1), jnp.concatenate(rights, axis=1),
            (((1,), (1,)), ((), ())), preferred_element_type=F32,
        )

    field = acc[:192] + acc[192:]

    for load in loads[6:9]:
        load.wait()
    z_parts = []
    for cyc in range(2):
        y = dot3(split_parts(field[:, cyc * 128 : cyc * 128 + 128]), (first[0], first[1]))
        for c in range(3):
            y_re = y[c * 64 : c * 64 + 64, :128]
            y_im = y[c * 64 : c * 64 + 64, 128:]
            z_re = y_re * twist[0] + y_im * twist[1]
            z_im = y_im * twist[0] - y_re * twist[1]
            z_parts.append(jnp.concatenate([z_re, z_im], axis=0))
    x = dot3((last[0], last[1]), split_parts(jnp.concatenate(z_parts, axis=1)))
    for cyc in range(2):
        for c in range(3):
            block = x[:, (cyc * 3 + c) * 128 : (cyc * 3 + c) * 128 + 128]
            spec_s[pl.ds(cyc * 8 + 2 * c, 32, stride=16), :] = block[:32]
            spec_s[pl.ds(cyc * 8 + 2 * c + 1, 32, stride=16), :] = block[32:]
        weight = jnp.sum(hits[cyc], axis=1, keepdims=True) * (1.0 / 8192)
        for r in (6, 7):
            spec_s[pl.ds(cyc * 8 + r, 32, stride=16), :] = jnp.broadcast_to(weight, (32, 128))

    def send_spectrum(where, to, skip, tiles, slot, send, recv):
        pltpu.make_async_remote_copy(
            spec_s.at[pl.ds(to * 16 + skip * 8, tiles * 8)], spec_r.at[pl.ds(slot * 8, tiles * 8)],
            send, recv, device_id=(where, to), device_id_type=MESH,
        ).start()

    def send_rim(where, skip, tiles, slot, recv):
        send = lambda to: send_spectrum(where, to, skip, tiles, slot, rim_send, recv)
        to_tm(send)
        send(tm)

    rims = []
    for at, bound, step, skip, tiles, slot, side in (
        (0, det > 0, -1, 0, 2, 67, 1),
        (1, det > 0, -1, 0, 1, 69, 1),
        (NTM - 2, det < NDET - 1, 1, 1, 1, 0, 0),
        (NTM - 1, det < NDET - 1, 1, 0, 2, 1, 0),
    ):
        here = jnp.logical_and(tm == at, bound)
        rims.append((here, tiles))

        @pl.when(here)
        def _():
            send_rim(det + step, skip, tiles, slot, rim_recv.at[side])

    to_tm(lambda to: send_spectrum(det, to, 0, 2, 3 + 2 * tm, spec_send, spec_recv))
    spec_r[pl.ds((3 + 2 * tm) * 8, 16), :] = spec_s[pl.ds(tm * 16, 16), :]
    for c in range(3):
        for cyc in range(2):
            block = field[c * 64 : c * 64 + 64, cyc * 128 : cyc * 128 + 128]
            block = jnp.concatenate([block[:, :64], block[:, 64:]], axis=0)
            map_s[c, pl.ds(cyc, 64, stride=2), :] = block.T
    loads[5].wait()
    loads[9].wait()
    loads[10].wait()

    @pl.when(det > 0)
    def _():
        for copy in go_down:
            copy.wait_recv()

    @pl.when(det < NDET - 1)
    def _():
        for copy in go_up:
            copy.wait_recv()

    for c in range(3):
        root_s[c] = jnp.sqrt(pp[c])

    @pl.when(det > 0)
    def _():
        span = spec_r.at[pl.ds(0, 24)]
        pltpu.make_async_copy(span, span, rim_recv.at[0]).wait()

    @pl.when(det < NDET - 1)
    def _():
        span = spec_r.at[pl.ds(0, 24)]
        pltpu.make_async_copy(span, span, rim_recv.at[1]).wait()

    span = spec_r.at[pl.ds(0, (NTM - 1) * 16)]
    pltpu.make_async_copy(span, span, spec_recv).wait()

    for j in range(7):
        bw[j, 5:75, :] = spec_r[pl.ds(j, 70, stride=8), :]
    noise_root = jnp.sqrt(bw[6])
    for j in range(6):
        noise = jnp.concatenate([edge[0, j], onoise[j], edge[1, j]], axis=0)
        prior = jnp.concatenate([edge[0, 6 + j], oprior[j], edge[1, 6 + j]], axis=0)
        bw[j] = bw[j] + noise_root * noise + root_s[j // 2] * prior

    moments = [jnp.zeros((8, 128), F32) for _ in range(6)]
    for c in range(3):
        precision = pp[c]
        root = root_s[c]
        side = root * (0.45 / SCALE)
        diagonal = (precision + bw[6] - SHIFT) * (1.0 / SCALE)

        def step(v):
            u = root * v
            beside = pltpu.roll(u, 1, 0) + pltpu.roll(u, 79, 0)
            return diagonal * v - side * beside

        for p in range(2):
            j = 2 * c + p
            v0 = bw[j]
            v1 = step(v0)
            v2 = step(v1)
            v3 = step(v2)
            own = [v[8:72] for v in (v0, v1, v2, v3)]
            v1_s[j] = own[1]
            v2_s[j] = own[2]
            for m, (a, b) in enumerate(((0, 0), (0, 1), (1, 1), (1, 2), (2, 2), (2, 3))):
                moments[m] = moments[m] + jnp.sum((own[a] * own[b]).reshape(8, 8, 128), axis=0)
    message = jnp.zeros((1, 128), F32)
    for m in range(6):
        value = jnp.sum(jnp.sum(moments[m], axis=0, keepdims=True), axis=1, keepdims=True)
        message = jnp.where(lane == m, jnp.broadcast_to(value, (1, 128)), message)
    own_row = mom_r.at[me]
    own_row[...] = message
    to_all(
        lambda to: pltpu.make_async_remote_copy(
            own_row, own_row, mom_send, mom_recv, device_id=to, device_id_type=MESH
        ).start()
    )
    rest = mom_r.at[pl.ds(0, NDEV - 1)]
    pltpu.make_async_copy(rest, rest, mom_recv).wait()
    sums = jnp.sum(mom_r[...], axis=0)
    nu = [jnp.sum(jnp.where(lane == m, sums, 0.0), axis=1, keepdims=True) for m in range(6)]

    zero = jnp.zeros((1, 1), F32)

    def inner(a, b):
        terms = {}
        for i, x_i in enumerate(a):
            for j, y_j in enumerate(b):
                terms[i + j] = terms.get(i + j, zero) + x_i * y_j
        out = zero
        for power, value in terms.items():
            out = out + value * nu[power]
        return out

    def image_of(a):
        longer = list(a) + [zero]
        return [SHIFT * longer[i] + (SCALE * longer[i - 1] if i else zero) for i in range(len(longer))]

    resid = [zero + 1.0]
    direction = [zero + 1.0]
    answer = [zero, zero, zero]
    norm_now = nu[0]
    for iteration in range(3):
        image = image_of(direction)
        alpha = norm_now / inner(direction, image)
        alpha = jnp.minimum(jnp.maximum(alpha, 0.0), STEP_MAX)
        for i, value in enumerate(direction):
            answer[i] = answer[i] + alpha * value
        if iteration < 2:
            resid = resid + [zero]
            resid = [r - alpha * w for r, w in zip(resid, image)]
            norm_next = jnp.maximum(inner(resid, resid), 0.0)
            beta = norm_next / norm_now
            direction = [r + beta * d for r, d in zip(resid, direction + [zero])]
            norm_now = norm_next
    small_out[...] = jnp.broadcast_to(own_gain, (8, 128))
    for j in range(6):
        sol_out[j] = answer[0] * bw[j, 8:72, :] + answer[1] * v1_s[j] + answer[2] * v2_s[j]

    span = sbuf.at[pl.ds(0, (NDEV - 1) * 8)]
    pltpu.make_async_copy(span, span, send_sem).wait()
    rest = stat_r.at[pl.ds(0, NDEV - 1)]
    pltpu.make_async_copy(rest, rest, stat_send).wait()
    span = spec_s.at[pl.ds(0, (NTM - 1) * 16)]
    pltpu.make_async_copy(span, span, spec_send).wait()
    rest = mom_r.at[pl.ds(0, NDEV - 1)]
    pltpu.make_async_copy(rest, rest, mom_send).wait()

    for here, tiles in rims:
        @pl.when(here)
        def _():
            span = spec_s.at[pl.ds(0, NTM * tiles * 8)]
            pltpu.make_async_copy(span, span, rim_send).wait()

    @pl.when(det < NDET - 1)
    def _():
        for copy in go_down:
            copy.wait_send()

    @pl.when(det > 0)
    def _():
        for copy in go_up:
            copy.wait_send()


def finish(small, map_in, sol_in, gain_out, map_out, sol_out, gain, out_sem):
    gain[...] = small[0:1, 0:1]
    stores = [
        pltpu.make_async_copy(sol_in, sol_out, out_sem.at[0]),
        pltpu.make_async_copy(map_in, map_out, out_sem.at[1]),
        pltpu.make_async_copy(gain, gain_out, out_sem.at[2]),
    ]
    for store in stores:
        store.start()
    for store in stores:
        store.wait()


def per_device(
    samples, pointing, angles, counts, sky_map, prior_precision, omega_noise, omega_prior
):
    sky = sky_map.reshape(3, 2, 64, 128).transpose(0, 2, 1, 3).reshape(3, 128, 128)
    vmem = pl.BlockSpec(memory_space=pltpu.VMEM)
    dma = pltpu.SemaphoreType.DMA
    anywhere = pl.BlockSpec(memory_space=pl.ANY)
    small, binned, solved = pl.pallas_call(
        kernel,
        name="gibbs_step",
        out_shape=(
            pltpu.VMEM((8, 128), F32),
            pltpu.VMEM((3, 128, 128), F32),
            pltpu.VMEM((6, 64, 128), F32),
        ),
        in_specs=[anywhere] * 12,
        out_specs=(vmem, vmem, vmem),
        scratch_shapes=[
            pltpu.VMEM((128, 256), F32),
            pltpu.VMEM((128, 256), jnp.int32),
            pltpu.VMEM((128, 256), F32),
            pltpu.VMEM((1, 128), jnp.int32),
            pltpu.VMEM((3, 128, 128), F32),
            pltpu.VMEM((6, 64, 128), F32),
            pltpu.VMEM((6, 64, 128), F32),
            pltpu.VMEM((2, 128, 256), BF16),
            pltpu.VMEM((2, 64, 128), F32),
            pltpu.VMEM((2, 64, 128), BF16),
            pltpu.VMEM((NDEV, 128), jnp.int32),
            pltpu.VMEM((NDEV, 128), F32),
            pltpu.VMEM((1024, 128), F32),
            pltpu.VMEM((1024, 128), F32),
            pltpu.VMEM((384, 256), BF16),
            pltpu.VMEM((2, 128, 128), F32),
            pltpu.VMEM((2, 128, 128), F32),
            pltpu.VMEM((2, 128, 128), F32),
            pltpu.VMEM((2, 128, 128), F32),
            pltpu.VMEM((3, 2, 128, 128), F32),
            pltpu.VMEM((2, 128, 128), F32),
            pltpu.VMEM((6, 2, 128, 128), F32),
            pltpu.VMEM((384, 256), F32),
            pltpu.VMEM((NDEV, 2, 128), F32),
            pltpu.VMEM((NTM * 16, 128), F32),
            pltpu.VMEM((70 * 8, 128), F32),
            pltpu.VMEM((3, 80, 128), F32),
            pltpu.VMEM((3, 80, 128), F32),
            pltpu.VMEM((2, 12, 8, 128), F32),
            pltpu.VMEM((7, 80, 128), F32),
            pltpu.VMEM((6, 64, 128), F32),
            pltpu.VMEM((6, 64, 128), F32),
            pltpu.VMEM((NDEV, 1, 128), F32),
            dma, dma((NGROUP,)), dma, dma, dma, dma,
            dma, dma((2,)), dma((2, 3)), dma((2, 3)), dma, dma,
            dma((12,)),
        ],
        compiler_params=pltpu.CompilerParams(collective_id=0, has_side_effects=True),
    )(
        samples.reshape(128, 256),
        pointing.reshape(128, 256),
        angles.reshape(128, 256),
        counts.reshape(1, 128),
        sky,
        prior_precision,
        omega_noise,
        omega_prior,
        *(jnp.asarray(t) for t in tables()),
    )
    gain, binned, solved = pl.pallas_call(
        finish,
        name="finish",
        out_shape=(
            jax.ShapeDtypeStruct((1, 1), F32),
            jax.ShapeDtypeStruct((3, 128, 128), F32),
            jax.ShapeDtypeStruct((6, 64, 128), F32),
        ),
        in_specs=[vmem, vmem, vmem],
        out_specs=(anywhere, anywhere, anywhere),
        scratch_shapes=[pltpu.VMEM((1, 1), F32), dma((3,))],
    )(*(pltpu.with_memory_space_constraint(x, pltpu.VMEM) for x in (small, binned, solved)))
    binned = binned.reshape(3, 64, 2, 128).transpose(0, 2, 1, 3).reshape(3, 2, 8192)
    return (gain, binned, solved)


def solution(mesh):
    return jax.shard_map(
        per_device,
        mesh=mesh,
        in_specs=(
            P("det", "tm", None, None),
            P("det", "tm", None, None),
            P("det", "tm", None, None),
            P("det", "tm", None),
            P(None, ("det", "tm"), None),
            P(None, "det", "tm"),
            P(None, "det", "tm"),
            P(None, "det", "tm"),
        ),
        out_specs=(P("det", "tm"), P(None, ("det", "tm"), None), P(None, "det", "tm")),
        check_vma=False,
    )
```

```python
import math

import jax
import jax.numpy as jnp
import numpy as np
from jax import lax
from jax.experimental import pallas as pl
from jax.experimental.pallas import tpu as pltpu
from jax.sharding import PartitionSpec as P

MESH = pl.DeviceIdType.MESH
F32 = jnp.float32
BF16 = jnp.bfloat16
NDET = 4
NTM = 32
NDEV = NDET * NTM
GROUP = 16
NGROUP = NDEV // GROUP
LOWER = 12
UNROLL = 64
SHIFT = 4.0
SCALE = 4.0
STEP_MAX = 20.0


def near_first():
    ring = (0, 1, 2, 1)
    return sorted(
        ((x, y, z, c) for x in range(4) for y in range(4) for z in range(4) for c in range(2)),
        key=lambda o: 4 * (ring[o[0]] + ring[o[1]] + ring[o[2]]) + o[3],
    )


NEAR = near_first()


def tables():
    h, i = np.divmod(np.arange(128), 64)
    a = 2 * i + h
    k = np.arange(128)
    ang = 2.0 * np.pi * (np.outer(a, k) % 128) / 128
    first = np.concatenate([np.cos(ang), -np.sin(ang)], axis=1)
    b = np.arange(64)
    ang = 2.0 * np.pi * np.outer(b, k) / 8192
    twist = np.stack([np.cos(ang), np.sin(ang)])
    q = np.arange(32)
    ang = 2.0 * np.pi * (np.outer(q, b) % 64) / 64
    c, s = np.cos(ang), np.sin(ang)
    last = np.concatenate([np.concatenate([c, s], axis=1), np.concatenate([-s, c], axis=1)], axis=0)
    last = last / math.sqrt(8192)
    def split(x):
        upper = x.astype(np.float32).astype(jnp.bfloat16)
        return np.stack([upper, (x - upper.astype(np.float64)).astype(jnp.bfloat16)])

    codes = np.asarray([o[0] + 4 * o[1] + 16 * o[2] + 64 * o[3] for o in NEAR], np.int32)
    codes = np.ascontiguousarray(np.broadcast_to(codes[:, None], (NDEV, 128)))
    return [split(first), twist.astype(np.float32), split(last), codes]


def split_parts(x):
    upper = x.astype(BF16)
    return upper, (x - upper.astype(F32)).astype(BF16)


def dot3(a, b):
    out = jnp.dot(a[0], b[0], preferred_element_type=F32)
    out = out + jnp.dot(a[0], b[1], preferred_element_type=F32)
    return out + jnp.dot(a[1], b[0], preferred_element_type=F32)


def sine_cosine(x):
    k = jnp.floor(x * (2.0 / math.pi) + 0.5)
    r = ((x - k * 1.5703125) - k * 4.837512969970703125e-4) - k * 7.549789948768648e-8
    z = r * r
    sine = r + r * z * (-1.6666654611e-1 + z * (8.3321608736e-3 - z * 1.9515295891e-4))
    cosine = 1.0 - 0.5 * z + z * z * (
        4.166664568298827e-2 + z * (-1.388731625493765e-3 + z * 2.443315711809948e-5)
    )
    q = k.astype(jnp.int32) & 3
    odd = (q & 1) == 1
    s = jnp.where(odd, cosine, sine)
    c = jnp.where(odd, sine, cosine)
    s = jnp.where(q >= 2, -s, s)
    c = jnp.where((q == 1) | (q == 2), -c, c)
    return s, c


def one_hot(row, rows):
    value = jnp.broadcast_to(row, (16, 128)).astype(BF16)
    index = lax.broadcasted_iota(jnp.int32, (rows, 128), 0).astype(F32).astype(BF16)
    same = index.reshape(rows // 16, 16, 128) == value[None]
    return jnp.where(same, jnp.ones((), BF16), jnp.zeros((), BF16)).reshape(rows, 128)


def kernel(
    samples_in, pointing_in, angles_in, counts_in, sky_in, prec, onoise_in, oprior_in,
    first_in, twist_in, last_in, codes_in,
    small_out, map_s, sol_out,
    samples, pointing, angles, counts, sky, onoise, oprior, first, twist, last, codes, match_s,
    sbuf, rbuf, table, hi_s, lo_s, cos_s, sin_s, look, sums_s, wsplit, acc,
    stat_r, spec_s, spec_r, pp, root_s, edge, bw, v1_s, v2_s, mom_r,
    send_sem, recv_sem, stat_send, stat_recv, spec_send, spec_recv,
    rim_send, rim_recv, edge_send, edge_recv, mom_send, mom_recv, in_sem,
):
    det = lax.axis_index("det")
    tm = lax.axis_index("tm")
    me = det * NTM + tm

    ty, tz, tc = tm // 8, (tm // 2) % 4, tm % 2
    at_z = [(tz + o) % 4 * 2 for o in range(4)]
    at_c = [tc, 1 - tc]
    at_y = [(ty + o) % 4 * 8 for o in range(4)]
    at_det = [(det + o) % NDET for o in range(NDET)]

    def to_tm(act):
        def row(y, own):
            for z in (2, 1, 3, 0):
                for c in (1, 0):
                    if not (own and z == 0 and c == 0):
                        act(y * 8 + at_z[z] + at_c[c])

        @pl.loop(0, 3)
        def _(d):
            row((ty + jnp.where(d == 0, 2, jnp.where(d == 1, 1, 3))) % 4, False)

        row(ty, True)

    def to_all(act):
        to_tm(lambda to: [act((at_det[x], to)) for x in (2, 1, 3, 0)])
        for x in (2, 1, 3):
            act((at_det[x], tm))

    barrier = pltpu.get_barrier_semaphore()
    to_all(lambda to: pl.semaphore_signal(barrier, inc=1, device_id=to, device_id_type=MESH))

    loads = [
        pltpu.make_async_copy(src, dst, in_sem.at[i])
        for i, (src, dst) in enumerate((
            (samples_in, samples), (pointing_in, pointing), (angles_in, angles), (counts_in, counts),
            (sky_in, sky), (prec, pp.at[:, 8:72, :]), (first_in, first), (twist_in, twist),
            (last_in, last), (onoise_in, onoise), (oprior_in, oprior), (codes_in, codes),
        ))
    ]
    for load in loads:
        load.start()

    for load in loads[:4]:
        load.wait()

    row_i = lax.broadcasted_iota(jnp.int32, (128, 128), 0)
    col_i = lax.broadcasted_iota(jnp.int32, (128, 128), 1)
    for half in range(2):
        lanes = slice(half * 128, half * 128 + 128)
        sbuf[pl.ds(half, 128, stride=8), :] = samples[:, lanes]
        sbuf[pl.ds(2 + half, 128, stride=8), :] = angles[:, lanes]
        sbuf[pl.ds(4 + half, 128, stride=8), :] = pointing[:, lanes].astype(F32)
    count_row = jnp.broadcast_to(counts[...].astype(F32), (128, 128))
    count_col = jnp.sum(jnp.where(row_i == col_i, count_row, 0.0), axis=1, keepdims=True)
    count_full = jnp.broadcast_to(count_col, (128, 128))
    sbuf[pl.ds(6, 128, stride=8), :] = count_full
    sbuf[pl.ds(7, 128, stride=8), :] = count_full

    loads[4].wait()

    for c in range(3):
        blocks = []
        for cyc in range(2):
            turned = sky[c, pl.ds(cyc, 64, stride=2), :].T
            blocks.append(jnp.concatenate([turned[:64], turned[64:]], axis=1))
        full = jnp.concatenate(blocks, axis=1)
        upper = full.astype(BF16)
        table[pl.ds(c * 64, 64), :] = upper
        table[pl.ds(192 + c * 64, 64), :] = (full - upper.astype(F32)).astype(BF16)

    bw[:, 0:8, :] = jnp.zeros((7, 8, 128), F32)
    bw[:, 72:80, :] = jnp.zeros((7, 8, 128), F32)

    @pl.when(det == 0)
    def _():
        pp[:, 0:8, :] = jnp.zeros((3, 8, 128), F32)
        edge[0] = jnp.zeros((12, 8, 128), F32)
        spec_r[0:24, :] = jnp.zeros((24, 128), F32)

    @pl.when(det == NDET - 1)
    def _():
        pp[:, 72:80, :] = jnp.zeros((3, 8, 128), F32)
        edge[1] = jnp.zeros((12, 8, 128), F32)
        spec_r[67 * 8 : 70 * 8, :] = jnp.zeros((24, 128), F32)

    loads[11].wait()
    code = codes[...]
    source = ((code & 3) + det) % 4 * 32 + (((code >> 2) & 3) + ty) % 4 * 8
    source = source + (((code >> 4) & 3) + tz) % 4 * 2 + ((code >> 6) + tc) % 2
    match_s[...] = jnp.where(source == col_i, 1.0, 0.0)
    acc[...] = jnp.zeros_like(acc)
    pl.semaphore_wait(barrier, NDEV - 1)

    for s, (x, y, z, c) in enumerate(NEAR):
        if s == 0:
            continue
        where = at_det[-x % 4]
        to = at_y[-y % 4] + at_z[-z % 4] + at_c[c]
        pltpu.make_async_remote_copy(
            sbuf.at[pl.ds((where * NTM + to) * 8, 8)], rbuf.at[s * 8 : s * 8 + 8],
            send_sem, recv_sem.at[s // GROUP], device_id=(where, to), device_id_type=MESH,
        ).start()
    rbuf[0:8, :] = sbuf[pl.ds(me * 8, 8), :]

    down = ((det + 1) % NDET, tm)
    up = ((det + NDET - 1) % NDET, tm)

    def edge_copies(rows, side, padded, to):
        pairs = (
            (prec.at[:, rows, :], pp.at[:, padded, :]),
            (onoise_in.at[:, rows, :], edge.at[side, 0:6]),
            (oprior_in.at[:, rows, :], edge.at[side, 6:12]),
        )
        return [
            pltpu.make_async_remote_copy(
                src, dst, edge_send.at[side, i], edge_recv.at[side, i], device_id=to, device_id_type=MESH
            )
            for i, (src, dst) in enumerate(pairs)
        ]

    go_down = edge_copies(slice(56, 64), 0, slice(0, 8), down)
    go_up = edge_copies(slice(0, 8), 1, slice(72, 80), up)

    @pl.when(det < NDET - 1)
    def _():
        for copy in go_down:
            copy.start()

    @pl.when(det > 0)
    def _():
        for copy in go_up:
            copy.start()

    col_index = lax.broadcasted_iota(jnp.int32, (64, 128), 0).astype(F32)

    slot_index = lax.broadcasted_iota(jnp.int32, (GROUP, 128), 1).astype(F32)

    def gather_group(group):
        base = group * GROUP
        here = pl.ds(base, GROUP)

        def row(r):
            return rbuf[pl.ds(base * 8 + r, GROUP, stride=8), :]

        for half in range(2):
            pixel = row(4 + half).astype(jnp.int32)
            upper = (pixel >> 13) * 128 + ((pixel >> 6) & 1) * 64 + ((pixel >> 7) & 63)
            hi_s[half, here, :] = upper.astype(F32)
            lo_s[half, here, :] = (pixel & 63).astype(F32)
        pixel = jnp.concatenate(
            [rbuf[pl.ds((base + LOWER) * 8 + 4 + half, GROUP - LOWER, stride=8), :] for half in range(2)], axis=0
        ).astype(jnp.int32)
        in_row, at_lane = ((pixel >> 7) & 63) * 2 + (pixel >> 13), pixel & 127
        picked = [jnp.zeros((8, 128), F32) for _ in range(3)]

        def permute_rows(first_r, last_r):
            for r in range(first_r, last_r):
                same = in_row == r
                for c in range(3):
                    line = jnp.broadcast_to(sky[c, r : r + 1, :], (8, 128))
                    taken = jnp.take_along_axis(line, at_lane, axis=1)
                    picked[c] = jnp.where(same, taken, picked[c])

        for u in range(LOWER):
            s = base + u
            hots = [one_hot(hi_s[half, pl.ds(s, 1), :], 256) for half in range(2)]
            got = jnp.dot(table[...], jnp.concatenate(hots, axis=1), preferred_element_type=F32)
            got = got[:192] + got[192:]
            for half in range(2):
                low = lo_s[half, pl.ds(s, 1), :]
                same = col_index == low
                for c in range(3):
                    part = got[c * 64 : c * 64 + 64, half * 128 : half * 128 + 128]
                    look[c, half, pl.ds(s, 1), :] = jnp.sum(
                        jnp.where(same, part, 0.0), axis=0, keepdims=True
                    )
            permute_rows(u * 128 // LOWER, (u + 1) * 128 // LOWER)
        for half in range(2):
            for c in range(3):
                look[c, half, pl.ds(base + LOWER, GROUP - LOWER), :] = picked[c][half * 4 : half * 4 + 4]
        count = row(6)
        cross = jnp.zeros((GROUP, 128), F32)
        square = jnp.zeros((GROUP, 128), F32)
        for half in range(2):
            sine, cosine = sine_cosine(2.0 * row(2 + half))
            sin_s[half, here, :] = sine
            cos_s[half, here, :] = cosine
            signal = look[0, half, here, :] + look[1, half, here, :] * cosine + look[2, half, here, :] * sine
            look[0, half, here, :] = signal
            masked = jnp.where(slot_index + 128.0 * half < count, signal, 0.0)
            cross = cross + masked * row(half)
            square = square + masked * signal
        sums_s[0, here, :] = cross
        sums_s[1, here, :] = square

    @pl.loop(0, NGROUP)
    def _(group):
        @pl.when(group == 0)
        def _():
            span = rbuf.at[pl.ds(0, (GROUP - 1) * 8)]
            pltpu.make_async_copy(span, span, recv_sem.at[0]).wait()

        @pl.when(group > 0)
        def _():
            span = rbuf.at[pl.ds(0, GROUP * 8)]
            pltpu.make_async_copy(span, span, recv_sem.at[group]).wait()

        gather_group(group)

    match = match_s[...] > 0.5
    cross, square = (
        jnp.sum(
            jnp.where(match, jnp.sum(sums_s[k], axis=1, keepdims=True), 0.0), axis=0, keepdims=True
        )
        for k in range(2)
    )
    mine = stat_r.at[me]
    mine[...] = jnp.concatenate([cross, square], axis=0)
    to_all(
        lambda to: pltpu.make_async_remote_copy(
            mine, mine, stat_send, stat_recv, device_id=to, device_id_type=MESH
        ).start()
    )
    count = rbuf[pl.ds(6, 128, stride=8), :]
    slot = col_i.astype(F32)
    hits = [jnp.zeros((1, 128), F32) for _ in range(2)]
    for half in range(2):
        good = slot + 128.0 * half < count
        for first_w, value in ((0, rbuf[pl.ds(half, 128, stride=8), :]), (3, look[0, half])):
            value = jnp.where(good, value, 0.0)
            wsplit[first_w, half] = value
            wsplit[first_w + 1, half] = value * cos_s[half]
            wsplit[first_w + 2, half] = value * sin_s[half]
        late = jnp.where(hi_s[half] >= 128.0, 1.0, 0.0)
        valid = jnp.where(good, 1.0, 0.0)
        hits[1] = hits[1] + jnp.sum(valid * late, axis=0, keepdims=True)
        hits[0] = hits[0] + jnp.sum(valid * (1.0 - late), axis=0, keepdims=True)
    rest = stat_r.at[pl.ds(0, NDEV - 1)]
    pltpu.make_async_copy(rest, rest, stat_recv).wait()
    total = jnp.sum(stat_r[...], axis=0)
    gains = total[0:1] / (total[1:2] + 1e-06)
    lane = lax.broadcasted_iota(jnp.int32, (1, 128), 1)
    own_gain = jnp.sum(jnp.where(lane == me, gains, 0.0), axis=1, keepdims=True)
    gain_col = jnp.sum(jnp.where(match, gains, 0.0), axis=1, keepdims=True)
    gain_full = jnp.broadcast_to(gain_col, (128, 128))

    for half in range(2):
        for c in range(3):
            weight = wsplit[c, half] - gain_full * wsplit[3 + c, half]
            upper = weight.astype(BF16).astype(F32)
            wsplit[c, half] = upper
            wsplit[3 + c, half] = weight - upper

    low_index = lax.broadcasted_iota(jnp.int32, (64, 128), 0).astype(F32).astype(BF16).reshape(4, 16, 128)

    @pl.loop(0, NDEV // UNROLL)
    def _(step):
        lefts = []
        rights = []
        for u in range(UNROLL):
            s = step * UNROLL + u
            for half in range(2):
                rights.append(one_hot(hi_s[half, pl.ds(s, 1), :], 256))
                low = jnp.broadcast_to(lo_s[half, pl.ds(s, 1), :], (16, 128)).astype(BF16)
                same = low_index == low[None]
                rows = []
                for w in range(6):
                    value = jnp.broadcast_to(wsplit[w, half, pl.ds(s, 1), :], (16, 128)).astype(BF16)
                    rows.append(jnp.where(same, value[None], jnp.zeros((), BF16)).reshape(64, 128))
                lefts.append(jnp.concatenate(rows, axis=0))
        acc[...] += lax.dot_general(
            jnp.concatenate(lefts, axis=1), jnp.concatenate(rights, axis=1),
            (((1,), (1,)), ((), ())), preferred_element_type=F32,
        )

    field = acc[:192] + acc[192:]

    for load in loads[6:9]:
        load.wait()
    z_parts = []
    for cyc in range(2):
        y = dot3(split_parts(field[:, cyc * 128 : cyc * 128 + 128]), (first[0], first[1]))
        for c in range(3):
            y_re = y[c * 64 : c * 64 + 64, :128]
            y_im = y[c * 64 : c * 64 + 64, 128:]
            z_re = y_re * twist[0] + y_im * twist[1]
            z_im = y_im * twist[0] - y_re * twist[1]
            z_parts.append(jnp.concatenate([z_re, z_im], axis=0))
    x = dot3((last[0], last[1]), split_parts(jnp.concatenate(z_parts, axis=1)))
    for cyc in range(2):
        for c in range(3):
            block = x[:, (cyc * 3 + c) * 128 : (cyc * 3 + c) * 128 + 128]
            spec_s[pl.ds(cyc * 8 + 2 * c, 32, stride=16), :] = block[:32]
            spec_s[pl.ds(cyc * 8 + 2 * c + 1, 32, stride=16), :] = block[32:]
        weight = jnp.sum(hits[cyc], axis=1, keepdims=True) * (1.0 / 8192)
        for r in (6, 7):
            spec_s[pl.ds(cyc * 8 + r, 32, stride=16), :] = jnp.broadcast_to(weight, (32, 128))

    def send_spectrum(where, to, skip, tiles, slot, send, recv):
        pltpu.make_async_remote_copy(
            spec_s.at[pl.ds(to * 16 + skip * 8, tiles * 8)], spec_r.at[pl.ds(slot * 8, tiles * 8)],
            send, recv, device_id=(where, to), device_id_type=MESH,
        ).start()

    def send_rim(where, skip, tiles, slot, recv):
        send = lambda to: send_spectrum(where, to, skip, tiles, slot, rim_send, recv)
        to_tm(send)
        send(tm)

    rims = []
    for at, bound, step, skip, tiles, slot, side in (
        (0, det > 0, -1, 0, 2, 67, 1),
        (1, det > 0, -1, 0, 1, 69, 1),
        (NTM - 2, det < NDET - 1, 1, 1, 1, 0, 0),
        (NTM - 1, det < NDET - 1, 1, 0, 2, 1, 0),
    ):
        here = jnp.logical_and(tm == at, bound)
        rims.append((here, tiles))

        @pl.when(here)
        def _():
            send_rim(det + step, skip, tiles, slot, rim_recv.at[side])

    to_tm(lambda to: send_spectrum(det, to, 0, 2, 3 + 2 * tm, spec_send, spec_recv))
    spec_r[pl.ds((3 + 2 * tm) * 8, 16), :] = spec_s[pl.ds(tm * 16, 16), :]
    for c in range(3):
        for cyc in range(2):
            block = field[c * 64 : c * 64 + 64, cyc * 128 : cyc * 128 + 128]
            block = jnp.concatenate([block[:, :64], block[:, 64:]], axis=0)
            map_s[c, pl.ds(cyc, 64, stride=2), :] = block.T
    loads[5].wait()
    loads[9].wait()
    loads[10].wait()

    @pl.when(det > 0)
    def _():
        for copy in go_down:
            copy.wait_recv()

    @pl.when(det < NDET - 1)
    def _():
        for copy in go_up:
            copy.wait_recv()

    for c in range(3):
        root_s[c] = jnp.sqrt(pp[c])

    @pl.when(det > 0)
    def _():
        span = spec_r.at[pl.ds(0, 24)]
        pltpu.make_async_copy(span, span, rim_recv.at[0]).wait()

    @pl.when(det < NDET - 1)
    def _():
        span = spec_r.at[pl.ds(0, 24)]
        pltpu.make_async_copy(span, span, rim_recv.at[1]).wait()

    span = spec_r.at[pl.ds(0, (NTM - 1) * 16)]
    pltpu.make_async_copy(span, span, spec_recv).wait()

    for j in range(7):
        bw[j, 5:75, :] = spec_r[pl.ds(j, 70, stride=8), :]
    noise_root = jnp.sqrt(bw[6])
    for j in range(6):
        noise = jnp.concatenate([edge[0, j], onoise[j], edge[1, j]], axis=0)
        prior = jnp.concatenate([edge[0, 6 + j], oprior[j], edge[1, 6 + j]], axis=0)
        bw[j] = bw[j] + noise_root * noise + root_s[j // 2] * prior

    moments = [jnp.zeros((8, 128), F32) for _ in range(6)]
    for c in range(3):
        precision = pp[c]
        root = root_s[c]
        side = root * (0.45 / SCALE)
        diagonal = (precision + bw[6] - SHIFT) * (1.0 / SCALE)

        def step(v):
            u = root * v
            beside = pltpu.roll(u, 1, 0) + pltpu.roll(u, 79, 0)
            return diagonal * v - side * beside

        for p in range(2):
            j = 2 * c + p
            v0 = bw[j]
            v1 = step(v0)
            v2 = step(v1)
            v3 = step(v2)
            own = [v[8:72] for v in (v0, v1, v2, v3)]
            v1_s[j] = own[1]
            v2_s[j] = own[2]
            for m, (a, b) in enumerate(((0, 0), (0, 1), (1, 1), (1, 2), (2, 2), (2, 3))):
                moments[m] = moments[m] + jnp.sum((own[a] * own[b]).reshape(8, 8, 128), axis=0)
    message = jnp.zeros((1, 128), F32)
    for m in range(6):
        value = jnp.sum(jnp.sum(moments[m], axis=0, keepdims=True), axis=1, keepdims=True)
        message = jnp.where(lane == m, jnp.broadcast_to(value, (1, 128)), message)
    own_row = mom_r.at[me]
    own_row[...] = message
    to_all(
        lambda to: pltpu.make_async_remote_copy(
            own_row, own_row, mom_send, mom_recv, device_id=to, device_id_type=MESH
        ).start()
    )
    rest = mom_r.at[pl.ds(0, NDEV - 1)]
    pltpu.make_async_copy(rest, rest, mom_recv).wait()
    sums = jnp.sum(mom_r[...], axis=0)
    nu = [jnp.sum(jnp.where(lane == m, sums, 0.0), axis=1, keepdims=True) for m in range(6)]

    zero = jnp.zeros((1, 1), F32)

    def inner(a, b):
        terms = {}
        for i, x_i in enumerate(a):
            for j, y_j in enumerate(b):
                terms[i + j] = terms.get(i + j, zero) + x_i * y_j
        out = zero
        for power, value in terms.items():
            out = out + value * nu[power]
        return out

    def image_of(a):
        longer = list(a) + [zero]
        return [SHIFT * longer[i] + (SCALE * longer[i - 1] if i else zero) for i in range(len(longer))]

    resid = [zero + 1.0]
    direction = [zero + 1.0]
    answer = [zero, zero, zero]
    norm_now = nu[0]
    for iteration in range(3):
        image = image_of(direction)
        alpha = norm_now / inner(direction, image)
        alpha = jnp.minimum(jnp.maximum(alpha, 0.0), STEP_MAX)
        for i, value in enumerate(direction):
            answer[i] = answer[i] + alpha * value
        if iteration < 2:
            resid = resid + [zero]
            resid = [r - alpha * w for r, w in zip(resid, image)]
            norm_next = jnp.maximum(inner(resid, resid), 0.0)
            beta = norm_next / norm_now
            direction = [r + beta * d for r, d in zip(resid, direction + [zero])]
            norm_now = norm_next
    small_out[...] = jnp.broadcast_to(own_gain, (8, 128))
    for j in range(6):
        sol_out[j] = answer[0] * bw[j, 8:72, :] + answer[1] * v1_s[j] + answer[2] * v2_s[j]

    span = sbuf.at[pl.ds(0, (NDEV - 1) * 8)]
    pltpu.make_async_copy(span, span, send_sem).wait()
    rest = stat_r.at[pl.ds(0, NDEV - 1)]
    pltpu.make_async_copy(rest, rest, stat_send).wait()
    span = spec_s.at[pl.ds(0, (NTM - 1) * 16)]
    pltpu.make_async_copy(span, span, spec_send).wait()
    rest = mom_r.at[pl.ds(0, NDEV - 1)]
    pltpu.make_async_copy(rest, rest, mom_send).wait()

    for here, tiles in rims:
        @pl.when(here)
        def _():
            span = spec_s.at[pl.ds(0, NTM * tiles * 8)]
            pltpu.make_async_copy(span, span, rim_send).wait()

    @pl.when(det < NDET - 1)
    def _():
        for copy in go_down:
            copy.wait_send()

    @pl.when(det > 0)
    def _():
        for copy in go_up:
            copy.wait_send()


def finish(small, map_in, sol_in, gain_out, map_out, sol_out, gain, out_sem):
    gain[...] = small[0:1, 0:1]
    stores = [
        pltpu.make_async_copy(sol_in, sol_out, out_sem.at[0]),
        pltpu.make_async_copy(map_in, map_out, out_sem.at[1]),
        pltpu.make_async_copy(gain, gain_out, out_sem.at[2]),
    ]
    for store in stores:
        store.start()
    for store in stores:
        store.wait()


def per_device(
    samples, pointing, angles, counts, sky_map, prior_precision, omega_noise, omega_prior
):
    sky = sky_map.reshape(3, 2, 64, 128).transpose(0, 2, 1, 3).reshape(3, 128, 128)
    vmem = pl.BlockSpec(memory_space=pltpu.VMEM)
    dma = pltpu.SemaphoreType.DMA
    anywhere = pl.BlockSpec(memory_space=pl.ANY)
    small, binned, solved = pl.pallas_call(
        kernel,
        name="gibbs_step",
        out_shape=(
            pltpu.VMEM((8, 128), F32),
            pltpu.VMEM((3, 128, 128), F32),
            pltpu.VMEM((6, 64, 128), F32),
        ),
        in_specs=[anywhere] * 12,
        out_specs=(vmem, vmem, vmem),
        scratch_shapes=[
            pltpu.VMEM((128, 256), F32),
            pltpu.VMEM((128, 256), jnp.int32),
            pltpu.VMEM((128, 256), F32),
            pltpu.VMEM((1, 128), jnp.int32),
            pltpu.VMEM((3, 128, 128), F32),
            pltpu.VMEM((6, 64, 128), F32),
            pltpu.VMEM((6, 64, 128), F32),
            pltpu.VMEM((2, 128, 256), BF16),
            pltpu.VMEM((2, 64, 128), F32),
            pltpu.VMEM((2, 64, 128), BF16),
            pltpu.VMEM((NDEV, 128), jnp.int32),
            pltpu.VMEM((NDEV, 128), F32),
            pltpu.VMEM((1024, 128), F32),
            pltpu.VMEM((1024, 128), F32),
            pltpu.VMEM((384, 256), BF16),
            pltpu.VMEM((2, 128, 128), F32),
            pltpu.VMEM((2, 128, 128), F32),
            pltpu.VMEM((2, 128, 128), F32),
            pltpu.VMEM((2, 128, 128), F32),
            pltpu.VMEM((3, 2, 128, 128), F32),
            pltpu.VMEM((2, 128, 128), F32),
            pltpu.VMEM((6, 2, 128, 128), F32),
            pltpu.VMEM((384, 256), F32),
            pltpu.VMEM((NDEV, 2, 128), F32),
            pltpu.VMEM((NTM * 16, 128), F32),
            pltpu.VMEM((70 * 8, 128), F32),
            pltpu.VMEM((3, 80, 128), F32),
            pltpu.VMEM((3, 80, 128), F32),
            pltpu.VMEM((2, 12, 8, 128), F32),
            pltpu.VMEM((7, 80, 128), F32),
            pltpu.VMEM((6, 64, 128), F32),
            pltpu.VMEM((6, 64, 128), F32),
            pltpu.VMEM((NDEV, 1, 128), F32),
            dma, dma((NGROUP,)), dma, dma, dma, dma,
            dma, dma((2,)), dma((2, 3)), dma((2, 3)), dma, dma,
            dma((12,)),
        ],
        compiler_params=pltpu.CompilerParams(collective_id=0, has_side_effects=True),
    )(
        samples.reshape(128, 256),
        pointing.reshape(128, 256),
        angles.reshape(128, 256),
        counts.reshape(1, 128),
        sky,
        prior_precision,
        omega_noise,
        omega_prior,
        *(jnp.asarray(t) for t in tables()),
    )
    gain, binned, solved = pl.pallas_call(
        finish,
        name="finish",
        out_shape=(
            jax.ShapeDtypeStruct((1, 1), F32),
            jax.ShapeDtypeStruct((3, 128, 128), F32),
            jax.ShapeDtypeStruct((6, 64, 128), F32),
        ),
        in_specs=[vmem, vmem, vmem],
        out_specs=(anywhere, anywhere, anywhere),
        scratch_shapes=[pltpu.VMEM((1, 1), F32), dma((3,))],
    )(*(pltpu.with_memory_space_constraint(x, pltpu.VMEM) for x in (small, binned, solved)))
    binned = binned.reshape(3, 64, 2, 128).transpose(0, 2, 1, 3).reshape(3, 2, 8192)
    return (gain, binned, solved)


def solution(mesh):
    return jax.shard_map(
        per_device,
        mesh=mesh,
        in_specs=(
            P("det", "tm", None, None),
            P("det", "tm", None, None),
            P("det", "tm", None, None),
            P("det", "tm", None),
            P(None, ("det", "tm"), None),
            P(None, "det", "tm"),
            P(None, "det", "tm"),
            P(None, "det", "tm"),
        ),
        out_specs=(P("det", "tm"), P(None, ("det", "tm"), None), P(None, "det", "tm")),
        check_vma=False,
    )
```

```python
import math

import jax
import jax.numpy as jnp
import numpy as np
from jax import lax
from jax.experimental import pallas as pl
from jax.experimental.pallas import tpu as pltpu
from jax.sharding import PartitionSpec as P

MESH = pl.DeviceIdType.MESH
F32 = jnp.float32
BF16 = jnp.bfloat16
NDET = 4
NTM = 32
NDEV = NDET * NTM
GROUP = 16
NGROUP = NDEV // GROUP
LOWER = 12
UNROLL = 64
SHIFT = 4.0
SCALE = 4.0
STEP_MAX = 20.0


def near_first():
    ring = (0, 1, 2, 1)
    return sorted(
        ((x, y, z, c) for x in range(4) for y in range(4) for z in range(4) for c in range(2)),
        key=lambda o: 4 * (ring[o[0]] + ring[o[1]] + ring[o[2]]) + o[3],
    )


NEAR = near_first()


def tables():
    h, i = np.divmod(np.arange(128), 64)
    a = 2 * i + h
    k = np.arange(128)
    ang = 2.0 * np.pi * (np.outer(a, k) % 128) / 128
    first = np.concatenate([np.cos(ang), -np.sin(ang)], axis=1)
    b = np.arange(64)
    ang = 2.0 * np.pi * np.outer(b, k) / 8192
    twist = np.stack([np.cos(ang), np.sin(ang)])
    q = np.arange(32)
    ang = 2.0 * np.pi * (np.outer(q, b) % 64) / 64
    c, s = np.cos(ang), np.sin(ang)
    last = np.concatenate([np.concatenate([c, s], axis=1), np.concatenate([-s, c], axis=1)], axis=0)
    last = last / math.sqrt(8192)
    def split(x):
        upper = x.astype(np.float32).astype(jnp.bfloat16)
        return np.stack([upper, (x - upper.astype(np.float64)).astype(jnp.bfloat16)])

    codes = np.asarray([o[0] + 4 * o[1] + 16 * o[2] + 64 * o[3] for o in NEAR], np.int32)
    codes = np.ascontiguousarray(np.broadcast_to(codes[:, None], (NDEV, 128)))
    return [split(first), twist.astype(np.float32), split(last), codes]


def split_parts(x):
    upper = x.astype(BF16)
    return upper, (x - upper.astype(F32)).astype(BF16)


def dot3(a, b):
    out = jnp.dot(a[0], b[0], preferred_element_type=F32)
    out = out + jnp.dot(a[0], b[1], preferred_element_type=F32)
    return out + jnp.dot(a[1], b[0], preferred_element_type=F32)


def sine_cosine(x):
    k = jnp.floor(x * (2.0 / math.pi) + 0.5)
    r = ((x - k * 1.5703125) - k * 4.837512969970703125e-4) - k * 7.549789948768648e-8
    z = r * r
    sine = r + r * z * (-1.6666654611e-1 + z * (8.3321608736e-3 - z * 1.9515295891e-4))
    cosine = 1.0 - 0.5 * z + z * z * (
        4.166664568298827e-2 + z * (-1.388731625493765e-3 + z * 2.443315711809948e-5)
    )
    q = k.astype(jnp.int32) & 3
    odd = (q & 1) == 1
    s = jnp.where(odd, cosine, sine)
    c = jnp.where(odd, sine, cosine)
    s = jnp.where(q >= 2, -s, s)
    c = jnp.where((q == 1) | (q == 2), -c, c)
    return s, c


def one_hot(row, rows):
    value = jnp.broadcast_to(row, (16, 128)).astype(BF16)
    index = lax.broadcasted_iota(jnp.int32, (rows, 128), 0).astype(F32).astype(BF16)
    same = index.reshape(rows // 16, 16, 128) == value[None]
    return jnp.where(same, jnp.ones((), BF16), jnp.zeros((), BF16)).reshape(rows, 128)


def kernel(
    samples_in, pointing_in, angles_in, counts_in, sky_in, prec, onoise_in, oprior_in,
    first_in, twist_in, last_in, codes_in,
    small_out, map_s, sol_out,
    samples, pointing, angles, counts, sky, onoise, oprior, first, twist, last, codes, match_s,
    sbuf, rbuf, table, hi_s, lo_s, cos_s, sin_s, look, sums_s, wsplit, acc,
    stat_r, spec_s, spec_r, pp, root_s, edge, bw, v1_s, v2_s, mom_r,
    send_sem, recv_sem, stat_send, stat_recv, spec_send, spec_recv,
    rim_send, rim_recv, edge_send, edge_recv, mom_send, mom_recv, in_sem,
):
    det = lax.axis_index("det")
    tm = lax.axis_index("tm")
    me = det * NTM + tm

    ty, tz, tc = tm // 8, (tm // 2) % 4, tm % 2
    at_z = [(tz + o) % 4 * 2 for o in range(4)]
    at_c = [tc, 1 - tc]
    at_y = [(ty + o) % 4 * 8 for o in range(4)]
    at_det = [(det + o) % NDET for o in range(NDET)]

    def to_tm(act):
        def row(y, own):
            for z in (2, 1, 3, 0):
                for c in (1, 0):
                    if not (own and z == 0 and c == 0):
                        act(y * 8 + at_z[z] + at_c[c])

        @pl.loop(0, 3)
        def _(d):
            row((ty + jnp.where(d == 0, 2, jnp.where(d == 1, 1, 3))) % 4, False)

        row(ty, True)

    def to_all(act):
        to_tm(lambda to: [act((at_det[x], to)) for x in (2, 1, 3, 0)])
        for x in (2, 1, 3):
            act((at_det[x], tm))

    barrier = pltpu.get_barrier_semaphore()
    to_all(lambda to: pl.semaphore_signal(barrier, inc=1, device_id=to, device_id_type=MESH))

    loads = [
        pltpu.make_async_copy(src, dst, in_sem.at[i])
        for i, (src, dst) in enumerate((
            (samples_in, samples), (pointing_in, pointing), (angles_in, angles), (counts_in, counts),
            (sky_in, sky), (prec, pp.at[:, 8:72, :]), (first_in, first), (twist_in, twist),
            (last_in, last), (onoise_in, onoise), (oprior_in, oprior), (codes_in, codes),
        ))
    ]
    for load in loads:
        load.start()

    for load in loads[:4]:
        load.wait()

    row_i = lax.broadcasted_iota(jnp.int32, (128, 128), 0)
    col_i = lax.broadcasted_iota(jnp.int32, (128, 128), 1)
    for half in range(2):
        lanes = slice(half * 128, half * 128 + 128)
        sbuf[pl.ds(half, 128, stride=8), :] = samples[:, lanes]
        sbuf[pl.ds(2 + half, 128, stride=8), :] = angles[:, lanes]
        sbuf[pl.ds(4 + half, 128, stride=8), :] = pointing[:, lanes].astype(F32)
    count_row = jnp.broadcast_to(counts[...].astype(F32), (128, 128))
    count_col = jnp.sum(jnp.where(row_i == col_i, count_row, 0.0), axis=1, keepdims=True)
    count_full = jnp.broadcast_to(count_col, (128, 128))
    sbuf[pl.ds(6, 128, stride=8), :] = count_full
    sbuf[pl.ds(7, 128, stride=8), :] = count_full

    loads[4].wait()

    for c in range(3):
        blocks = []
        for cyc in range(2):
            turned = sky[c, pl.ds(cyc, 64, stride=2), :].T
            blocks.append(jnp.concatenate([turned[:64], turned[64:]], axis=1))
        full = jnp.concatenate(blocks, axis=1)
        upper = full.astype(BF16)
        table[pl.ds(c * 64, 64), :] = upper
        table[pl.ds(192 + c * 64, 64), :] = (full - upper.astype(F32)).astype(BF16)

    bw[:, 0:8, :] = jnp.zeros((7, 8, 128), F32)
    bw[:, 72:80, :] = jnp.zeros((7, 8, 128), F32)

    @pl.when(det == 0)
    def _():
        pp[:, 0:8, :] = jnp.zeros((3, 8, 128), F32)
        edge[0] = jnp.zeros((12, 8, 128), F32)
        spec_r[0:24, :] = jnp.zeros((24, 128), F32)

    @pl.when(det == NDET - 1)
    def _():
        pp[:, 72:80, :] = jnp.zeros((3, 8, 128), F32)
        edge[1] = jnp.zeros((12, 8, 128), F32)
        spec_r[67 * 8 : 70 * 8, :] = jnp.zeros((24, 128), F32)

    loads[11].wait()
    code = codes[...]
    source = ((code & 3) + det) % 4 * 32 + (((code >> 2) & 3) + ty) % 4 * 8
    source = source + (((code >> 4) & 3) + tz) % 4 * 2 + ((code >> 6) + tc) % 2
    match_s[...] = jnp.where(source == col_i, 1.0, 0.0)
    acc[...] = jnp.zeros_like(acc)
    pl.semaphore_wait(barrier, NDEV - 1)

    for s, (x, y, z, c) in enumerate(NEAR):
        if s == 0:
            continue
        where = at_det[-x % 4]
        to = at_y[-y % 4] + at_z[-z % 4] + at_c[c]
        pltpu.make_async_remote_copy(
            sbuf.at[pl.ds((where * NTM + to) * 8, 8)], rbuf.at[s * 8 : s * 8 + 8],
            send_sem, recv_sem.at[s // GROUP], device_id=(where, to), device_id_type=MESH,
        ).start()
    rbuf[0:8, :] = sbuf[pl.ds(me * 8, 8), :]

    down = ((det + 1) % NDET, tm)
    up = ((det + NDET - 1) % NDET, tm)

    def edge_copies(rows, side, padded, to):
        pairs = (
            (prec.at[:, rows, :], pp.at[:, padded, :]),
            (onoise_in.at[:, rows, :], edge.at[side, 0:6]),
            (oprior_in.at[:, rows, :], edge.at[side, 6:12]),
        )
        return [
            pltpu.make_async_remote_copy(
                src, dst, edge_send.at[side, i], edge_recv.at[side, i], device_id=to, device_id_type=MESH
            )
            for i, (src, dst) in enumerate(pairs)
        ]

    go_down = edge_copies(slice(56, 64), 0, slice(0, 8), down)
    go_up = edge_copies(slice(0, 8), 1, slice(72, 80), up)

    @pl.when(det < NDET - 1)
    def _():
        for copy in go_down:
            copy.start()

    @pl.when(det > 0)
    def _():
        for copy in go_up:
            copy.start()

    col_index = lax.broadcasted_iota(jnp.int32, (64, 128), 0).astype(F32)

    slot_index = lax.broadcasted_iota(jnp.int32, (GROUP, 128), 1).astype(F32)

    def gather_group(group):
        base = group * GROUP
        here = pl.ds(base, GROUP)

        def row(r):
            return rbuf[pl.ds(base * 8 + r, GROUP, stride=8), :]

        for half in range(2):
            pixel = row(4 + half).astype(jnp.int32)
            upper = (pixel >> 13) * 128 + ((pixel >> 6) & 1) * 64 + ((pixel >> 7) & 63)
            hi_s[half, here, :] = upper.astype(F32)
            lo_s[half, here, :] = (pixel & 63).astype(F32)
        pixel = jnp.concatenate(
            [rbuf[pl.ds((base + LOWER) * 8 + 4 + half, GROUP - LOWER, stride=8), :] for half in range(2)], axis=0
        ).astype(jnp.int32)
        in_row, at_lane = ((pixel >> 7) & 63) * 2 + (pixel >> 13), pixel & 127
        picked = [jnp.zeros((8, 128), F32) for _ in range(3)]

        def permute_rows(first_r, last_r):
            for r in range(first_r, last_r):
                same = in_row == r
                for c in range(3):
                    line = jnp.broadcast_to(sky[c, r : r + 1, :], (8, 128))
                    taken = jnp.take_along_axis(line, at_lane, axis=1)
                    picked[c] = jnp.where(same, taken, picked[c])

        for u in range(LOWER):
            s = base + u
            hots = [one_hot(hi_s[half, pl.ds(s, 1), :], 256) for half in range(2)]
            got = jnp.dot(table[...], jnp.concatenate(hots, axis=1), preferred_element_type=F32)
            got = got[:192] + got[192:]
            for half in range(2):
                low = lo_s[half, pl.ds(s, 1), :]
                same = col_index == low
                for c in range(3):
                    part = got[c * 64 : c * 64 + 64, half * 128 : half * 128 + 128]
                    look[c, half, pl.ds(s, 1), :] = jnp.sum(
                        jnp.where(same, part, 0.0), axis=0, keepdims=True
                    )
            permute_rows(u * 128 // LOWER, (u + 1) * 128 // LOWER)
        for half in range(2):
            for c in range(3):
                look[c, half, pl.ds(base + LOWER, GROUP - LOWER), :] = picked[c][half * 4 : half * 4 + 4]
        count = row(6)
        cross = jnp.zeros((GROUP, 128), F32)
        square = jnp.zeros((GROUP, 128), F32)
        for half in range(2):
            sine, cosine = sine_cosine(2.0 * row(2 + half))
            sin_s[half, here, :] = sine
            cos_s[half, here, :] = cosine
            signal = look[0, half, here, :] + look[1, half, here, :] * cosine + look[2, half, here, :] * sine
            look[0, half, here, :] = signal
            masked = jnp.where(slot_index + 128.0 * half < count, signal, 0.0)
            cross = cross + masked * row(half)
            square = square + masked * signal
        sums_s[0, here, :] = cross
        sums_s[1, here, :] = square

    @pl.loop(0, NGROUP)
    def _(group):
        @pl.when(group == 0)
        def _():
            span = rbuf.at[pl.ds(0, (GROUP - 1) * 8)]
            pltpu.make_async_copy(span, span, recv_sem.at[0]).wait()

        @pl.when(group > 0)
        def _():
            span = rbuf.at[pl.ds(0, GROUP * 8)]
            pltpu.make_async_copy(span, span, recv_sem.at[group]).wait()

        gather_group(group)

    match = match_s[...] > 0.5
    cross, square = (
        jnp.sum(
            jnp.where(match, jnp.sum(sums_s[k], axis=1, keepdims=True), 0.0), axis=0, keepdims=True
        )
        for k in range(2)
    )
    mine = stat_r.at[me // 4, pl.ds(me % 4 * 2, 2), :]
    mine[...] = jnp.concatenate([cross, square], axis=0)
    to_all(
        lambda to: pltpu.make_async_remote_copy(
            mine, mine, stat_send, stat_recv, device_id=to, device_id_type=MESH
        ).start()
    )
    count = rbuf[pl.ds(6, 128, stride=8), :]
    slot = col_i.astype(F32)
    hits = [jnp.zeros((1, 128), F32) for _ in range(2)]
    for half in range(2):
        good = slot + 128.0 * half < count
        for first_w, value in ((0, rbuf[pl.ds(half, 128, stride=8), :]), (3, look[0, half])):
            value = jnp.where(good, value, 0.0)
            wsplit[first_w, half] = value
            wsplit[first_w + 1, half] = value * cos_s[half]
            wsplit[first_w + 2, half] = value * sin_s[half]
        late = jnp.where(hi_s[half] >= 128.0, 1.0, 0.0)
        valid = jnp.where(good, 1.0, 0.0)
        hits[1] = hits[1] + jnp.sum(valid * late, axis=0, keepdims=True)
        hits[0] = hits[0] + jnp.sum(valid * (1.0 - late), axis=0, keepdims=True)
    rest = sbuf.at[pl.ds(0, 2 * (NDEV - 1))]
    pltpu.make_async_copy(rest, rest, stat_recv).wait()
    total = jnp.sum(stat_r[...], axis=0)
    total = total[0:2] + total[2:4] + total[4:6] + total[6:8]
    gains = total[0:1] / (total[1:2] + 1e-06)
    lane = lax.broadcasted_iota(jnp.int32, (1, 128), 1)
    own_gain = jnp.sum(jnp.where(lane == me, gains, 0.0), axis=1, keepdims=True)
    gain_col = jnp.sum(jnp.where(match, gains, 0.0), axis=1, keepdims=True)
    gain_full = jnp.broadcast_to(gain_col, (128, 128))

    for half in range(2):
        for c in range(3):
            weight = wsplit[c, half] - gain_full * wsplit[3 + c, half]
            upper = weight.astype(BF16).astype(F32)
            wsplit[c, half] = upper
            wsplit[3 + c, half] = weight - upper

    low_index = lax.broadcasted_iota(jnp.int32, (64, 128), 0).astype(F32).astype(BF16).reshape(4, 16, 128)

    @pl.loop(0, NDEV // UNROLL)
    def _(step):
        lefts = []
        rights = []
        for u in range(UNROLL):
            s = step * UNROLL + u
            for half in range(2):
                rights.append(one_hot(hi_s[half, pl.ds(s, 1), :], 256))
                low = jnp.broadcast_to(lo_s[half, pl.ds(s, 1), :], (16, 128)).astype(BF16)
                same = low_index == low[None]
                rows = []
                for w in range(6):
                    value = jnp.broadcast_to(wsplit[w, half, pl.ds(s, 1), :], (16, 128)).astype(BF16)
                    rows.append(jnp.where(same, value[None], jnp.zeros((), BF16)).reshape(64, 128))
                lefts.append(jnp.concatenate(rows, axis=0))
        acc[...] += lax.dot_general(
            jnp.concatenate(lefts, axis=1), jnp.concatenate(rights, axis=1),
            (((1,), (1,)), ((), ())), preferred_element_type=F32,
        )

    field = acc[:192] + acc[192:]

    for load in loads[6:9]:
        load.wait()
    z_parts = []
    for cyc in range(2):
        y = dot3(split_parts(field[:, cyc * 128 : cyc * 128 + 128]), (first[0], first[1]))
        for c in range(3):
            y_re = y[c * 64 : c * 64 + 64, :128]
            y_im = y[c * 64 : c * 64 + 64, 128:]
            z_re = y_re * twist[0] + y_im * twist[1]
            z_im = y_im * twist[0] - y_re * twist[1]
            z_parts.append(jnp.concatenate([z_re, z_im], axis=0))
    x = dot3((last[0], last[1]), split_parts(jnp.concatenate(z_parts, axis=1)))
    for cyc in range(2):
        for c in range(3):
            block = x[:, (cyc * 3 + c) * 128 : (cyc * 3 + c) * 128 + 128]
            spec_s[pl.ds(cyc * 8 + 2 * c, 32, stride=16), :] = block[:32]
            spec_s[pl.ds(cyc * 8 + 2 * c + 1, 32, stride=16), :] = block[32:]
        weight = jnp.sum(hits[cyc], axis=1, keepdims=True) * (1.0 / 8192)
        for r in (6, 7):
            spec_s[pl.ds(cyc * 8 + r, 32, stride=16), :] = jnp.broadcast_to(weight, (32, 128))

    def send_spectrum(where, to, skip, tiles, slot, send, recv):
        pltpu.make_async_remote_copy(
            spec_s.at[pl.ds(to * 16 + skip * 8, tiles * 8)], spec_r.at[pl.ds(slot * 8, tiles * 8)],
            send, recv, device_id=(where, to), device_id_type=MESH,
        ).start()

    def send_rim(where, skip, tiles, slot, recv):
        send = lambda to: send_spectrum(where, to, skip, tiles, slot, rim_send, recv)
        to_tm(send)
        send(tm)

    rims = []
    for at, bound, step, skip, tiles, slot, side in (
        (0, det > 0, -1, 0, 2, 67, 1),
        (1, det > 0, -1, 0, 1, 69, 1),
        (NTM - 2, det < NDET - 1, 1, 1, 1, 0, 0),
        (NTM - 1, det < NDET - 1, 1, 0, 2, 1, 0),
    ):
        here = jnp.logical_and(tm == at, bound)
        rims.append((here, tiles))

        @pl.when(here)
        def _():
            send_rim(det + step, skip, tiles, slot, rim_recv.at[side])

    to_tm(lambda to: send_spectrum(det, to, 0, 2, 3 + 2 * tm, spec_send, spec_recv))
    spec_r[pl.ds((3 + 2 * tm) * 8, 16), :] = spec_s[pl.ds(tm * 16, 16), :]
    for c in range(3):
        for cyc in range(2):
            block = field[c * 64 : c * 64 + 64, cyc * 128 : cyc * 128 + 128]
            block = jnp.concatenate([block[:, :64], block[:, 64:]], axis=0)
            map_s[c, pl.ds(cyc, 64, stride=2), :] = block.T
    loads[5].wait()
    loads[9].wait()
    loads[10].wait()

    @pl.when(det > 0)
    def _():
        for copy in go_down:
            copy.wait_recv()

    @pl.when(det < NDET - 1)
    def _():
        for copy in go_up:
            copy.wait_recv()

    for c in range(3):
        root_s[c] = jnp.sqrt(pp[c])

    @pl.when(det > 0)
    def _():
        span = spec_r.at[pl.ds(0, 24)]
        pltpu.make_async_copy(span, span, rim_recv.at[0]).wait()

    @pl.when(det < NDET - 1)
    def _():
        span = spec_r.at[pl.ds(0, 24)]
        pltpu.make_async_copy(span, span, rim_recv.at[1]).wait()

    span = spec_r.at[pl.ds(0, (NTM - 1) * 16)]
    pltpu.make_async_copy(span, span, spec_recv).wait()

    for j in range(7):
        bw[j, 5:75, :] = spec_r[pl.ds(j, 70, stride=8), :]
    noise_root = jnp.sqrt(bw[6])
    for j in range(6):
        noise = jnp.concatenate([edge[0, j], onoise[j], edge[1, j]], axis=0)
        prior = jnp.concatenate([edge[0, 6 + j], oprior[j], edge[1, 6 + j]], axis=0)
        bw[j] = bw[j] + noise_root * noise + root_s[j // 2] * prior

    moments = [jnp.zeros((8, 128), F32) for _ in range(6)]
    for c in range(3):
        precision = pp[c]
        root = root_s[c]
        side = root * (0.45 / SCALE)
        diagonal = (precision + bw[6] - SHIFT) * (1.0 / SCALE)

        def step(v):
            u = root * v
            beside = pltpu.roll(u, 1, 0) + pltpu.roll(u, 79, 0)
            return diagonal * v - side * beside

        for p in range(2):
            j = 2 * c + p
            v0 = bw[j]
            v1 = step(v0)
            v2 = step(v1)
            v3 = step(v2)
            own = [v[8:72] for v in (v0, v1, v2, v3)]
            v1_s[j] = own[1]
            v2_s[j] = own[2]
            for m, (a, b) in enumerate(((0, 0), (0, 1), (1, 1), (1, 2), (2, 2), (2, 3))):
                moments[m] = moments[m] + jnp.sum((own[a] * own[b]).reshape(8, 8, 128), axis=0)
    message = jnp.zeros((1, 128), F32)
    for m in range(6):
        value = jnp.sum(jnp.sum(moments[m], axis=0, keepdims=True), axis=1, keepdims=True)
        message = jnp.where(lane == m, jnp.broadcast_to(value, (1, 128)), message)
    own_row = mom_r.at[me // 8, pl.ds(me % 8, 1), :]
    own_row[...] = message
    to_all(
        lambda to: pltpu.make_async_remote_copy(
            own_row, own_row, mom_send, mom_recv, device_id=to, device_id_type=MESH
        ).start()
    )
    rest = sbuf.at[pl.ds(0, NDEV - 1)]
    pltpu.make_async_copy(rest, rest, mom_recv).wait()
    sums = jnp.sum(jnp.sum(mom_r[...], axis=0), axis=0, keepdims=True)
    nu = [jnp.sum(jnp.where(lane == m, sums, 0.0), axis=1, keepdims=True) for m in range(6)]

    zero = jnp.zeros((1, 1), F32)

    def inner(a, b):
        terms = {}
        for i, x_i in enumerate(a):
            for j, y_j in enumerate(b):
                terms[i + j] = terms.get(i + j, zero) + x_i * y_j
        out = zero
        for power, value in terms.items():
            out = out + value * nu[power]
        return out

    def image_of(a):
        longer = list(a) + [zero]
        return [SHIFT * longer[i] + (SCALE * longer[i - 1] if i else zero) for i in range(len(longer))]

    resid = [zero + 1.0]
    direction = [zero + 1.0]
    answer = [zero, zero, zero]
    norm_now = nu[0]
    for iteration in range(3):
        image = image_of(direction)
        alpha = norm_now / inner(direction, image)
        alpha = jnp.minimum(jnp.maximum(alpha, 0.0), STEP_MAX)
        for i, value in enumerate(direction):
            answer[i] = answer[i] + alpha * value
        if iteration < 2:
            resid = resid + [zero]
            resid = [r - alpha * w for r, w in zip(resid, image)]
            norm_next = jnp.maximum(inner(resid, resid), 0.0)
            beta = norm_next / norm_now
            direction = [r + beta * d for r, d in zip(resid, direction + [zero])]
            norm_now = norm_next
    small_out[...] = jnp.broadcast_to(own_gain, (8, 128))
    for j in range(6):
        sol_out[j] = answer[0] * bw[j, 8:72, :] + answer[1] * v1_s[j] + answer[2] * v2_s[j]

    span = sbuf.at[pl.ds(0, (NDEV - 1) * 8)]
    pltpu.make_async_copy(span, span, send_sem).wait()
    rest = sbuf.at[pl.ds(0, 2 * (NDEV - 1))]
    pltpu.make_async_copy(rest, rest, stat_send).wait()
    span = spec_s.at[pl.ds(0, (NTM - 1) * 16)]
    pltpu.make_async_copy(span, span, spec_send).wait()
    rest = sbuf.at[pl.ds(0, NDEV - 1)]
    pltpu.make_async_copy(rest, rest, mom_send).wait()

    for here, tiles in rims:
        @pl.when(here)
        def _():
            span = spec_s.at[pl.ds(0, NTM * tiles * 8)]
            pltpu.make_async_copy(span, span, rim_send).wait()

    @pl.when(det < NDET - 1)
    def _():
        for copy in go_down:
            copy.wait_send()

    @pl.when(det > 0)
    def _():
        for copy in go_up:
            copy.wait_send()


def finish(small, map_in, sol_in, gain_out, map_out, sol_out, gain, out_sem):
    gain[...] = small[0:1, 0:1]
    stores = [
        pltpu.make_async_copy(sol_in, sol_out, out_sem.at[0]),
        pltpu.make_async_copy(map_in, map_out, out_sem.at[1]),
        pltpu.make_async_copy(gain, gain_out, out_sem.at[2]),
    ]
    for store in stores:
        store.start()
    for store in stores:
        store.wait()


def per_device(
    samples, pointing, angles, counts, sky_map, prior_precision, omega_noise, omega_prior
):
    sky = sky_map.reshape(3, 2, 64, 128).transpose(0, 2, 1, 3).reshape(3, 128, 128)
    vmem = pl.BlockSpec(memory_space=pltpu.VMEM)
    dma = pltpu.SemaphoreType.DMA
    anywhere = pl.BlockSpec(memory_space=pl.ANY)
    small, binned, solved = pl.pallas_call(
        kernel,
        name="gibbs_step",
        out_shape=(
            pltpu.VMEM((8, 128), F32),
            pltpu.VMEM((3, 128, 128), F32),
            pltpu.VMEM((6, 64, 128), F32),
        ),
        in_specs=[anywhere] * 12,
        out_specs=(vmem, vmem, vmem),
        scratch_shapes=[
            pltpu.VMEM((128, 256), F32),
            pltpu.VMEM((128, 256), jnp.int32),
            pltpu.VMEM((128, 256), F32),
            pltpu.VMEM((1, 128), jnp.int32),
            pltpu.VMEM((3, 128, 128), F32),
            pltpu.VMEM((6, 64, 128), F32),
            pltpu.VMEM((6, 64, 128), F32),
            pltpu.VMEM((2, 128, 256), BF16),
            pltpu.VMEM((2, 64, 128), F32),
            pltpu.VMEM((2, 64, 128), BF16),
            pltpu.VMEM((NDEV, 128), jnp.int32),
            pltpu.VMEM((NDEV, 128), F32),
            pltpu.VMEM((1024, 128), F32),
            pltpu.VMEM((1024, 128), F32),
            pltpu.VMEM((384, 256), BF16),
            pltpu.VMEM((2, 128, 128), F32),
            pltpu.VMEM((2, 128, 128), F32),
            pltpu.VMEM((2, 128, 128), F32),
            pltpu.VMEM((2, 128, 128), F32),
            pltpu.VMEM((3, 2, 128, 128), F32),
            pltpu.VMEM((2, 128, 128), F32),
            pltpu.VMEM((6, 2, 128, 128), F32),
            pltpu.VMEM((384, 256), F32),
            pltpu.VMEM((NDEV // 4, 8, 128), F32),
            pltpu.VMEM((NTM * 16, 128), F32),
            pltpu.VMEM((70 * 8, 128), F32),
            pltpu.VMEM((3, 80, 128), F32),
            pltpu.VMEM((3, 80, 128), F32),
            pltpu.VMEM((2, 12, 8, 128), F32),
            pltpu.VMEM((7, 80, 128), F32),
            pltpu.VMEM((6, 64, 128), F32),
            pltpu.VMEM((6, 64, 128), F32),
            pltpu.VMEM((NDEV // 8, 8, 128), F32),
            dma, dma((NGROUP,)), dma, dma, dma, dma,
            dma, dma((2,)), dma((2, 3)), dma((2, 3)), dma, dma,
            dma((12,)),
        ],
        compiler_params=pltpu.CompilerParams(collective_id=0, has_side_effects=True),
    )(
        samples.reshape(128, 256),
        pointing.reshape(128, 256),
        angles.reshape(128, 256),
        counts.reshape(1, 128),
        sky,
        prior_precision,
        omega_noise,
        omega_prior,
        *(jnp.asarray(t) for t in tables()),
    )
    gain, binned, solved = pl.pallas_call(
        finish,
        name="finish",
        out_shape=(
            jax.ShapeDtypeStruct((1, 1), F32),
            jax.ShapeDtypeStruct((3, 128, 128), F32),
            jax.ShapeDtypeStruct((6, 64, 128), F32),
        ),
        in_specs=[vmem, vmem, vmem],
        out_specs=(anywhere, anywhere, anywhere),
        scratch_shapes=[pltpu.VMEM((1, 1), F32), dma((3,))],
    )(*(pltpu.with_memory_space_constraint(x, pltpu.VMEM) for x in (small, binned, solved)))
    binned = binned.reshape(3, 64, 2, 128).transpose(0, 2, 1, 3).reshape(3, 2, 8192)
    return (gain, binned, solved)


def solution(mesh):
    return jax.shard_map(
        per_device,
        mesh=mesh,
        in_specs=(
            P("det", "tm", None, None),
            P("det", "tm", None, None),
            P("det", "tm", None, None),
            P("det", "tm", None),
            P(None, ("det", "tm"), None),
            P(None, "det", "tm"),
            P(None, "det", "tm"),
            P(None, "det", "tm"),
        ),
        out_specs=(P("det", "tm"), P(None, ("det", "tm"), None), P(None, "det", "tm")),
        check_vma=False,
    )
```

```python
import math

import jax
import jax.numpy as jnp
import numpy as np
from jax import lax
from jax.experimental import pallas as pl
from jax.experimental.pallas import tpu as pltpu
from jax.sharding import PartitionSpec as P

MESH = pl.DeviceIdType.MESH
F32 = jnp.float32
BF16 = jnp.bfloat16
NDET = 4
NTM = 32
NDEV = NDET * NTM
GROUP = 16
NGROUP = NDEV // GROUP
LOWER = 12
UNROLL = 128
SHIFT = 4.0
SCALE = 4.0
STEP_MAX = 20.0


def near_first():
    ring = (0, 1, 2, 1)
    return sorted(
        ((x, y, z, c) for x in range(4) for y in range(4) for z in range(4) for c in range(2)),
        key=lambda o: 4 * (ring[o[0]] + ring[o[1]] + ring[o[2]]) + o[3],
    )


NEAR = near_first()


def tables():
    h, i = np.divmod(np.arange(128), 64)
    a = 2 * i + h
    k = np.arange(128)
    ang = 2.0 * np.pi * (np.outer(a, k) % 128) / 128
    first = np.concatenate([np.cos(ang), -np.sin(ang)], axis=1)
    b = np.arange(64)
    ang = 2.0 * np.pi * np.outer(b, k) / 8192
    twist = np.stack([np.cos(ang), np.sin(ang)])
    q = np.arange(32)
    ang = 2.0 * np.pi * (np.outer(q, b) % 64) / 64
    c, s = np.cos(ang), np.sin(ang)
    last = np.concatenate([np.concatenate([c, s], axis=1), np.concatenate([-s, c], axis=1)], axis=0)
    last = last / math.sqrt(8192)
    def split(x):
        upper = x.astype(np.float32).astype(jnp.bfloat16)
        return np.stack([upper, (x - upper.astype(np.float64)).astype(jnp.bfloat16)])

    codes = np.asarray([o[0] + 4 * o[1] + 16 * o[2] + 64 * o[3] for o in NEAR], np.int32)
    codes = np.ascontiguousarray(np.broadcast_to(codes[:, None], (NDEV, 128)))
    return [split(first), twist.astype(np.float32), split(last), codes]


def split_parts(x):
    upper = x.astype(BF16)
    return upper, (x - upper.astype(F32)).astype(BF16)


def dot3(a, b):
    out = jnp.dot(a[0], b[0], preferred_element_type=F32)
    out = out + jnp.dot(a[0], b[1], preferred_element_type=F32)
    return out + jnp.dot(a[1], b[0], preferred_element_type=F32)


def sine_cosine(x):
    k = jnp.floor(x * (2.0 / math.pi) + 0.5)
    r = ((x - k * 1.5703125) - k * 4.837512969970703125e-4) - k * 7.549789948768648e-8
    z = r * r
    sine = r + r * z * (-1.6666654611e-1 + z * (8.3321608736e-3 - z * 1.9515295891e-4))
    cosine = 1.0 - 0.5 * z + z * z * (
        4.166664568298827e-2 + z * (-1.388731625493765e-3 + z * 2.443315711809948e-5)
    )
    q = k.astype(jnp.int32) & 3
    odd = (q & 1) == 1
    s = jnp.where(odd, cosine, sine)
    c = jnp.where(odd, sine, cosine)
    s = jnp.where(q >= 2, -s, s)
    c = jnp.where((q == 1) | (q == 2), -c, c)
    return s, c


def one_hot(row, rows):
    value = jnp.broadcast_to(row, (16, 128)).astype(BF16)
    index = lax.broadcasted_iota(jnp.int32, (rows, 128), 0).astype(F32).astype(BF16)
    same = index.reshape(rows // 16, 16, 128) == value[None]
    return jnp.where(same, jnp.ones((), BF16), jnp.zeros((), BF16)).reshape(rows, 128)


def kernel(
    samples_in, pointing_in, angles_in, counts_in, sky_in, prec, onoise_in, oprior_in,
    first_in, twist_in, last_in, codes_in,
    small_out, map_s, sol_out,
    samples, pointing, angles, counts, sky, onoise, oprior, first, twist, last, codes, match_s,
    sbuf, rbuf, table, hi_s, lo_s, cos_s, sin_s, look, sums_s, wsplit, acc,
    stat_r, spec_s, spec_r, pp, root_s, edge, bw, v1_s, v2_s, mom_r,
    send_sem, recv_sem, stat_send, stat_recv, spec_send, spec_recv,
    rim_send, rim_recv, edge_send, edge_recv, mom_send, mom_recv, in_sem,
):
    det = lax.axis_index("det")
    tm = lax.axis_index("tm")
    me = det * NTM + tm

    ty, tz, tc = tm // 8, (tm // 2) % 4, tm % 2
    at_z = [(tz + o) % 4 * 2 for o in range(4)]
    at_c = [tc, 1 - tc]
    at_y = [(ty + o) % 4 * 8 for o in range(4)]
    at_det = [(det + o) % NDET for o in range(NDET)]

    def to_tm(act):
        def row(y, own):
            for z in (2, 1, 3, 0):
                for c in (1, 0):
                    if not (own and z == 0 and c == 0):
                        act(y * 8 + at_z[z] + at_c[c])

        @pl.loop(0, 3)
        def _(d):
            row((ty + jnp.where(d == 0, 2, jnp.where(d == 1, 1, 3))) % 4, False)

        row(ty, True)

    def to_all(act):
        to_tm(lambda to: [act((at_det[x], to)) for x in (2, 1, 3, 0)])
        for x in (2, 1, 3):
            act((at_det[x], tm))

    barrier = pltpu.get_barrier_semaphore()
    to_all(lambda to: pl.semaphore_signal(barrier, inc=1, device_id=to, device_id_type=MESH))

    loads = [
        pltpu.make_async_copy(src, dst, in_sem.at[i])
        for i, (src, dst) in enumerate((
            (samples_in, samples), (pointing_in, pointing), (angles_in, angles), (counts_in, counts),
            (sky_in, sky), (prec, pp.at[:, 8:72, :]), (first_in, first), (twist_in, twist),
            (last_in, last), (onoise_in, onoise), (oprior_in, oprior), (codes_in, codes),
        ))
    ]
    for load in loads:
        load.start()

    for load in loads[:4]:
        load.wait()

    row_i = lax.broadcasted_iota(jnp.int32, (128, 128), 0)
    col_i = lax.broadcasted_iota(jnp.int32, (128, 128), 1)
    for half in range(2):
        lanes = slice(half * 128, half * 128 + 128)
        sbuf[pl.ds(half, 128, stride=8), :] = samples[:, lanes]
        sbuf[pl.ds(2 + half, 128, stride=8), :] = angles[:, lanes]
        sbuf[pl.ds(4 + half, 128, stride=8), :] = pointing[:, lanes].astype(F32)
    count_row = jnp.broadcast_to(counts[...].astype(F32), (128, 128))
    count_col = jnp.sum(jnp.where(row_i == col_i, count_row, 0.0), axis=1, keepdims=True)
    count_full = jnp.broadcast_to(count_col, (128, 128))
    sbuf[pl.ds(6, 128, stride=8), :] = count_full
    sbuf[pl.ds(7, 128, stride=8), :] = count_full

    loads[4].wait()

    for c in range(3):
        blocks = []
        for cyc in range(2):
            turned = sky[c, pl.ds(cyc, 64, stride=2), :].T
            blocks.append(jnp.concatenate([turned[:64], turned[64:]], axis=1))
        full = jnp.concatenate(blocks, axis=1)
        upper = full.astype(BF16)
        table[pl.ds(c * 64, 64), :] = upper
        table[pl.ds(192 + c * 64, 64), :] = (full - upper.astype(F32)).astype(BF16)

    bw[:, 0:8, :] = jnp.zeros((7, 8, 128), F32)
    bw[:, 72:80, :] = jnp.zeros((7, 8, 128), F32)

    @pl.when(det == 0)
    def _():
        pp[:, 0:8, :] = jnp.zeros((3, 8, 128), F32)
        edge[0] = jnp.zeros((12, 8, 128), F32)
        spec_r[0:24, :] = jnp.zeros((24, 128), F32)

    @pl.when(det == NDET - 1)
    def _():
        pp[:, 72:80, :] = jnp.zeros((3, 8, 128), F32)
        edge[1] = jnp.zeros((12, 8, 128), F32)
        spec_r[67 * 8 : 70 * 8, :] = jnp.zeros((24, 128), F32)

    loads[11].wait()
    code = codes[...]
    source = ((code & 3) + det) % 4 * 32 + (((code >> 2) & 3) + ty) % 4 * 8
    source = source + (((code >> 4) & 3) + tz) % 4 * 2 + ((code >> 6) + tc) % 2
    match_s[...] = jnp.where(source == col_i, 1.0, 0.0)
    acc[...] = jnp.zeros_like(acc)
    pl.semaphore_wait(barrier, NDEV - 1)

    for s, (x, y, z, c) in enumerate(NEAR):
        if s == 0:
            continue
        where = at_det[-x % 4]
        to = at_y[-y % 4] + at_z[-z % 4] + at_c[c]
        pltpu.make_async_remote_copy(
            sbuf.at[pl.ds((where * NTM + to) * 8, 8)], rbuf.at[s * 8 : s * 8 + 8],
            send_sem, recv_sem.at[s // GROUP], device_id=(where, to), device_id_type=MESH,
        ).start()
    rbuf[0:8, :] = sbuf[pl.ds(me * 8, 8), :]

    down = ((det + 1) % NDET, tm)
    up = ((det + NDET - 1) % NDET, tm)

    def edge_copies(rows, side, padded, to):
        pairs = (
            (prec.at[:, rows, :], pp.at[:, padded, :]),
            (onoise_in.at[:, rows, :], edge.at[side, 0:6]),
            (oprior_in.at[:, rows, :], edge.at[side, 6:12]),
        )
        return [
            pltpu.make_async_remote_copy(
                src, dst, edge_send.at[side, i], edge_recv.at[side, i], device_id=to, device_id_type=MESH
            )
            for i, (src, dst) in enumerate(pairs)
        ]

    go_down = edge_copies(slice(56, 64), 0, slice(0, 8), down)
    go_up = edge_copies(slice(0, 8), 1, slice(72, 80), up)

    @pl.when(det < NDET - 1)
    def _():
        for copy in go_down:
            copy.start()

    @pl.when(det > 0)
    def _():
        for copy in go_up:
            copy.start()

    col_index = lax.broadcasted_iota(jnp.int32, (64, 128), 0).astype(F32)

    slot_index = lax.broadcasted_iota(jnp.int32, (GROUP, 128), 1).astype(F32)

    def gather_group(group):
        base = group * GROUP
        here = pl.ds(base, GROUP)

        def row(r):
            return rbuf[pl.ds(base * 8 + r, GROUP, stride=8), :]

        for half in range(2):
            pixel = row(4 + half).astype(jnp.int32)
            upper = (pixel >> 13) * 128 + ((pixel >> 6) & 1) * 64 + ((pixel >> 7) & 63)
            hi_s[half, here, :] = upper.astype(F32)
            lo_s[half, here, :] = (pixel & 63).astype(F32)
        pixel = jnp.concatenate(
            [rbuf[pl.ds((base + LOWER) * 8 + 4 + half, GROUP - LOWER, stride=8), :] for half in range(2)], axis=0
        ).astype(jnp.int32)
        in_row, at_lane = ((pixel >> 7) & 63) * 2 + (pixel >> 13), pixel & 127
        picked = [jnp.zeros((8, 128), F32) for _ in range(3)]

        def permute_rows(first_r, last_r):
            for r in range(first_r, last_r):
                same = in_row == r
                for c in range(3):
                    line = jnp.broadcast_to(sky[c, r : r + 1, :], (8, 128))
                    taken = jnp.take_along_axis(line, at_lane, axis=1)
                    picked[c] = jnp.where(same, taken, picked[c])

        for u in range(LOWER):
            s = base + u
            hots = [one_hot(hi_s[half, pl.ds(s, 1), :], 256) for half in range(2)]
            got = jnp.dot(table[...], jnp.concatenate(hots, axis=1), preferred_element_type=F32)
            got = got[:192] + got[192:]
            for half in range(2):
                low = lo_s[half, pl.ds(s, 1), :]
                same = col_index == low
                for c in range(3):
                    part = got[c * 64 : c * 64 + 64, half * 128 : half * 128 + 128]
                    look[c, half, pl.ds(s, 1), :] = jnp.sum(
                        jnp.where(same, part, 0.0), axis=0, keepdims=True
                    )
            permute_rows(u * 128 // LOWER, (u + 1) * 128 // LOWER)
        for half in range(2):
            for c in range(3):
                look[c, half, pl.ds(base + LOWER, GROUP - LOWER), :] = picked[c][half * 4 : half * 4 + 4]
        count = row(6)
        cross = jnp.zeros((GROUP, 128), F32)
        square = jnp.zeros((GROUP, 128), F32)
        for half in range(2):
            sine, cosine = sine_cosine(2.0 * row(2 + half))
            sin_s[half, here, :] = sine
            cos_s[half, here, :] = cosine
            signal = look[0, half, here, :] + look[1, half, here, :] * cosine + look[2, half, here, :] * sine
            look[0, half, here, :] = signal
            masked = jnp.where(slot_index + 128.0 * half < count, signal, 0.0)
            cross = cross + masked * row(half)
            square = square + masked * signal
        sums_s[0, here, :] = cross
        sums_s[1, here, :] = square

    @pl.loop(0, NGROUP)
    def _(group):
        @pl.when(group == 0)
        def _():
            span = rbuf.at[pl.ds(0, (GROUP - 1) * 8)]
            pltpu.make_async_copy(span, span, recv_sem.at[0]).wait()

        @pl.when(group > 0)
        def _():
            span = rbuf.at[pl.ds(0, GROUP * 8)]
            pltpu.make_async_copy(span, span, recv_sem.at[group]).wait()

        gather_group(group)

    match = match_s[...] > 0.5
    cross, square = (
        jnp.sum(
            jnp.where(match, jnp.sum(sums_s[k], axis=1, keepdims=True), 0.0), axis=0, keepdims=True
        )
        for k in range(2)
    )
    mine = stat_r.at[me // 4, pl.ds(me % 4 * 2, 2), :]
    mine[...] = jnp.concatenate([cross, square], axis=0)
    to_all(
        lambda to: pltpu.make_async_remote_copy(
            mine, mine, stat_send, stat_recv, device_id=to, device_id_type=MESH
        ).start()
    )
    count = rbuf[pl.ds(6, 128, stride=8), :]
    slot = col_i.astype(F32)
    hits = [jnp.zeros((1, 128), F32) for _ in range(2)]
    for half in range(2):
        good = slot + 128.0 * half < count
        for first_w, value in ((0, rbuf[pl.ds(half, 128, stride=8), :]), (3, look[0, half])):
            value = jnp.where(good, value, 0.0)
            wsplit[first_w, half] = value
            wsplit[first_w + 1, half] = value * cos_s[half]
            wsplit[first_w + 2, half] = value * sin_s[half]
        late = jnp.where(hi_s[half] >= 128.0, 1.0, 0.0)
        valid = jnp.where(good, 1.0, 0.0)
        hits[1] = hits[1] + jnp.sum(valid * late, axis=0, keepdims=True)
        hits[0] = hits[0] + jnp.sum(valid * (1.0 - late), axis=0, keepdims=True)
    rest = sbuf.at[pl.ds(0, 2 * (NDEV - 1))]
    pltpu.make_async_copy(rest, rest, stat_recv).wait()
    total = jnp.sum(stat_r[...], axis=0)
    total = total[0:2] + total[2:4] + total[4:6] + total[6:8]
    gains = total[0:1] / (total[1:2] + 1e-06)
    lane = lax.broadcasted_iota(jnp.int32, (1, 128), 1)
    own_gain = jnp.sum(jnp.where(lane == me, gains, 0.0), axis=1, keepdims=True)
    gain_col = jnp.sum(jnp.where(match, gains, 0.0), axis=1, keepdims=True)
    gain_full = jnp.broadcast_to(gain_col, (128, 128))

    for half in range(2):
        for c in range(3):
            weight = wsplit[c, half] - gain_full * wsplit[3 + c, half]
            upper = weight.astype(BF16).astype(F32)
            wsplit[c, half] = upper
            wsplit[3 + c, half] = weight - upper

    low_index = lax.broadcasted_iota(jnp.int32, (64, 128), 0).astype(F32).astype(BF16).reshape(4, 16, 128)

    @pl.loop(0, NDEV // UNROLL)
    def _(step):
        lefts = []
        rights = []
        for u in range(UNROLL):
            s = step * UNROLL + u
            for half in range(2):
                rights.append(one_hot(hi_s[half, pl.ds(s, 1), :], 256))
                low = jnp.broadcast_to(lo_s[half, pl.ds(s, 1), :], (16, 128)).astype(BF16)
                same = low_index == low[None]
                rows = []
                for w in range(6):
                    value = jnp.broadcast_to(wsplit[w, half, pl.ds(s, 1), :], (16, 128)).astype(BF16)
                    rows.append(jnp.where(same, value[None], jnp.zeros((), BF16)).reshape(64, 128))
                lefts.append(jnp.concatenate(rows, axis=0))
        acc[...] += lax.dot_general(
            jnp.concatenate(lefts, axis=1), jnp.concatenate(rights, axis=1),
            (((1,), (1,)), ((), ())), preferred_element_type=F32,
        )

    field = acc[:192] + acc[192:]

    for load in loads[6:9]:
        load.wait()
    z_parts = []
    for cyc in range(2):
        y = dot3(split_parts(field[:, cyc * 128 : cyc * 128 + 128]), (first[0], first[1]))
        for c in range(3):
            y_re = y[c * 64 : c * 64 + 64, :128]
            y_im = y[c * 64 : c * 64 + 64, 128:]
            z_re = y_re * twist[0] + y_im * twist[1]
            z_im = y_im * twist[0] - y_re * twist[1]
            z_parts.append(jnp.concatenate([z_re, z_im], axis=0))
    x = dot3((last[0], last[1]), split_parts(jnp.concatenate(z_parts, axis=1)))
    for cyc in range(2):
        for c in range(3):
            block = x[:, (cyc * 3 + c) * 128 : (cyc * 3 + c) * 128 + 128]
            spec_s[pl.ds(cyc * 8 + 2 * c, 32, stride=16), :] = block[:32]
            spec_s[pl.ds(cyc * 8 + 2 * c + 1, 32, stride=16), :] = block[32:]
        weight = jnp.sum(hits[cyc], axis=1, keepdims=True) * (1.0 / 8192)
        for r in (6, 7):
            spec_s[pl.ds(cyc * 8 + r, 32, stride=16), :] = jnp.broadcast_to(weight, (32, 128))

    def send_spectrum(where, to, skip, tiles, slot, send, recv):
        pltpu.make_async_remote_copy(
            spec_s.at[pl.ds(to * 16 + skip * 8, tiles * 8)], spec_r.at[pl.ds(slot * 8, tiles * 8)],
            send, recv, device_id=(where, to), device_id_type=MESH,
        ).start()

    def send_rim(where, skip, tiles, slot, recv):
        send = lambda to: send_spectrum(where, to, skip, tiles, slot, rim_send, recv)
        to_tm(send)
        send(tm)

    rims = []
    for at, bound, step, skip, tiles, slot, side in (
        (0, det > 0, -1, 0, 2, 67, 1),
        (1, det > 0, -1, 0, 1, 69, 1),
        (NTM - 2, det < NDET - 1, 1, 1, 1, 0, 0),
        (NTM - 1, det < NDET - 1, 1, 0, 2, 1, 0),
    ):
        here = jnp.logical_and(tm == at, bound)
        rims.append((here, tiles))

        @pl.when(here)
        def _():
            send_rim(det + step, skip, tiles, slot, rim_recv.at[side])

    to_tm(lambda to: send_spectrum(det, to, 0, 2, 3 + 2 * tm, spec_send, spec_recv))
    spec_r[pl.ds((3 + 2 * tm) * 8, 16), :] = spec_s[pl.ds(tm * 16, 16), :]
    for c in range(3):
        for cyc in range(2):
            block = field[c * 64 : c * 64 + 64, cyc * 128 : cyc * 128 + 128]
            block = jnp.concatenate([block[:, :64], block[:, 64:]], axis=0)
            map_s[c, pl.ds(cyc, 64, stride=2), :] = block.T
    loads[5].wait()
    loads[9].wait()
    loads[10].wait()

    @pl.when(det > 0)
    def _():
        for copy in go_down:
            copy.wait_recv()

    @pl.when(det < NDET - 1)
    def _():
        for copy in go_up:
            copy.wait_recv()

    for c in range(3):
        root_s[c] = jnp.sqrt(pp[c])

    @pl.when(det > 0)
    def _():
        span = spec_r.at[pl.ds(0, 24)]
        pltpu.make_async_copy(span, span, rim_recv.at[0]).wait()

    @pl.when(det < NDET - 1)
    def _():
        span = spec_r.at[pl.ds(0, 24)]
        pltpu.make_async_copy(span, span, rim_recv.at[1]).wait()

    span = spec_r.at[pl.ds(0, (NTM - 1) * 16)]
    pltpu.make_async_copy(span, span, spec_recv).wait()

    for j in range(7):
        bw[j, 5:75, :] = spec_r[pl.ds(j, 70, stride=8), :]
    noise_root = jnp.sqrt(bw[6])
    for j in range(6):
        noise = jnp.concatenate([edge[0, j], onoise[j], edge[1, j]], axis=0)
        prior = jnp.concatenate([edge[0, 6 + j], oprior[j], edge[1, 6 + j]], axis=0)
        bw[j] = bw[j] + noise_root * noise + root_s[j // 2] * prior

    moments = [jnp.zeros((8, 128), F32) for _ in range(6)]
    for c in range(3):
        precision = pp[c]
        root = root_s[c]
        side = root * (0.45 / SCALE)
        diagonal = (precision + bw[6] - SHIFT) * (1.0 / SCALE)

        def step(v):
            u = root * v
            beside = pltpu.roll(u, 1, 0) + pltpu.roll(u, 79, 0)
            return diagonal * v - side * beside

        for p in range(2):
            j = 2 * c + p
            v0 = bw[j]
            v1 = step(v0)
            v2 = step(v1)
            v3 = step(v2)
            own = [v[8:72] for v in (v0, v1, v2, v3)]
            v1_s[j] = own[1]
            v2_s[j] = own[2]
            for m, (a, b) in enumerate(((0, 0), (0, 1), (1, 1), (1, 2), (2, 2), (2, 3))):
                moments[m] = moments[m] + jnp.sum((own[a] * own[b]).reshape(8, 8, 128), axis=0)
    message = jnp.zeros((1, 128), F32)
    for m in range(6):
        value = jnp.sum(jnp.sum(moments[m], axis=0, keepdims=True), axis=1, keepdims=True)
        message = jnp.where(lane == m, jnp.broadcast_to(value, (1, 128)), message)
    own_row = mom_r.at[me // 8, pl.ds(me % 8, 1), :]
    own_row[...] = message
    to_all(
        lambda to: pltpu.make_async_remote_copy(
            own_row, own_row, mom_send, mom_recv, device_id=to, device_id_type=MESH
        ).start()
    )
    rest = sbuf.at[pl.ds(0, NDEV - 1)]
    pltpu.make_async_copy(rest, rest, mom_recv).wait()
    sums = jnp.sum(jnp.sum(mom_r[...], axis=0), axis=0, keepdims=True)
    nu = [jnp.sum(jnp.where(lane == m, sums, 0.0), axis=1, keepdims=True) for m in range(6)]

    zero = jnp.zeros((1, 1), F32)

    def inner(a, b):
        terms = {}
        for i, x_i in enumerate(a):
            for j, y_j in enumerate(b):
                terms[i + j] = terms.get(i + j, zero) + x_i * y_j
        out = zero
        for power, value in terms.items():
            out = out + value * nu[power]
        return out

    def image_of(a):
        longer = list(a) + [zero]
        return [SHIFT * longer[i] + (SCALE * longer[i - 1] if i else zero) for i in range(len(longer))]

    resid = [zero + 1.0]
    direction = [zero + 1.0]
    answer = [zero, zero, zero]
    norm_now = nu[0]
    for iteration in range(3):
        image = image_of(direction)
        alpha = norm_now / inner(direction, image)
        alpha = jnp.minimum(jnp.maximum(alpha, 0.0), STEP_MAX)
        for i, value in enumerate(direction):
            answer[i] = answer[i] + alpha * value
        if iteration < 2:
            resid = resid + [zero]
            resid = [r - alpha * w for r, w in zip(resid, image)]
            norm_next = jnp.maximum(inner(resid, resid), 0.0)
            beta = norm_next / norm_now
            direction = [r + beta * d for r, d in zip(resid, direction + [zero])]
            norm_now = norm_next
    small_out[...] = jnp.broadcast_to(own_gain, (8, 128))
    for j in range(6):
        sol_out[j] = answer[0] * bw[j, 8:72, :] + answer[1] * v1_s[j] + answer[2] * v2_s[j]

    span = sbuf.at[pl.ds(0, (NDEV - 1) * 8)]
    pltpu.make_async_copy(span, span, send_sem).wait()
    rest = sbuf.at[pl.ds(0, 2 * (NDEV - 1))]
    pltpu.make_async_copy(rest, rest, stat_send).wait()
    span = spec_s.at[pl.ds(0, (NTM - 1) * 16)]
    pltpu.make_async_copy(span, span, spec_send).wait()
    rest = sbuf.at[pl.ds(0, NDEV - 1)]
    pltpu.make_async_copy(rest, rest, mom_send).wait()

    for here, tiles in rims:
        @pl.when(here)
        def _():
            span = spec_s.at[pl.ds(0, NTM * tiles * 8)]
            pltpu.make_async_copy(span, span, rim_send).wait()

    @pl.when(det < NDET - 1)
    def _():
        for copy in go_down:
            copy.wait_send()

    @pl.when(det > 0)
    def _():
        for copy in go_up:
            copy.wait_send()


def finish(small, map_in, sol_in, gain_out, map_out, sol_out, gain, out_sem):
    gain[...] = small[0:1, 0:1]
    stores = [
        pltpu.make_async_copy(sol_in, sol_out, out_sem.at[0]),
        pltpu.make_async_copy(map_in, map_out, out_sem.at[1]),
        pltpu.make_async_copy(gain, gain_out, out_sem.at[2]),
    ]
    for store in stores:
        store.start()
    for store in stores:
        store.wait()


def per_device(
    samples, pointing, angles, counts, sky_map, prior_precision, omega_noise, omega_prior
):
    sky = sky_map.reshape(3, 2, 64, 128).transpose(0, 2, 1, 3).reshape(3, 128, 128)
    vmem = pl.BlockSpec(memory_space=pltpu.VMEM)
    dma = pltpu.SemaphoreType.DMA
    anywhere = pl.BlockSpec(memory_space=pl.ANY)
    small, binned, solved = pl.pallas_call(
        kernel,
        name="gibbs_step",
        out_shape=(
            pltpu.VMEM((8, 128), F32),
            pltpu.VMEM((3, 128, 128), F32),
            pltpu.VMEM((6, 64, 128), F32),
        ),
        in_specs=[anywhere] * 12,
        out_specs=(vmem, vmem, vmem),
        scratch_shapes=[
            pltpu.VMEM((128, 256), F32),
            pltpu.VMEM((128, 256), jnp.int32),
            pltpu.VMEM((128, 256), F32),
            pltpu.VMEM((1, 128), jnp.int32),
            pltpu.VMEM((3, 128, 128), F32),
            pltpu.VMEM((6, 64, 128), F32),
            pltpu.VMEM((6, 64, 128), F32),
            pltpu.VMEM((2, 128, 256), BF16),
            pltpu.VMEM((2, 64, 128), F32),
            pltpu.VMEM((2, 64, 128), BF16),
            pltpu.VMEM((NDEV, 128), jnp.int32),
            pltpu.VMEM((NDEV, 128), F32),
            pltpu.VMEM((1024, 128), F32),
            pltpu.VMEM((1024, 128), F32),
            pltpu.VMEM((384, 256), BF16),
            pltpu.VMEM((2, 128, 128), F32),
            pltpu.VMEM((2, 128, 128), F32),
            pltpu.VMEM((2, 128, 128), F32),
            pltpu.VMEM((2, 128, 128), F32),
            pltpu.VMEM((3, 2, 128, 128), F32),
            pltpu.VMEM((2, 128, 128), F32),
            pltpu.VMEM((6, 2, 128, 128), F32),
            pltpu.VMEM((384, 256), F32),
            pltpu.VMEM((NDEV // 4, 8, 128), F32),
            pltpu.VMEM((NTM * 16, 128), F32),
            pltpu.VMEM((70 * 8, 128), F32),
            pltpu.VMEM((3, 80, 128), F32),
            pltpu.VMEM((3, 80, 128), F32),
            pltpu.VMEM((2, 12, 8, 128), F32),
            pltpu.VMEM((7, 80, 128), F32),
            pltpu.VMEM((6, 64, 128), F32),
            pltpu.VMEM((6, 64, 128), F32),
            pltpu.VMEM((NDEV // 8, 8, 128), F32),
            dma, dma((NGROUP,)), dma, dma, dma, dma,
            dma, dma((2,)), dma((2, 3)), dma((2, 3)), dma, dma,
            dma((12,)),
        ],
        compiler_params=pltpu.CompilerParams(collective_id=0, has_side_effects=True),
    )(
        samples.reshape(128, 256),
        pointing.reshape(128, 256),
        angles.reshape(128, 256),
        counts.reshape(1, 128),
        sky,
        prior_precision,
        omega_noise,
        omega_prior,
        *(jnp.asarray(t) for t in tables()),
    )
    gain, binned, solved = pl.pallas_call(
        finish,
        name="finish",
        out_shape=(
            jax.ShapeDtypeStruct((1, 1), F32),
            jax.ShapeDtypeStruct((3, 128, 128), F32),
            jax.ShapeDtypeStruct((6, 64, 128), F32),
        ),
        in_specs=[vmem, vmem, vmem],
        out_specs=(anywhere, anywhere, anywhere),
        scratch_shapes=[pltpu.VMEM((1, 1), F32), dma((3,))],
    )(*(pltpu.with_memory_space_constraint(x, pltpu.VMEM) for x in (small, binned, solved)))
    binned = binned.reshape(3, 64, 2, 128).transpose(0, 2, 1, 3).reshape(3, 2, 8192)
    return (gain, binned, solved)


def solution(mesh):
    return jax.shard_map(
        per_device,
        mesh=mesh,
        in_specs=(
            P("det", "tm", None, None),
            P("det", "tm", None, None),
            P("det", "tm", None, None),
            P("det", "tm", None),
            P(None, ("det", "tm"), None),
            P(None, "det", "tm"),
            P(None, "det", "tm"),
            P(None, "det", "tm"),
        ),
        out_specs=(P("det", "tm"), P(None, ("det", "tm"), None), P(None, "det", "tm")),
        check_vma=False,
    )
```

```python
import math

import jax
import jax.numpy as jnp
import numpy as np
from jax import lax
from jax.experimental import pallas as pl
from jax.experimental.pallas import tpu as pltpu
from jax.sharding import PartitionSpec as P

MESH = pl.DeviceIdType.MESH
F32 = jnp.float32
BF16 = jnp.bfloat16
NDET = 4
NTM = 32
NDEV = NDET * NTM
GROUP = 16
NGROUP = NDEV // GROUP
LOWER = 12
UNROLL = 128
SHIFT = 4.0
SCALE = 4.0
STEP_MAX = 20.0


def near_first():
    ring = (0, 1, 2, 1)
    return sorted(
        ((x, y, z, c) for x in range(4) for y in range(4) for z in range(4) for c in range(2)),
        key=lambda o: 4 * (ring[o[0]] + ring[o[1]] + ring[o[2]]) + o[3],
    )


NEAR = near_first()


def tables():
    h, i = np.divmod(np.arange(128), 64)
    a = 2 * i + h
    k = np.arange(128)
    ang = 2.0 * np.pi * (np.outer(a, k) % 128) / 128
    first = np.concatenate([np.cos(ang), -np.sin(ang)], axis=1)
    b = np.arange(64)
    ang = 2.0 * np.pi * np.outer(b, k) / 8192
    twist = np.stack([np.cos(ang), np.sin(ang)])
    q = np.arange(32)
    ang = 2.0 * np.pi * (np.outer(q, b) % 64) / 64
    c, s = np.cos(ang), np.sin(ang)
    last = np.concatenate([np.concatenate([c, s], axis=1), np.concatenate([-s, c], axis=1)], axis=0)
    last = last / math.sqrt(8192)
    def split(x):
        upper = x.astype(np.float32).astype(jnp.bfloat16)
        return np.stack([upper, (x - upper.astype(np.float64)).astype(jnp.bfloat16)])

    codes = np.asarray([o[0] + 4 * o[1] + 16 * o[2] + 64 * o[3] for o in NEAR], np.int32)
    codes = np.ascontiguousarray(np.broadcast_to(codes[:, None], (NDEV, 128)))
    return [split(first), twist.astype(np.float32), split(last), codes]


def split_parts(x):
    upper = x.astype(BF16)
    return upper, (x - upper.astype(F32)).astype(BF16)


def dot3(a, b):
    out = jnp.dot(a[0], b[0], preferred_element_type=F32)
    out = out + jnp.dot(a[0], b[1], preferred_element_type=F32)
    return out + jnp.dot(a[1], b[0], preferred_element_type=F32)


def sine_cosine(x):
    k = jnp.floor(x * (2.0 / math.pi) + 0.5)
    r = ((x - k * 1.5703125) - k * 4.837512969970703125e-4) - k * 7.549789948768648e-8
    z = r * r
    sine = r + r * z * (-1.6666654611e-1 + z * (8.3321608736e-3 - z * 1.9515295891e-4))
    cosine = 1.0 - 0.5 * z + z * z * (
        4.166664568298827e-2 + z * (-1.388731625493765e-3 + z * 2.443315711809948e-5)
    )
    q = k.astype(jnp.int32) & 3
    odd = (q & 1) == 1
    s = jnp.where(odd, cosine, sine)
    c = jnp.where(odd, sine, cosine)
    s = jnp.where(q >= 2, -s, s)
    c = jnp.where((q == 1) | (q == 2), -c, c)
    return s, c


def one_hot(row, rows):
    value = jnp.broadcast_to(row, (16, 128)).astype(BF16)
    index = lax.broadcasted_iota(jnp.int32, (rows, 128), 0).astype(F32).astype(BF16)
    same = index.reshape(rows // 16, 16, 128) == value[None]
    return jnp.where(same, jnp.ones((), BF16), jnp.zeros((), BF16)).reshape(rows, 128)


def kernel(
    samples_in, pointing_in, angles_in, counts_in, sky_in, prec, onoise_in, oprior_in,
    first_in, twist_in, last_in, codes_in,
    small_out, map_s, sol_out,
    samples, pointing, angles, counts, sky, onoise, oprior, first, twist, last, codes, match_s,
    sbuf, rbuf, table, hi_s, lo_s, cos_s, sin_s, look, sums_s, wsplit, acc,
    stat_r, spec_s, spec_r, pp, root_s, edge, bw, v1_s, v2_s, mom_r,
    send_sem, recv_sem, stat_send, stat_recv, spec_send, spec_recv,
    rim_send, rim_recv, edge_send, edge_recv, mom_send, mom_recv, in_sem,
):
    det = lax.axis_index("det")
    tm = lax.axis_index("tm")
    me = det * NTM + tm

    ty, tz, tc = tm // 8, (tm // 2) % 4, tm % 2
    at_z = [(tz + o) % 4 * 2 for o in range(4)]
    at_c = [tc, 1 - tc]
    at_y = [(ty + o) % 4 * 8 for o in range(4)]
    at_det = [(det + o) % NDET for o in range(NDET)]

    def to_tm(act):
        def row(y, own):
            for z in (2, 1, 3, 0):
                for c in (1, 0):
                    if not (own and z == 0 and c == 0):
                        act(y * 8 + at_z[z] + at_c[c])

        @pl.loop(0, 3)
        def _(d):
            row((ty + jnp.where(d == 0, 2, jnp.where(d == 1, 1, 3))) % 4, False)

        row(ty, True)

    def to_all(act):
        to_tm(lambda to: [act((at_det[x], to)) for x in (2, 1, 3, 0)])
        for x in (2, 1, 3):
            act((at_det[x], tm))

    barrier = pltpu.get_barrier_semaphore()
    to_all(lambda to: pl.semaphore_signal(barrier, inc=1, device_id=to, device_id_type=MESH))

    loads = [
        pltpu.make_async_copy(src, dst, in_sem.at[i])
        for i, (src, dst) in enumerate((
            (samples_in, samples), (pointing_in, pointing), (angles_in, angles), (counts_in, counts),
            (sky_in, sky), (prec, pp.at[:, 8:72, :]), (first_in, first), (twist_in, twist),
            (last_in, last), (onoise_in, onoise), (oprior_in, oprior), (codes_in, codes),
        ))
    ]
    for load in loads:
        load.start()

    for load in loads[:4]:
        load.wait()

    row_i = lax.broadcasted_iota(jnp.int32, (128, 128), 0)
    col_i = lax.broadcasted_iota(jnp.int32, (128, 128), 1)
    for half in range(2):
        lanes = slice(half * 128, half * 128 + 128)
        sbuf[pl.ds(half, 128, stride=8), :] = samples[:, lanes]
        sbuf[pl.ds(2 + half, 128, stride=8), :] = angles[:, lanes]
        sbuf[pl.ds(4 + half, 128, stride=8), :] = pointing[:, lanes].astype(F32)
    count_row = jnp.broadcast_to(counts[...].astype(F32), (128, 128))
    count_col = jnp.sum(jnp.where(row_i == col_i, count_row, 0.0), axis=1, keepdims=True)
    count_full = jnp.broadcast_to(count_col, (128, 128))
    sbuf[pl.ds(6, 128, stride=8), :] = count_full
    sbuf[pl.ds(7, 128, stride=8), :] = count_full

    loads[4].wait()

    for c in range(3):
        blocks = []
        for cyc in range(2):
            turned = sky[c, pl.ds(cyc, 64, stride=2), :].T
            blocks.append(jnp.concatenate([turned[:64], turned[64:]], axis=1))
        full = jnp.concatenate(blocks, axis=1)
        upper = full.astype(BF16)
        table[pl.ds(c * 64, 64), :] = upper
        table[pl.ds(192 + c * 64, 64), :] = (full - upper.astype(F32)).astype(BF16)

    bw[:, 0:8, :] = jnp.zeros((7, 8, 128), F32)
    bw[:, 72:80, :] = jnp.zeros((7, 8, 128), F32)

    @pl.when(det == 0)
    def _():
        pp[:, 0:8, :] = jnp.zeros((3, 8, 128), F32)
        edge[0] = jnp.zeros((12, 8, 128), F32)
        spec_r[0:24, :] = jnp.zeros((24, 128), F32)

    @pl.when(det == NDET - 1)
    def _():
        pp[:, 72:80, :] = jnp.zeros((3, 8, 128), F32)
        edge[1] = jnp.zeros((12, 8, 128), F32)
        spec_r[67 * 8 : 70 * 8, :] = jnp.zeros((24, 128), F32)

    loads[11].wait()
    code = codes[...]
    source = ((code & 3) + det) % 4 * 32 + (((code >> 2) & 3) + ty) % 4 * 8
    source = source + (((code >> 4) & 3) + tz) % 4 * 2 + ((code >> 6) + tc) % 2
    match_s[...] = jnp.where(source == col_i, 1.0, 0.0)
    pl.semaphore_wait(barrier, NDEV - 1)

    for s, (x, y, z, c) in enumerate(NEAR):
        if s == 0:
            continue
        where = at_det[-x % 4]
        to = at_y[-y % 4] + at_z[-z % 4] + at_c[c]
        pltpu.make_async_remote_copy(
            sbuf.at[pl.ds((where * NTM + to) * 8, 8)], rbuf.at[s * 8 : s * 8 + 8],
            send_sem, recv_sem.at[s // GROUP], device_id=(where, to), device_id_type=MESH,
        ).start()
    rbuf[0:8, :] = sbuf[pl.ds(me * 8, 8), :]

    down = ((det + 1) % NDET, tm)
    up = ((det + NDET - 1) % NDET, tm)

    def edge_copies(rows, side, padded, to):
        pairs = (
            (prec.at[:, rows, :], pp.at[:, padded, :]),
            (onoise_in.at[:, rows, :], edge.at[side, 0:6]),
            (oprior_in.at[:, rows, :], edge.at[side, 6:12]),
        )
        return [
            pltpu.make_async_remote_copy(
                src, dst, edge_send.at[side, i], edge_recv.at[side, i], device_id=to, device_id_type=MESH
            )
            for i, (src, dst) in enumerate(pairs)
        ]

    go_down = edge_copies(slice(56, 64), 0, slice(0, 8), down)
    go_up = edge_copies(slice(0, 8), 1, slice(72, 80), up)

    @pl.when(det < NDET - 1)
    def _():
        for copy in go_down:
            copy.start()

    @pl.when(det > 0)
    def _():
        for copy in go_up:
            copy.start()

    col_index = lax.broadcasted_iota(jnp.int32, (64, 128), 0).astype(F32)

    slot_index = lax.broadcasted_iota(jnp.int32, (GROUP, 128), 1).astype(F32)

    def gather_group(group):
        base = group * GROUP
        here = pl.ds(base, GROUP)

        def row(r):
            return rbuf[pl.ds(base * 8 + r, GROUP, stride=8), :]

        for half in range(2):
            pixel = row(4 + half).astype(jnp.int32)
            upper = (pixel >> 13) * 128 + ((pixel >> 6) & 1) * 64 + ((pixel >> 7) & 63)
            hi_s[half, here, :] = upper.astype(F32)
            lo_s[half, here, :] = (pixel & 63).astype(F32)
        pixel = jnp.concatenate(
            [rbuf[pl.ds((base + LOWER) * 8 + 4 + half, GROUP - LOWER, stride=8), :] for half in range(2)], axis=0
        ).astype(jnp.int32)
        in_row, at_lane = ((pixel >> 7) & 63) * 2 + (pixel >> 13), pixel & 127
        picked = [jnp.zeros((8, 128), F32) for _ in range(3)]

        def permute_rows(first_r, last_r):
            for r in range(first_r, last_r):
                same = in_row == r
                for c in range(3):
                    line = jnp.broadcast_to(sky[c, r : r + 1, :], (8, 128))
                    taken = jnp.take_along_axis(line, at_lane, axis=1)
                    picked[c] = jnp.where(same, taken, picked[c])

        for u in range(LOWER):
            s = base + u
            hots = [one_hot(hi_s[half, pl.ds(s, 1), :], 256) for half in range(2)]
            got = jnp.dot(table[...], jnp.concatenate(hots, axis=1), preferred_element_type=F32)
            got = got[:192] + got[192:]
            for half in range(2):
                low = lo_s[half, pl.ds(s, 1), :]
                same = col_index == low
                for c in range(3):
                    part = got[c * 64 : c * 64 + 64, half * 128 : half * 128 + 128]
                    look[c, half, pl.ds(s, 1), :] = jnp.sum(
                        jnp.where(same, part, 0.0), axis=0, keepdims=True
                    )
            permute_rows(u * 128 // LOWER, (u + 1) * 128 // LOWER)
        for half in range(2):
            for c in range(3):
                look[c, half, pl.ds(base + LOWER, GROUP - LOWER), :] = picked[c][half * 4 : half * 4 + 4]
        count = row(6)
        cross = jnp.zeros((GROUP, 128), F32)
        square = jnp.zeros((GROUP, 128), F32)
        for half in range(2):
            sine, cosine = sine_cosine(2.0 * row(2 + half))
            sin_s[half, here, :] = sine
            cos_s[half, here, :] = cosine
            signal = look[0, half, here, :] + look[1, half, here, :] * cosine + look[2, half, here, :] * sine
            look[0, half, here, :] = signal
            masked = jnp.where(slot_index + 128.0 * half < count, signal, 0.0)
            cross = cross + masked * row(half)
            square = square + masked * signal
        sums_s[0, here, :] = cross
        sums_s[1, here, :] = square

    @pl.loop(0, NGROUP)
    def _(group):
        @pl.when(group == 0)
        def _():
            span = rbuf.at[pl.ds(0, (GROUP - 1) * 8)]
            pltpu.make_async_copy(span, span, recv_sem.at[0]).wait()

        @pl.when(group > 0)
        def _():
            span = rbuf.at[pl.ds(0, GROUP * 8)]
            pltpu.make_async_copy(span, span, recv_sem.at[group]).wait()

        gather_group(group)

    match = match_s[...] > 0.5
    cross, square = (
        jnp.sum(
            jnp.where(match, jnp.sum(sums_s[k], axis=1, keepdims=True), 0.0), axis=0, keepdims=True
        )
        for k in range(2)
    )
    mine = stat_r.at[me // 4, pl.ds(me % 4 * 2, 2), :]
    mine[...] = jnp.concatenate([cross, square], axis=0)
    to_all(
        lambda to: pltpu.make_async_remote_copy(
            mine, mine, stat_send, stat_recv, device_id=to, device_id_type=MESH
        ).start()
    )
    count = rbuf[pl.ds(6, 128, stride=8), :]
    slot = col_i.astype(F32)
    hits = [jnp.zeros((1, 128), F32) for _ in range(2)]
    for half in range(2):
        good = slot + 128.0 * half < count
        for first_w, value in ((0, rbuf[pl.ds(half, 128, stride=8), :]), (3, look[0, half])):
            value = jnp.where(good, value, 0.0)
            wsplit[first_w, half] = value
            wsplit[first_w + 1, half] = value * cos_s[half]
            wsplit[first_w + 2, half] = value * sin_s[half]
        late = jnp.where(hi_s[half] >= 128.0, 1.0, 0.0)
        valid = jnp.where(good, 1.0, 0.0)
        hits[1] = hits[1] + jnp.sum(valid * late, axis=0, keepdims=True)
        hits[0] = hits[0] + jnp.sum(valid * (1.0 - late), axis=0, keepdims=True)
    rest = sbuf.at[pl.ds(0, 2 * (NDEV - 1))]
    pltpu.make_async_copy(rest, rest, stat_recv).wait()
    total = jnp.sum(stat_r[...], axis=0)
    total = total[0:2] + total[2:4] + total[4:6] + total[6:8]
    gains = total[0:1] / (total[1:2] + 1e-06)
    lane = lax.broadcasted_iota(jnp.int32, (1, 128), 1)
    own_gain = jnp.sum(jnp.where(lane == me, gains, 0.0), axis=1, keepdims=True)
    gain_col = jnp.sum(jnp.where(match, gains, 0.0), axis=1, keepdims=True)
    gain_full = jnp.broadcast_to(gain_col, (128, 128))

    for half in range(2):
        for c in range(3):
            weight = wsplit[c, half] - gain_full * wsplit[3 + c, half]
            upper = weight.astype(BF16).astype(F32)
            wsplit[c, half] = upper
            wsplit[3 + c, half] = weight - upper

    low_index = lax.broadcasted_iota(jnp.int32, (64, 128), 0).astype(F32).astype(BF16).reshape(4, 16, 128)

    @pl.loop(0, NDEV // UNROLL)
    def _(step):
        lefts = []
        rights = []
        for u in range(UNROLL):
            s = step * UNROLL + u
            for half in range(2):
                rights.append(one_hot(hi_s[half, pl.ds(s, 1), :], 256))
                low = jnp.broadcast_to(lo_s[half, pl.ds(s, 1), :], (16, 128)).astype(BF16)
                same = low_index == low[None]
                rows = []
                for w in range(6):
                    value = jnp.broadcast_to(wsplit[w, half, pl.ds(s, 1), :], (16, 128)).astype(BF16)
                    rows.append(jnp.where(same, value[None], jnp.zeros((), BF16)).reshape(64, 128))
                lefts.append(jnp.concatenate(rows, axis=0))
        acc[...] = lax.dot_general(
            jnp.concatenate(lefts, axis=1), jnp.concatenate(rights, axis=1),
            (((1,), (1,)), ((), ())), preferred_element_type=F32,
        )

    field = acc[:192] + acc[192:]

    for load in loads[6:9]:
        load.wait()
    z_parts = []
    for cyc in range(2):
        y = dot3(split_parts(field[:, cyc * 128 : cyc * 128 + 128]), (first[0], first[1]))
        for c in range(3):
            y_re = y[c * 64 : c * 64 + 64, :128]
            y_im = y[c * 64 : c * 64 + 64, 128:]
            z_re = y_re * twist[0] + y_im * twist[1]
            z_im = y_im * twist[0] - y_re * twist[1]
            z_parts.append(jnp.concatenate([z_re, z_im], axis=0))
    x = dot3((last[0], last[1]), split_parts(jnp.concatenate(z_parts, axis=1)))
    for cyc in range(2):
        for c in range(3):
            block = x[:, (cyc * 3 + c) * 128 : (cyc * 3 + c) * 128 + 128]
            spec_s[pl.ds(cyc * 8 + 2 * c, 32, stride=16), :] = block[:32]
            spec_s[pl.ds(cyc * 8 + 2 * c + 1, 32, stride=16), :] = block[32:]
        weight = jnp.sum(hits[cyc], axis=1, keepdims=True) * (1.0 / 8192)
        for r in (6, 7):
            spec_s[pl.ds(cyc * 8 + r, 32, stride=16), :] = jnp.broadcast_to(weight, (32, 128))

    def send_spectrum(where, to, skip, tiles, slot, send, recv):
        pltpu.make_async_remote_copy(
            spec_s.at[pl.ds(to * 16 + skip * 8, tiles * 8)], spec_r.at[pl.ds(slot * 8, tiles * 8)],
            send, recv, device_id=(where, to), device_id_type=MESH,
        ).start()

    def send_rim(where, skip, tiles, slot, recv):
        send = lambda to: send_spectrum(where, to, skip, tiles, slot, rim_send, recv)
        to_tm(send)
        send(tm)

    rims = []
    for at, bound, step, skip, tiles, slot, side in (
        (0, det > 0, -1, 0, 2, 67, 1),
        (1, det > 0, -1, 0, 1, 69, 1),
        (NTM - 2, det < NDET - 1, 1, 1, 1, 0, 0),
        (NTM - 1, det < NDET - 1, 1, 0, 2, 1, 0),
    ):
        here = jnp.logical_and(tm == at, bound)
        rims.append((here, tiles))

        @pl.when(here)
        def _():
            send_rim(det + step, skip, tiles, slot, rim_recv.at[side])

    to_tm(lambda to: send_spectrum(det, to, 0, 2, 3 + 2 * tm, spec_send, spec_recv))
    spec_r[pl.ds((3 + 2 * tm) * 8, 16), :] = spec_s[pl.ds(tm * 16, 16), :]
    for c in range(3):
        for cyc in range(2):
            block = field[c * 64 : c * 64 + 64, cyc * 128 : cyc * 128 + 128]
            block = jnp.concatenate([block[:, :64], block[:, 64:]], axis=0)
            map_s[c, pl.ds(cyc, 64, stride=2), :] = block.T
    loads[5].wait()
    loads[9].wait()
    loads[10].wait()

    @pl.when(det > 0)
    def _():
        for copy in go_down:
            copy.wait_recv()

    @pl.when(det < NDET - 1)
    def _():
        for copy in go_up:
            copy.wait_recv()

    for c in range(3):
        root_s[c] = jnp.sqrt(pp[c])

    @pl.when(det > 0)
    def _():
        span = spec_r.at[pl.ds(0, 24)]
        pltpu.make_async_copy(span, span, rim_recv.at[0]).wait()

    @pl.when(det < NDET - 1)
    def _():
        span = spec_r.at[pl.ds(0, 24)]
        pltpu.make_async_copy(span, span, rim_recv.at[1]).wait()

    span = spec_r.at[pl.ds(0, (NTM - 1) * 16)]
    pltpu.make_async_copy(span, span, spec_recv).wait()

    for j in range(7):
        bw[j, 5:75, :] = spec_r[pl.ds(j, 70, stride=8), :]
    noise_root = jnp.sqrt(bw[6])
    for j in range(6):
        noise = jnp.concatenate([edge[0, j], onoise[j], edge[1, j]], axis=0)
        prior = jnp.concatenate([edge[0, 6 + j], oprior[j], edge[1, 6 + j]], axis=0)
        bw[j] = bw[j] + noise_root * noise + root_s[j // 2] * prior

    moments = [jnp.zeros((8, 128), F32) for _ in range(6)]
    for c in range(3):
        precision = pp[c]
        root = root_s[c]
        side = root * (0.45 / SCALE)
        diagonal = (precision + bw[6] - SHIFT) * (1.0 / SCALE)

        def step(v):
            u = root * v
            beside = pltpu.roll(u, 1, 0) + pltpu.roll(u, 79, 0)
            return diagonal * v - side * beside

        for p in range(2):
            j = 2 * c + p
            v0 = bw[j]
            v1 = step(v0)
            v2 = step(v1)
            v3 = step(v2)
            own = [v[8:72] for v in (v0, v1, v2, v3)]
            v1_s[j] = own[1]
            v2_s[j] = own[2]
            for m, (a, b) in enumerate(((0, 0), (0, 1), (1, 1), (1, 2), (2, 2), (2, 3))):
                moments[m] = moments[m] + jnp.sum((own[a] * own[b]).reshape(8, 8, 128), axis=0)
    message = jnp.zeros((1, 128), F32)
    for m in range(6):
        value = jnp.sum(jnp.sum(moments[m], axis=0, keepdims=True), axis=1, keepdims=True)
        message = jnp.where(lane == m, jnp.broadcast_to(value, (1, 128)), message)
    own_row = mom_r.at[me // 8, pl.ds(me % 8, 1), :]
    own_row[...] = message
    to_all(
        lambda to: pltpu.make_async_remote_copy(
            own_row, own_row, mom_send, mom_recv, device_id=to, device_id_type=MESH
        ).start()
    )
    rest = sbuf.at[pl.ds(0, NDEV - 1)]
    pltpu.make_async_copy(rest, rest, mom_recv).wait()
    sums = jnp.sum(jnp.sum(mom_r[...], axis=0), axis=0, keepdims=True)
    nu = [jnp.sum(jnp.where(lane == m, sums, 0.0), axis=1, keepdims=True) for m in range(6)]

    zero = jnp.zeros((1, 1), F32)

    def inner(a, b):
        terms = {}
        for i, x_i in enumerate(a):
            for j, y_j in enumerate(b):
                terms[i + j] = terms.get(i + j, zero) + x_i * y_j
        out = zero
        for power, value in terms.items():
            out = out + value * nu[power]
        return out

    def image_of(a):
        longer = list(a) + [zero]
        return [SHIFT * longer[i] + (SCALE * longer[i - 1] if i else zero) for i in range(len(longer))]

    resid = [zero + 1.0]
    direction = [zero + 1.0]
    answer = [zero, zero, zero]
    norm_now = nu[0]
    for iteration in range(3):
        image = image_of(direction)
        alpha = norm_now / inner(direction, image)
        alpha = jnp.minimum(jnp.maximum(alpha, 0.0), STEP_MAX)
        for i, value in enumerate(direction):
            answer[i] = answer[i] + alpha * value
        if iteration < 2:
            resid = resid + [zero]
            resid = [r - alpha * w for r, w in zip(resid, image)]
            norm_next = jnp.maximum(inner(resid, resid), 0.0)
            beta = norm_next / norm_now
            direction = [r + beta * d for r, d in zip(resid, direction + [zero])]
            norm_now = norm_next
    small_out[...] = jnp.broadcast_to(own_gain, (8, 128))
    for j in range(6):
        sol_out[j] = answer[0] * bw[j, 8:72, :] + answer[1] * v1_s[j] + answer[2] * v2_s[j]

    span = sbuf.at[pl.ds(0, (NDEV - 1) * 8)]
    pltpu.make_async_copy(span, span, send_sem).wait()
    rest = sbuf.at[pl.ds(0, 2 * (NDEV - 1))]
    pltpu.make_async_copy(rest, rest, stat_send).wait()
    span = spec_s.at[pl.ds(0, (NTM - 1) * 16)]
    pltpu.make_async_copy(span, span, spec_send).wait()
    rest = sbuf.at[pl.ds(0, NDEV - 1)]
    pltpu.make_async_copy(rest, rest, mom_send).wait()

    for here, tiles in rims:
        @pl.when(here)
        def _():
            span = spec_s.at[pl.ds(0, NTM * tiles * 8)]
            pltpu.make_async_copy(span, span, rim_send).wait()

    @pl.when(det < NDET - 1)
    def _():
        for copy in go_down:
            copy.wait_send()

    @pl.when(det > 0)
    def _():
        for copy in go_up:
            copy.wait_send()


def finish(small, map_in, sol_in, gain_out, map_out, sol_out, gain, out_sem):
    gain[...] = small[0:1, 0:1]
    stores = [
        pltpu.make_async_copy(sol_in, sol_out, out_sem.at[0]),
        pltpu.make_async_copy(map_in, map_out, out_sem.at[1]),
        pltpu.make_async_copy(gain, gain_out, out_sem.at[2]),
    ]
    for store in stores:
        store.start()
    for store in stores:
        store.wait()


def per_device(
    samples, pointing, angles, counts, sky_map, prior_precision, omega_noise, omega_prior
):
    sky = sky_map.reshape(3, 2, 64, 128).transpose(0, 2, 1, 3).reshape(3, 128, 128)
    vmem = pl.BlockSpec(memory_space=pltpu.VMEM)
    dma = pltpu.SemaphoreType.DMA
    anywhere = pl.BlockSpec(memory_space=pl.ANY)
    small, binned, solved = pl.pallas_call(
        kernel,
        name="gibbs_step",
        out_shape=(
            pltpu.VMEM((8, 128), F32),
            pltpu.VMEM((3, 128, 128), F32),
            pltpu.VMEM((6, 64, 128), F32),
        ),
        in_specs=[anywhere] * 12,
        out_specs=(vmem, vmem, vmem),
        scratch_shapes=[
            pltpu.VMEM((128, 256), F32),
            pltpu.VMEM((128, 256), jnp.int32),
            pltpu.VMEM((128, 256), F32),
            pltpu.VMEM((1, 128), jnp.int32),
            pltpu.VMEM((3, 128, 128), F32),
            pltpu.VMEM((6, 64, 128), F32),
            pltpu.VMEM((6, 64, 128), F32),
            pltpu.VMEM((2, 128, 256), BF16),
            pltpu.VMEM((2, 64, 128), F32),
            pltpu.VMEM((2, 64, 128), BF16),
            pltpu.VMEM((NDEV, 128), jnp.int32),
            pltpu.VMEM((NDEV, 128), F32),
            pltpu.VMEM((1024, 128), F32),
            pltpu.VMEM((1024, 128), F32),
            pltpu.VMEM((384, 256), BF16),
            pltpu.VMEM((2, 128, 128), F32),
            pltpu.VMEM((2, 128, 128), F32),
            pltpu.VMEM((2, 128, 128), F32),
            pltpu.VMEM((2, 128, 128), F32),
            pltpu.VMEM((3, 2, 128, 128), F32),
            pltpu.VMEM((2, 128, 128), F32),
            pltpu.VMEM((6, 2, 128, 128), F32),
            pltpu.VMEM((384, 256), F32),
            pltpu.VMEM((NDEV // 4, 8, 128), F32),
            pltpu.VMEM((NTM * 16, 128), F32),
            pltpu.VMEM((70 * 8, 128), F32),
            pltpu.VMEM((3, 80, 128), F32),
            pltpu.VMEM((3, 80, 128), F32),
            pltpu.VMEM((2, 12, 8, 128), F32),
            pltpu.VMEM((7, 80, 128), F32),
            pltpu.VMEM((6, 64, 128), F32),
            pltpu.VMEM((6, 64, 128), F32),
            pltpu.VMEM((NDEV // 8, 8, 128), F32),
            dma, dma((NGROUP,)), dma, dma, dma, dma,
            dma, dma((2,)), dma((2, 3)), dma((2, 3)), dma, dma,
            dma((12,)),
        ],
        compiler_params=pltpu.CompilerParams(collective_id=0, has_side_effects=True),
    )(
        samples.reshape(128, 256),
        pointing.reshape(128, 256),
        angles.reshape(128, 256),
        counts.reshape(1, 128),
        sky,
        prior_precision,
        omega_noise,
        omega_prior,
        *(jnp.asarray(t) for t in tables()),
    )
    gain, binned, solved = pl.pallas_call(
        finish,
        name="finish",
        out_shape=(
            jax.ShapeDtypeStruct((1, 1), F32),
            jax.ShapeDtypeStruct((3, 128, 128), F32),
            jax.ShapeDtypeStruct((6, 64, 128), F32),
        ),
        in_specs=[vmem, vmem, vmem],
        out_specs=(anywhere, anywhere, anywhere),
        scratch_shapes=[pltpu.VMEM((1, 1), F32), dma((3,))],
    )(*(pltpu.with_memory_space_constraint(x, pltpu.VMEM) for x in (small, binned, solved)))
    binned = binned.reshape(3, 64, 2, 128).transpose(0, 2, 1, 3).reshape(3, 2, 8192)
    return (gain, binned, solved)


def solution(mesh):
    return jax.shard_map(
        per_device,
        mesh=mesh,
        in_specs=(
            P("det", "tm", None, None),
            P("det", "tm", None, None),
            P("det", "tm", None, None),
            P("det", "tm", None),
            P(None, ("det", "tm"), None),
            P(None, "det", "tm"),
            P(None, "det", "tm"),
            P(None, "det", "tm"),
        ),
        out_specs=(P("det", "tm"), P(None, ("det", "tm"), None), P(None, "det", "tm")),
        check_vma=False,
    )
```
